32 devices in a mesh: seq: 8 (over z, y), dp: 4 (over x, core).
Axes of the slice: x: 2, y: 2, z: 4, core: 2. Of those that a mesh axis runs over, the one named last changes fastest.
Arguments:
- block_input: bfloat16 [4, 1024, 1536], P('dp', 'seq'), may hold values from -6 to 6
- query_proj: bfloat16 [4, 1024, 768], P('dp', 'seq'), may hold values from -8 to 8
- key_proj: bfloat16 [4, 1024, 768], P('dp', 'seq'), may hold values from -8 to 8
- value_proj: bfloat16 [4, 1024, 768], P('dp', 'seq'), may hold values from -6 to 6
- lengths: int32 [4], P('dp'), may hold values from 256 to 1024, as said below
- out_proj: bfloat16 [1536, 768], replicated, may hold values from -0.21875 to 0.21875
- kernel: float32 [31, 1536], replicated, may hold values from -1 to 1
- conv_bias: float32 [1536], replicated, may hold values from -3 to 3
- grad_output: bfloat16 [4, 1024, 1536], P('dp', 'seq'), may hold values from -6 to 6
Outputs:
- block_output: bfloat16 [4, 1024, 1536], P('dp', 'seq')
- grad_input: bfloat16 [4, 1024, 1536], P('dp', 'seq')
- grad_query: bfloat16 [4, 1024, 768], P('dp', 'seq')
- grad_out_proj: float32 [1536, 768], P('seq')
- grad_kernel: float32 [31, 1536], P(None, 'seq')
- grad_bias: float32 [1536], P('seq')
The draws below stay inside these ranges and needn't reach their ends.
Inputs may be any that keep to these rules, and one draw needn't show every extreme that they name: `lengths`: frames at or after an utterance's length are padding; in every draw at least one utterance has all 1024 frames valid.
All inputs are finite; a program needn't handle non-finite values.
Results may differ from the reference program's by a relative error of at most 0.012.
The reference program's roundings to bfloat16 on the way count: a program that leaves them out, or rounds other values in their place, can miss the bound.
Values may be sent and summed in bfloat16 or wider, within the bound.
No kernel may reach another device: no remote copies, remote signals or barrier semaphores. Data moves between devices by JAX's collectives and lax.ppermute only.
A program may use at most 128 MiB of HBM per device.

```python
import math
import jax
import jax.numpy as jnp
from jax import lax

D = 1536
H = 8
HS = 96
KW = 31
HD = 768
L = 1024
B = 4


def query_key_pair(key):
    array_shape = (B, L, HD)
    key_values = jnp.clip(jax.random.normal(jax.random.fold_in(key, 11), array_shape, jnp.float32), -6.0, 6.0)
    query_values = jnp.clip(jax.random.normal(jax.random.fold_in(key, 12), array_shape, jnp.float32), -6.0, 6.0)
    return (query_values, key_values)


def draw_query_proj(key, part):
    return query_key_pair(key)[0].astype(jnp.bfloat16)


def draw_key_proj(key, part):
    return query_key_pair(key)[1].astype(jnp.bfloat16)


def draw_lengths(key, part):
    drawn_lengths = jax.random.randint(jax.random.fold_in(key, 21), (B,), L // 4, L + 1)
    full_index = jax.random.randint(jax.random.fold_in(key, 22), (), 0, B)
    return jnp.where(jnp.arange(B) == full_index, L, drawn_lengths).astype(jnp.int32)


def with_spikes(values, stream_key, source, target, blocks, factor):
    owner, partner = [(jnp.arange(values.shape[axis_at]) // (values.shape[axis_at] // blocks)).reshape([-1 if axis == axis_at else 1 for axis in range(values.ndim)]) for axis_at in (source, target)]
    chosen = jax.random.permutation(stream_key, blocks)[partner]
    strong = (owner == chosen) | (owner == (partner + blocks // 2) % blocks)
    return jnp.where(strong, factor * values, values)


def shard_levels(key, shape, shards, smallest, largest):
    level, own = 1.0, jax.random.fold_in(key, 6)
    for axis_at, shards_of in shards:
        heights = jnp.exp(jax.random.uniform(jax.random.fold_in(own, axis_at), (shards_of,), jnp.float32, smallest / len(shards), largest / len(shards)))
        level = level * jnp.repeat(heights, shape[axis_at] // shards_of).reshape([-1 if axis == axis_at else 1 for axis in range(len(shape))])
    return level


def normal_values(stream_key, shape, width, bound, cuts=(), held_as=jnp.bfloat16):
    values = jax.random.normal(stream_key, shape, jnp.float32) * width
    if len(cuts) > 0:
        values = shard_levels(stream_key, shape, cuts, -0.22, 0.18) * values
    return jnp.clip(values, min=-bound, max=bound).astype(held_as)


def heavy_noise(own_key, shape, scale, bound, split, heavy, dtype=jnp.bfloat16):
    values = scale * jax.random.normal(own_key, shape, jnp.float32)
    if split:
        values = values * shard_levels(own_key, shape, split, -0.22, 0.18)
    return jnp.clip(with_spikes(values, jax.random.fold_in(own_key, 3), *heavy), -bound, bound).astype(dtype)


def setup_inputs(seed: int = 0) -> dict:
    key_list = jax.random.split(jax.random.key(seed), 10)
    block_input = normal_values(key_list[0], (B, L, D), 1.0, 6.0, ((0, 4), (1, 8)))
    query_proj = draw_query_proj(jax.random.fold_in(key_list[9], 71), 0)
    key_proj = draw_key_proj(jax.random.fold_in(key_list[9], 71), 0)
    value_proj = normal_values(key_list[3], (B, L, HD), 1.0, 6.0, ((0, 4), (1, 8)))
    lengths = draw_lengths(jax.random.fold_in(key_list[9], 71), 0)
    out_proj = normal_values(key_list[5], (D, HD), HD ** -0.5, 0.21875)
    kernel = normal_values(key_list[6], (KW, D), KW ** -0.5, 1.0, (), jnp.float32)
    conv_bias = normal_values(key_list[7], (D,), 0.5, 3.0, (), jnp.float32)
    grad_output = heavy_noise(key_list[8], (B, L, D), 1.0, 6.0, ((0, 4), (1, 8)), (1, 2, 8, 2.0))
    return {"block_input": block_input, "query_proj": query_proj, "key_proj": key_proj, "value_proj": value_proj, "lengths": lengths, "out_proj": out_proj, "kernel": kernel, "conv_bias": conv_bias, "grad_output": grad_output}


def split_heads(matrix):
    return matrix.reshape(L, H, HS).transpose(1, 0, 2)

def head_scores(query_block, key_heads, score_scale, key_valid):
    scores = jnp.einsum('hqd,hkd->hqk', query_block.astype(jnp.float32), key_heads.astype(jnp.float32)) * score_scale
    return jnp.where(key_valid[None, None, :], scores, -jnp.inf)

def one_utterance(block_input, query_proj, key_proj, value_proj, utt_length, grad_output, out_proj, kernel, conv_bias):
    frame_index = jnp.arange(L)
    valid = frame_index < utt_length
    score_scale = 1.0 / math.sqrt(HS)
    block_rows = math.gcd(L, 512)
    block_count = L // block_rows
    query_heads = split_heads(query_proj)
    key_heads = split_heads(key_proj)
    value_heads = split_heads(value_proj)
    query_blocks = query_heads.reshape(H, block_count, block_rows, HS).transpose(1, 0, 2, 3)

    def forward_block(query_block):
        scores = head_scores(query_block, key_heads, score_scale, valid)
        row_top = lax.optimization_barrier(jnp.max(scores, axis=-1, keepdims=True))
        log_total = row_top + jnp.log(lax.optimization_barrier(jnp.sum(jnp.exp(scores - row_top), axis=-1, keepdims=True)))
        weights = jnp.exp(scores - log_total).astype(jnp.bfloat16)
        result = jnp.einsum('hqk,hkd->hqd', weights.astype(jnp.float32), value_heads.astype(jnp.float32))
        return (result, log_total[..., 0])
    outputs, log_totals = lax.map(forward_block, query_blocks)
    attended = outputs.transpose(0, 2, 1, 3).reshape(L, HD).astype(jnp.bfloat16)
    mixed_rows = (block_input.astype(jnp.float32) + jnp.dot(attended, out_proj.T, preferred_element_type=jnp.float32)).astype(jnp.bfloat16)
    masked = jnp.where(valid[:, None], mixed_rows, jnp.zeros_like(mixed_rows))
    halo_width = KW // 2
    padded = jnp.pad(masked.astype(jnp.float32), ((halo_width, halo_width), (0, 0)))
    conv_rows = jnp.broadcast_to(conv_bias, (L, D)).astype(jnp.float32)
    for tap in range(KW):
        conv_rows = conv_rows + kernel[tap] * padded[tap:tap + L]
    gate_rows = jax.nn.sigmoid(conv_rows)
    block_output = jnp.where(valid[:, None], mixed_rows.astype(jnp.float32) + conv_rows * gate_rows, 0.0).astype(jnp.bfloat16)
    grad_rows = jnp.where(valid[:, None], grad_output.astype(jnp.float32), 0.0)
    grad_conv = grad_rows * gate_rows * (1.0 + conv_rows * (1.0 - gate_rows))
    grad_kernel = jnp.stack([lax.optimization_barrier(jnp.sum(grad_conv * padded[tap:tap + L], axis=0)) for tap in range(KW)])
    grad_bias = lax.optimization_barrier(jnp.sum(grad_conv, axis=0))
    grad_padded = jnp.pad(grad_conv, ((halo_width, halo_width), (0, 0)))
    grad_masked = jnp.zeros((L, D), jnp.float32)
    for tap in range(KW):
        begin = 2 * halo_width - tap
        grad_masked = grad_masked + kernel[tap] * grad_padded[begin:begin + L]
    grad_input = (grad_rows + jnp.where(valid[:, None], grad_masked, 0.0)).astype(jnp.bfloat16)
    grad_out_proj = jnp.dot(grad_input.T, attended, preferred_element_type=jnp.float32)
    grad_attn = jnp.dot(grad_input, out_proj, preferred_element_type=jnp.float32).astype(jnp.bfloat16)
    row_delta = lax.optimization_barrier(jnp.sum((grad_attn.astype(jnp.float32) * attended.astype(jnp.float32)).reshape(L, H, HS), axis=-1))
    grad_blocks = split_heads(grad_attn).reshape(H, block_count, block_rows, HS).transpose(1, 0, 2, 3)
    delta_blocks = row_delta.T.reshape(H, block_count, block_rows).transpose(1, 0, 2)

    def backward_block(block_items):
        query_block, grad_block, lse_block, delta_block = block_items
        scores = head_scores(query_block, key_heads, score_scale, valid)
        probs = jnp.exp(scores - lse_block[..., None])
        grad_prob = jnp.einsum('hqd,hkd->hqk', grad_block.astype(jnp.float32), value_heads.astype(jnp.float32))
        grad_score = (probs * (grad_prob - delta_block[..., None])).astype(jnp.bfloat16)
        return jnp.einsum('hqk,hkd->hqd', grad_score.astype(jnp.float32), key_heads.astype(jnp.float32)) * score_scale
    grad_q_blocks = lax.map(backward_block, (query_blocks, grad_blocks, log_totals, delta_blocks))
    grad_query = grad_q_blocks.transpose(0, 2, 1, 3).reshape(L, HD).astype(jnp.bfloat16)
    return (block_output, grad_input, grad_query, grad_out_proj, grad_kernel, grad_bias)

def reference(block_input, query_proj, key_proj, value_proj, lengths, out_proj, kernel, conv_bias, grad_output):

    def per_utterance(utt_items):
        return one_utterance(utt_items[0], utt_items[1], utt_items[2], utt_items[3], utt_items[4], utt_items[5], out_proj, kernel, conv_bias)
    results = lax.map(per_utterance, (block_input, query_proj, key_proj, value_proj, lengths, grad_output))
    return (results[0], results[1], results[2], lax.optimization_barrier(jnp.sum(results[3], axis=0)), lax.optimization_barrier(jnp.sum(results[4], axis=0)), lax.optimization_barrier(jnp.sum(results[5], axis=0)))
```

```python
import functools
import math

import jax
import jax.numpy as jnp
from jax import lax
from jax.experimental import pallas as pl
from jax.experimental.pallas import tpu as pltpu
from jax.sharding import PartitionSpec as P

D = 1536
H = 8
HS = 96
KW = 31
HD = 768


def with_halo(x, sides, width):
    for axis, dim in sides:
        size, length = (lax.axis_size(axis), x.shape[dim])
        up = [(i, (i + 1) % size) for i in range(size - 1)]
        down = [(j, i) for i, j in up]
        last = lax.slice_in_dim(x, length - width, length, axis=dim)
        leading = lax.slice_in_dim(x, 0, width, axis=dim)
        before = lax.ppermute(last, axis, up)
        after = lax.ppermute(leading, axis, down)
        x = jnp.concatenate([before, x, after], axis=dim)
    return x


def forward_rows(query_one, key_one, value_one, key_valid, score_scale):
    row_total = query_one.shape[0]
    block_rows = math.gcd(row_total, 512)
    query_blocks = query_one.reshape(row_total // block_rows, block_rows, query_one.shape[1])

    def forward_one_block(query_block):
        scores = (
            lax.dot_general(
                query_block, key_one, (((1,), (1,)), ((), ())), preferred_element_type=jnp.float32
            )
            * score_scale
        )
        scores = jnp.where(key_valid[None, :], scores, -jnp.inf)
        row_top = jnp.max(scores, axis=-1, keepdims=True)
        log_total = row_top + jnp.log(jnp.sum(jnp.exp(scores - row_top), axis=-1, keepdims=True))
        weights = jnp.exp(scores - log_total).astype(jnp.bfloat16)
        return (jnp.dot(weights, value_one, preferred_element_type=jnp.float32), log_total[:, 0])

    outputs, log_totals = lax.map(forward_one_block, query_blocks)
    return (outputs.reshape(row_total, query_one.shape[1]), log_totals.reshape(row_total))


def backward_rows(
    query_one, key_one, value_one, grad_one, lse_one, delta_one, key_valid, score_scale
):
    row_total = query_one.shape[0]
    block_rows = math.gcd(row_total, 512)
    block_count = row_total // block_rows
    width = query_one.shape[1]

    def backward_one_block(items):
        query_block, grad_block, lse_block, delta_block = items
        scores = (
            lax.dot_general(
                query_block, key_one, (((1,), (1,)), ((), ())), preferred_element_type=jnp.float32
            )
            * score_scale
        )
        scores = jnp.where(key_valid[None, :], scores, -jnp.inf)
        probs = jnp.exp(scores - lse_block[:, None])
        grad_prob = lax.dot_general(
            grad_block, value_one, (((1,), (1,)), ((), ())), preferred_element_type=jnp.float32
        )
        grad_score = (probs * (grad_prob - delta_block[:, None])).astype(jnp.bfloat16)
        return jnp.dot(grad_score, key_one, preferred_element_type=jnp.float32) * score_scale

    results = lax.map(
        backward_one_block,
        (
            query_one.reshape(block_count, block_rows, width),
            grad_one.reshape(block_count, block_rows, width),
            lse_one.reshape(block_count, block_rows),
            delta_one.reshape(block_count, block_rows),
        ),
    )
    return results.reshape(row_total, width)


def general_device(
    block_input, query_proj, key_proj, value_proj, lengths, out_proj, kernel, conv_bias, grad_output
):
    frames_dev = block_input.shape[1]
    seq_count = lax.axis_size("seq")
    total_frames = frames_dev * seq_count
    first_frame = lax.axis_index("seq") * frames_dev
    utt_length = lengths[0]
    local_valid = first_frame + jnp.arange(frames_dev) < utt_length
    all_valid = jnp.arange(total_frames) < utt_length
    score_scale = 1.0 / math.sqrt(HS)
    halo_width = KW // 2
    group_size = seq_count // H
    sub_rows = frames_dev // group_size
    query_local = query_proj[0]

    def to_serving(matrix):
        return matrix.reshape(frames_dev, H, HS).transpose(1, 0, 2).reshape(seq_count, sub_rows, HS)

    def from_serving(returned):
        return returned.reshape(H, frames_dev, HS).transpose(1, 0, 2).reshape(frames_dev, HD)

    query_mine = lax.all_to_all(
        to_serving(query_local), "seq", split_axis=0, concat_axis=1, tiled=True
    )[0]
    key_send = jnp.repeat(
        key_proj[0].reshape(frames_dev, H, HS).transpose(1, 0, 2), group_size, axis=0
    )
    value_send = jnp.repeat(
        value_proj[0].reshape(frames_dev, H, HS).transpose(1, 0, 2), group_size, axis=0
    )
    key_mine, value_mine = (
        lax.all_to_all(key_send, "seq", split_axis=0, concat_axis=1, tiled=True),
        lax.all_to_all(value_send, "seq", split_axis=0, concat_axis=1, tiled=True),
    )
    key_mine = key_mine[0]
    value_mine = value_mine[0]
    head_out, head_lse = forward_rows(query_mine, key_mine, value_mine, all_valid, score_scale)
    head_attended = head_out.astype(jnp.bfloat16)
    attended = from_serving(
        lax.all_to_all(head_attended[None], "seq", split_axis=1, concat_axis=0, tiled=True)
    )
    projected = lax.dot_general(
        attended, out_proj, (((1,), (1,)), ((), ())), preferred_element_type=jnp.float32
    )
    mixed_rows = (block_input[0].astype(jnp.float32) + projected).astype(jnp.bfloat16)
    masked = jnp.where(local_valid[:, None], mixed_rows, jnp.zeros_like(mixed_rows))
    padded = with_halo(masked, (("seq", 0),), halo_width).astype(jnp.float32)
    conv_rows = jnp.broadcast_to(conv_bias, (frames_dev, D))
    for tap in range(KW):
        conv_rows = conv_rows + kernel[tap] * padded[tap : tap + frames_dev]
    gate_rows = jax.nn.sigmoid(conv_rows)
    block_output = jnp.where(
        local_valid[:, None], mixed_rows.astype(jnp.float32) + conv_rows * gate_rows, 0.0
    ).astype(jnp.bfloat16)
    grad_rows = jnp.where(local_valid[:, None], grad_output[0].astype(jnp.float32), 0.0)
    grad_conv = grad_rows * gate_rows * (1.0 + conv_rows * (1.0 - gate_rows))
    kernel_local = jnp.stack(
        [jnp.sum(grad_conv * padded[tap : tap + frames_dev], axis=0) for tap in range(KW)]
    )
    bias_local = jnp.sum(grad_conv, axis=0)
    grad_padded = with_halo(grad_conv, (("seq", 0),), halo_width)
    grad_masked = jnp.zeros((frames_dev, D), jnp.float32)
    for tap in range(KW):
        begin = 2 * halo_width - tap
        grad_masked = grad_masked + kernel[tap] * grad_padded[begin : begin + frames_dev]
    grad_input = (grad_rows + jnp.where(local_valid[:, None], grad_masked, 0.0)).astype(
        jnp.bfloat16
    )
    grad_attn = jnp.dot(grad_input, out_proj, preferred_element_type=jnp.float32).astype(
        jnp.bfloat16
    )
    grad_mine = lax.all_to_all(
        to_serving(grad_attn), "seq", split_axis=0, concat_axis=1, tiled=True
    )[0]
    delta_mine = jnp.sum(grad_mine.astype(jnp.float32) * head_attended.astype(jnp.float32), axis=-1)
    grad_q_mine = backward_rows(
        query_mine, key_mine, value_mine, grad_mine, head_lse, delta_mine, all_valid, score_scale
    ).astype(jnp.bfloat16)
    grad_query = from_serving(
        lax.all_to_all(grad_q_mine[None], "seq", split_axis=1, concat_axis=0, tiled=True)
    )
    term_block = lax.dot_general(
        grad_input, attended, (((0,), (0,)), ((), ())), preferred_element_type=jnp.float32
    )
    partial_rows = lax.psum_scatter(term_block, "seq", scatter_dimension=0, tiled=True)
    summed = lax.psum(partial_rows.astype(jnp.bfloat16), "dp").astype(jnp.float32)
    kernel_total, bias_total = lax.psum((kernel_local, bias_local), ("seq", "dp"))
    shard_width = D // seq_count
    offset = lax.axis_index("seq") * shard_width
    grad_kernel = lax.dynamic_slice_in_dim(kernel_total, offset, shard_width, 1)
    grad_bias = lax.dynamic_slice_in_dim(bias_total, offset, shard_width, 0)
    return (block_output[None], grad_input[None], grad_query[None], summed, grad_kernel, grad_bias)


BF16 = jnp.bfloat16
F32 = jnp.float32
TAP_ROWS = 32
WIDE = 32
SIDE = 16
CHUNK = 384
LANES = 128
MASKED_SCORE = -1e30
VMEM_LIMIT = 56 * 1024 * 1024
SCORE_SCALE = 1.0 / math.sqrt(HS)
LOG2_SCALE = SCORE_SCALE * math.log2(math.e)


def fits_fast(sizes):
    seq_count, dp_count = sizes["seq"], sizes["dp"]
    piece = D // (seq_count * dp_count)
    return seq_count == H and dp_count * seq_count * piece == D and piece == 48


def params():
    return pltpu.CompilerParams(vmem_limit_bytes=VMEM_LIMIT)


def whole(shape):
    return pl.BlockSpec(shape, lambda *_: (0,) * len(shape))


def pack_kernel(q_ref, k_ref, v_ref, out_ref):
    for place, ref in enumerate((q_ref, k_ref, v_ref)):
        frames = ref.shape[0]
        out_ref[:, place * HS : (place + 1) * HS, :] = ref[...].T.reshape(H, HS, frames)


def pack_heads(q, k, v):
    frames = q.shape[0]
    return pl.pallas_call(
        pack_kernel,
        out_shape=jax.ShapeDtypeStruct((H, 3 * HS, frames), BF16),
        compiler_params=params(),
        name="pack_heads",
    )(q, k, v)


def key_rows(k_ref, length, keys_sc):
    blocks, _, frames = k_ref.shape
    for block in range(blocks):
        row = lax.broadcasted_iota(jnp.int32, (LANES - HS, frames), 0)
        key = lax.broadcasted_iota(jnp.int32, (LANES - HS, frames), 1) + block * frames
        extra = jnp.where((row == 0) & (key >= length), MASKED_SCORE, 0.0)
        tall = jnp.concatenate([k_ref[block].astype(F32), extra], axis=0)
        keys_sc[block * frames : (block + 1) * frames, :] = tall.T.astype(BF16)


def query_columns(q_ref):
    query = jnp.concatenate([q_ref[0], q_ref[1]], axis=1)
    row = lax.broadcasted_iota(jnp.int32, (LANES - HS, query.shape[1]), 0)
    return jnp.concatenate([query, jnp.where(row == 0, 1.0, 0.0).astype(BF16)], axis=0)


def side_by_side(ref, wide_sc):
    blocks, _, frames = ref.shape
    for block in range(blocks):
        wide_sc[:, block * frames : (block + 1) * frames] = ref[block]


def forward_kernel(length_ref, q_ref, k_ref, v_ref, out_ref, lse_ref, keys_sc, values_sc):
    step = pl.program_id(0)
    blocks, _, frames = k_ref.shape

    @pl.when(step == 0)
    def _():
        key_rows(k_ref, length_ref[0], keys_sc)
        side_by_side(v_ref, values_sc)

    scores = jnp.dot(keys_sc[...], query_columns(q_ref), preferred_element_type=F32) * LOG2_SCALE
    top = jnp.max(scores, axis=0, keepdims=True)
    raised = jnp.exp2(scores - top)
    total = jnp.sum(raised, axis=0, keepdims=True)
    weights = (raised * (1.0 / total)).astype(BF16)
    lse_ref[...] = top + jnp.log2(total)
    mixed = jnp.dot(values_sc[...], weights, preferred_element_type=F32).astype(BF16)
    out_ref[2 * step, :HS, :] = mixed[:, :frames]
    out_ref[2 * step + 1, :HS, :] = mixed[:, frames:]

    @pl.when(step == pl.num_programs(0) - 1)
    def _():
        lane = lax.broadcasted_iota(jnp.int32, (HS, frames), 1)
        nothing = jnp.zeros((HS, frames), F32)
        for block in range(blocks):
            left = nothing
            right = nothing
            if block > 0:
                left = pltpu.roll(out_ref[block - 1, :HS, :].astype(F32), WIDE, 1)
            if block < blocks - 1:
                right = pltpu.roll(out_ref[block + 1, :HS, :].astype(F32), WIDE, 1)
            both = jnp.where(lane < WIDE, left, right)
            lower = pltpu.roll(both[HS // 2 :], 2 * WIDE, 1)
            packed = jnp.where(lane[: HS // 2] < 2 * WIDE, both[: HS // 2], lower)
            out_ref[block, HS:, :] = packed.astype(BF16)


def forward_heads(length, received):
    blocks, _, frames = received.shape
    total = blocks * frames
    block = (blocks, HS, frames)
    return pl.pallas_call(
        forward_kernel,
        grid=(blocks // 2,),
        in_specs=[
            pl.BlockSpec(memory_space=pltpu.SMEM),
            pl.BlockSpec((2, HS, frames), lambda i: (i, 0, 0)),
            pl.BlockSpec(block, lambda i: (0, 1, 0)),
            pl.BlockSpec(block, lambda i: (0, 2, 0)),
        ],
        out_specs=[
            whole((blocks, HS + HS // 2, frames)),
            pl.BlockSpec((1, 2 * frames), lambda i: (0, i)),
        ],
        out_shape=[
            jax.ShapeDtypeStruct((blocks, HS + HS // 2, frames), BF16),
            jax.ShapeDtypeStruct((1, total), F32),
        ],
        scratch_shapes=[pltpu.VMEM((total, LANES), BF16), pltpu.VMEM((HS, total), BF16)],
        compiler_params=params(),
        name="forward_heads",
    )(length, received, received, received)


def backward_kernel(
    length_ref, q_ref, k_ref, v_ref, grad_ref, head_ref, lse_ref, out_ref, keys_sc, values_sc, wide_sc
):
    step = pl.program_id(0)
    blocks, _, frames = k_ref.shape

    @pl.when(step == 0)
    def _():
        key_rows(k_ref, length_ref[0], keys_sc)
        side_by_side(k_ref, wide_sc)
        for block in range(blocks):
            rows = v_ref[block].astype(F32).T.astype(BF16)
            values_sc[block * frames : (block + 1) * frames, :] = rows

    scores = jnp.dot(keys_sc[...], query_columns(q_ref), preferred_element_type=F32) * LOG2_SCALE
    probs = jnp.exp2(scores - lse_ref[...])
    grad = jnp.concatenate([grad_ref[0], grad_ref[1]], axis=1)
    head = jnp.concatenate([head_ref[0], head_ref[1]], axis=1)
    delta = jnp.sum(grad.astype(F32) * head.astype(F32), axis=0, keepdims=True)
    grad_prob = jnp.dot(values_sc[...], grad, preferred_element_type=F32)
    grad_score = (probs * (grad_prob - delta)).astype(BF16)
    result = jnp.dot(wide_sc[...], grad_score, preferred_element_type=F32) * SCORE_SCALE
    out_ref[0] = result[:, :frames].astype(BF16)
    out_ref[1] = result[:, frames:].astype(BF16)


def backward_heads(length, received, grads, heads, lse):
    blocks, _, frames = received.shape
    total = blocks * frames
    block = (blocks, HS, frames)
    pair = pl.BlockSpec((2, HS, frames), lambda i: (i, 0, 0))
    return pl.pallas_call(
        backward_kernel,
        grid=(blocks // 2,),
        in_specs=[
            pl.BlockSpec(memory_space=pltpu.SMEM),
            pair,
            pl.BlockSpec(block, lambda i: (0, 1, 0)),
            pl.BlockSpec(block, lambda i: (0, 2, 0)),
            pair,
            pair,
            pl.BlockSpec((1, 2 * frames), lambda i: (0, i)),
        ],
        out_specs=pair,
        out_shape=jax.ShapeDtypeStruct((blocks, HS, frames), BF16),
        scratch_shapes=[
            pltpu.VMEM((total, LANES), BF16),
            pltpu.VMEM((total, HS), BF16),
            pltpu.VMEM((HS, total), BF16),
        ],
        compiler_params=params(),
        name="backward_heads",
    )(length, received, received, received, grads, heads, lse)


def shifted_sum(ref, tile, rows, weight_of, start):
    total = start
    for low in range(8):
        base = ref[tile, low : low + rows + 24, :]
        for high in range(4):
            offset = 8 * high + low
            if 1 <= offset < TAP_ROWS:
                total = total + weight_of(offset) * base[8 * high : 8 * high + rows]
    return total


def middle_kernel(
    info_ref,
    main_ref,
    edge_ref,
    input_ref,
    cot_ref,
    before_ref,
    after_ref,
    proj_ref,
    tap_ref,
    bias_ref,
    block_out_ref,
    grad_in_ref,
    grad_heads_ref,
    *rest,
):
    piece_refs = rest[:-6]
    att_sc, grad_sc, masked_sc, gate_sc, taps_sc, piece_sc = rest[-6:]
    dp_count = len(piece_refs)
    step = pl.program_id(0)
    frames = input_ref.shape[0]
    tiles = CHUNK // LANES
    rows = frames + 2 * WIDE
    span = frames + 2 * SIDE
    first, length, mine = info_ref[0], info_ref[1], info_ref[2]

    @pl.when(step == 0)
    def _():
        main = main_ref[...].reshape(HD, frames)
        att_sc[WIDE : WIDE + frames, :] = main.T
        edge = edge_ref[...].astype(F32).reshape(H * (HS // 2), frames)
        lower = pltpu.roll(edge, frames - 2 * WIDE, 1)
        half = (H, HS // 2, frames)
        tall = jnp.concatenate([edge.reshape(half), lower.reshape(half)], axis=1)
        turned = tall.reshape(HD, frames).T.astype(BF16)
        att_sc[:WIDE, :] = turned[:WIDE]
        att_sc[WIDE + frames :, :] = turned[WIDE : 2 * WIDE]
        grad_sc[...] = jnp.zeros_like(grad_sc)

    projected = lax.dot_general(
        att_sc[...], proj_ref[...], (((1,), (1,)), ((), ())), preferred_element_type=F32
    )
    wide_input = jnp.concatenate(
        [before_ref[:WIDE, :], input_ref[...], after_ref[:WIDE, :]], axis=0
    ).astype(F32)
    mixed = (wide_input + projected).astype(BF16).astype(F32)
    frame = first - WIDE + lax.broadcasted_iota(jnp.int32, (rows, CHUNK), 0)
    valid = (frame >= 0) & (frame < length)
    masked = jnp.where(valid, mixed, 0.0)
    cot = jnp.concatenate(
        [before_ref[WIDE:, :], cot_ref[...], after_ref[WIDE:, :]], axis=0
    ).astype(F32)
    inner = slice(WIDE - SIDE, WIDE + SIDE + frames)
    cot = jnp.where(valid[inner], cot, 0.0)
    for tile in range(tiles):
        masked_sc[tile] = masked[:, tile * LANES : (tile + 1) * LANES]

    own = slice(SIDE, SIDE + frames)
    here = valid[WIDE : WIDE + frames, :LANES]
    for tile in range(tiles):
        lanes = slice(tile * LANES, (tile + 1) * LANES)
        start = jnp.broadcast_to(bias_ref[:, lanes], (span, LANES))
        conv = shifted_sum(
            masked_sc, tile, span, lambda offset: tap_ref[offset - 1 : offset, lanes], start
        )
        gate = lax.logistic(conv)
        center = masked_sc[tile, WIDE : WIDE + frames, :]
        block_out_ref[:, lanes] = jnp.where(here, center + conv[own] * gate[own], 0.0).astype(BF16)
        gated = cot[:, lanes] * gate * (1.0 + conv * (1.0 - gate))
        gate_sc[tile] = gated
        owned = gated[own]
        for low in range(8):
            base = masked_sc[tile, SIDE + low : SIDE + low + frames + 24, :]
            for high in range(4):
                offset = 8 * high + low
                if 1 <= offset < TAP_ROWS:
                    product = owned * base[8 * high : 8 * high + frames]
                    taps_sc[offset - 1, :, lanes] = product.reshape(frames // 8, 8, LANES).sum(0)
        taps_sc[TAP_ROWS - 1, :, lanes] = owned.reshape(frames // 8, 8, LANES).sum(0)
        back = shifted_sum(
            gate_sc,
            tile,
            frames,
            lambda offset: tap_ref[KW - offset : KW - offset + 1, lanes],
            jnp.zeros((frames, LANES), F32),
        )
        grad_in_ref[:, lanes] = (cot[own, lanes] + jnp.where(here, back, 0.0)).astype(BF16)

    grad_in = grad_in_ref[...]
    grad_sc[...] += jnp.dot(grad_in, proj_ref[...], preferred_element_type=F32)

    piece = 48
    half = piece // 2
    slabs = CHUNK // (dp_count * piece)
    turned = grad_in.T.reshape(slabs * dp_count, piece, frames)
    taps = jnp.sum(taps_sc[...], axis=1)
    high_part = taps.astype(BF16).astype(F32)
    low_part = taps - high_part
    four = jnp.concatenate([high_part, low_part, high_part, low_part], axis=0)
    tall = four.T.reshape(slabs * dp_count, piece, LANES)
    lane = lax.broadcasted_iota(jnp.int32, (half, LANES), 1)
    slab_count = D // (dp_count * piece)
    for owner in range(dp_count):
        packed = []
        for slab in range(slabs):
            source = slab * dp_count + owner
            where = pl.multiple_of((step * slabs + slab) * piece, piece)
            piece_sc[owner, pl.ds(where, piece), :] = turned[source]
            packed.append(
                jnp.where(lane < LANES // 2, tall[source, :half], tall[source, half:])
            )
        where = pl.multiple_of(slab_count * piece + step * slabs * half, slabs * half)
        piece_sc[owner, pl.ds(where, slabs * half), :] = jnp.concatenate(packed, axis=0).astype(BF16)

    @pl.when(step == pl.num_programs(0) - 1)
    def _():
        grad_heads_ref[...] = grad_sc[...].T.astype(BF16).reshape(H, HS, frames)
        for away, ref in enumerate(piece_refs):
            ref[...] = piece_sc[lax.rem(mine + away, dp_count)]


def middle(info, returned, block_input, grad_output, before, after, out_proj, kernel, bias, dp_count):
    frames = block_input.shape[0]
    halo = WIDE + SIDE
    piece_rows = D // dp_count + D // dp_count // 2
    column = lambda count: pl.BlockSpec((count, CHUNK), lambda i: (0, i))
    return pl.pallas_call(
        middle_kernel,
        grid=(D // CHUNK,),
        in_specs=[
            pl.BlockSpec(memory_space=pltpu.SMEM),
            pl.BlockSpec((H, HS, frames), lambda i: (0, 0, 0)),
            pl.BlockSpec((H, HS // 2, frames), lambda i: (0, 2, 0)),
            column(frames),
            column(frames),
            column(halo),
            column(halo),
            pl.BlockSpec((CHUNK, HD), lambda i: (i, 0)),
            column(KW),
            column(1),
        ],
        out_specs=[
            column(frames),
            column(frames),
            whole((H, HS, frames)),
        ]
        + [whole((piece_rows, frames))] * dp_count,
        out_shape=[
            jax.ShapeDtypeStruct((frames, D), BF16),
            jax.ShapeDtypeStruct((frames, D), BF16),
            jax.ShapeDtypeStruct((H, HS, frames), BF16),
        ]
        + [jax.ShapeDtypeStruct((piece_rows, frames), BF16)] * dp_count,
        scratch_shapes=[
            pltpu.VMEM((frames + 2 * WIDE, HD), BF16),
            pltpu.VMEM((frames, HD), F32),
            pltpu.VMEM((CHUNK // LANES, frames + 2 * WIDE, LANES), F32),
            pltpu.VMEM((CHUNK // LANES, frames + 2 * SIDE, LANES), F32),
            pltpu.VMEM((TAP_ROWS, 8, CHUNK), F32),
            pltpu.VMEM((dp_count, piece_rows, frames), BF16),
        ],
        compiler_params=params(),
        name="middle",
    )(info, returned, returned, block_input, grad_output, before, after, out_proj, kernel, bias)


def split_parts(lane, value):
    high_part = value.astype(BF16).astype(F32)
    low_part = pltpu.roll(value - high_part, TAP_ROWS, 1)
    return jnp.where(lane % (2 * TAP_ROWS) < TAP_ROWS, high_part, low_part)


def join_parts(value):
    return value + pltpu.roll(value, LANES - TAP_ROWS, 1)


def product_kernel(*refs):
    out_ref = refs[-1]
    count = (len(refs) - 1) // 2
    pieces, heads = refs[:count], refs[count : 2 * count]
    slabs, piece, _ = out_ref.shape
    frames = pieces[0].shape[1]
    height = slabs * piece
    total = jnp.zeros((height, HD), F32)
    taps = jnp.zeros((height // 2, frames), F32)
    for piece_ref, head_ref in zip(pieces, heads):
        total += lax.dot_general(
            piece_ref[:height, :],
            head_ref[...].reshape(HD, frames),
            (((1,), (1,)), ((), ())),
            preferred_element_type=F32,
        )
        taps += piece_ref[height:, :].astype(F32)
    out_ref[:, :, :HD] = total.astype(BF16).reshape(slabs, piece, HD)
    lane = lax.broadcasted_iota(jnp.int32, taps.shape, 1)
    parts = split_parts(lane, join_parts(taps)).reshape(slabs, piece // 2, LANES)
    padded = jnp.concatenate([parts, jnp.zeros_like(parts)], axis=1)
    out_ref[:, :, HD:] = padded.astype(BF16)


def product(pieces, heads, returned, seq_count):
    frames = returned.shape[2]
    piece_rows = pieces[0].shape[0]
    height = piece_rows * 2 // 3
    head_spec = whole((H, HS, frames))
    return pl.pallas_call(
        product_kernel,
        grid=(1,),
        in_specs=[whole((piece_rows, frames))] * len(pieces) + [head_spec] * len(pieces),
        out_specs=whole((seq_count, height // seq_count, HD + LANES)),
        out_shape=jax.ShapeDtypeStruct((seq_count, height // seq_count, HD + LANES), BF16),
        compiler_params=params(),
        name="product",
    )(*pieces, returned, *heads)


def sum_kernel(in_ref, out_ref):
    total = jnp.sum(in_ref[...].astype(F32), axis=0)
    out_ref[:, :HD] = total[:, :HD].astype(BF16)
    taps = total[:, HD:]
    lane = lax.broadcasted_iota(jnp.int32, taps.shape, 1)
    out_ref[:, HD:] = split_parts(lane, join_parts(taps)).astype(BF16)


def sum_shares(shares):
    _, piece, width = shares.shape
    return pl.pallas_call(
        sum_kernel,
        out_shape=jax.ShapeDtypeStruct((piece, width), BF16),
        compiler_params=params(),
        name="sum_shares",
    )(shares)


def finish_kernel(in_ref, proj_ref, tap_ref, bias_ref):
    owners, piece, _ = in_ref.shape
    half = piece // 2
    columns = []
    for owner in range(owners):
        proj_ref[owner * piece : (owner + 1) * piece, :] = in_ref[owner, :, :HD].astype(F32)
        taps = join_parts(in_ref[owner, :half, HD:].astype(F32))
        columns += [taps, pltpu.roll(taps, LANES // 2, 1)]
    turned = jnp.concatenate(columns, axis=0).T
    tap_ref[...] = turned[:KW]
    bias_ref[...] = turned[KW : KW + 1]


def finish(gathered):
    owners, piece, _ = gathered.shape
    width = owners * piece
    return pl.pallas_call(
        finish_kernel,
        out_shape=[
            jax.ShapeDtypeStruct((width, HD), F32),
            jax.ShapeDtypeStruct((KW, width), F32),
            jax.ShapeDtypeStruct((1, width), F32),
        ],
        compiler_params=params(),
        name="finish",
    )(gathered)


def unpack_kernel(in_ref, out_ref):
    out_ref[...] = in_ref[...].reshape(HD, in_ref.shape[2]).T


def unpack_heads(heads):
    frames = heads.shape[2]
    return pl.pallas_call(
        unpack_kernel,
        out_shape=jax.ShapeDtypeStruct((frames, HD), BF16),
        compiler_params=params(),
        name="unpack_heads",
    )(heads)


def exchange(blocks, axis):
    return lax.all_to_all(blocks, axis, split_axis=0, concat_axis=0, tiled=True)


def fast_device(
    block_input, query_proj, key_proj, value_proj, lengths, out_proj, kernel, conv_bias, grad_output
):
    frames = block_input.shape[1]
    seq_count = lax.axis_size("seq")
    dp_count = lax.axis_size("dp")
    first_frame = lax.axis_index("seq") * frames
    info = jnp.stack([first_frame, lengths[0], lax.axis_index("dp")]).astype(jnp.int32)

    received = exchange(pack_heads(query_proj[0], key_proj[0], value_proj[0]), "seq")

    last = jnp.concatenate([block_input[0, frames - WIDE :], grad_output[0, frames - SIDE :]])
    leading = jnp.concatenate([block_input[0, :WIDE], grad_output[0, :SIDE]])
    up = [(i, i + 1) for i in range(seq_count - 1)]
    down = [(j, i) for i, j in up]
    before = lax.ppermute(last, "seq", up)
    after = lax.ppermute(leading, "seq", down)

    sent, lse = forward_heads(lengths, received)
    returned = exchange(sent, "seq")
    mine = returned[:, :HS]
    shifts = [[(i, (i + away) % dp_count) for i in range(dp_count)] for away in range(1, dp_count)]
    heads = [lax.ppermute(mine, "dp", shift) for shift in shifts]

    block_output, grad_input, grad_heads, *pieces = middle(
        info,
        returned,
        block_input[0],
        grad_output[0],
        before,
        after,
        out_proj,
        kernel,
        conv_bias[None],
        dp_count,
    )
    grads = exchange(grad_heads, "seq")
    moved = [pieces[0]] + [
        lax.ppermute(piece, "dp", shift) for piece, shift in zip(pieces[1:], shifts)
    ]
    grad_query = unpack_heads(exchange(backward_heads(lengths, received, grads, sent, lse), "seq"))

    shares = exchange(product(moved, heads, returned, seq_count), "seq")
    gathered = lax.all_gather(sum_shares(shares), "dp")
    grad_proj, grad_kernel, grad_bias = finish(gathered)
    return (block_output[None], grad_input[None], grad_query[None], grad_proj, grad_kernel, grad_bias[0])


def solution(mesh):
    device_fn = fast_device if fits_fast(mesh.shape) else general_device
    placed = (
        P("dp", "seq", None),
        P("dp", "seq", None),
        P("dp", "seq", None),
        P("dp", "seq", None),
        P("dp"),
        P(),
        P(),
        P(),
        P("dp", "seq", None),
    )
    return jax.shard_map(
        device_fn,
        mesh=mesh,
        in_specs=placed,
        out_specs=(
            P("dp", "seq", None),
            P("dp", "seq", None),
            P("dp", "seq", None),
            P("seq", None),
            P(None, "seq"),
            P("seq"),
        ),
        check_vma=False,
    )
```

```python
import functools
import math

import jax
import jax.numpy as jnp
from jax import lax
from jax.experimental import pallas as pl
from jax.experimental.pallas import tpu as pltpu
from jax.sharding import PartitionSpec as P

D = 1536
H = 8
HS = 96
KW = 31
HD = 768


def with_halo(x, sides, width):
    for axis, dim in sides:
        size, length = (lax.axis_size(axis), x.shape[dim])
        up = [(i, (i + 1) % size) for i in range(size - 1)]
        down = [(j, i) for i, j in up]
        last = lax.slice_in_dim(x, length - width, length, axis=dim)
        leading = lax.slice_in_dim(x, 0, width, axis=dim)
        before = lax.ppermute(last, axis, up)
        after = lax.ppermute(leading, axis, down)
        x = jnp.concatenate([before, x, after], axis=dim)
    return x


def forward_rows(query_one, key_one, value_one, key_valid, score_scale):
    row_total = query_one.shape[0]
    block_rows = math.gcd(row_total, 512)
    query_blocks = query_one.reshape(row_total // block_rows, block_rows, query_one.shape[1])

    def forward_one_block(query_block):
        scores = (
            lax.dot_general(
                query_block, key_one, (((1,), (1,)), ((), ())), preferred_element_type=jnp.float32
            )
            * score_scale
        )
        scores = jnp.where(key_valid[None, :], scores, -jnp.inf)
        row_top = jnp.max(scores, axis=-1, keepdims=True)
        log_total = row_top + jnp.log(jnp.sum(jnp.exp(scores - row_top), axis=-1, keepdims=True))
        weights = jnp.exp(scores - log_total).astype(jnp.bfloat16)
        return (jnp.dot(weights, value_one, preferred_element_type=jnp.float32), log_total[:, 0])

    outputs, log_totals = lax.map(forward_one_block, query_blocks)
    return (outputs.reshape(row_total, query_one.shape[1]), log_totals.reshape(row_total))


def backward_rows(
    query_one, key_one, value_one, grad_one, lse_one, delta_one, key_valid, score_scale
):
    row_total = query_one.shape[0]
    block_rows = math.gcd(row_total, 512)
    block_count = row_total // block_rows
    width = query_one.shape[1]

    def backward_one_block(items):
        query_block, grad_block, lse_block, delta_block = items
        scores = (
            lax.dot_general(
                query_block, key_one, (((1,), (1,)), ((), ())), preferred_element_type=jnp.float32
            )
            * score_scale
        )
        scores = jnp.where(key_valid[None, :], scores, -jnp.inf)
        probs = jnp.exp(scores - lse_block[:, None])
        grad_prob = lax.dot_general(
            grad_block, value_one, (((1,), (1,)), ((), ())), preferred_element_type=jnp.float32
        )
        grad_score = (probs * (grad_prob - delta_block[:, None])).astype(jnp.bfloat16)
        return jnp.dot(grad_score, key_one, preferred_element_type=jnp.float32) * score_scale

    results = lax.map(
        backward_one_block,
        (
            query_one.reshape(block_count, block_rows, width),
            grad_one.reshape(block_count, block_rows, width),
            lse_one.reshape(block_count, block_rows),
            delta_one.reshape(block_count, block_rows),
        ),
    )
    return results.reshape(row_total, width)


def general_device(
    block_input, query_proj, key_proj, value_proj, lengths, out_proj, kernel, conv_bias, grad_output
):
    frames_dev = block_input.shape[1]
    seq_count = lax.axis_size("seq")
    total_frames = frames_dev * seq_count
    first_frame = lax.axis_index("seq") * frames_dev
    utt_length = lengths[0]
    local_valid = first_frame + jnp.arange(frames_dev) < utt_length
    all_valid = jnp.arange(total_frames) < utt_length
    score_scale = 1.0 / math.sqrt(HS)
    halo_width = KW // 2
    group_size = seq_count // H
    sub_rows = frames_dev // group_size
    query_local = query_proj[0]

    def to_serving(matrix):
        return matrix.reshape(frames_dev, H, HS).transpose(1, 0, 2).reshape(seq_count, sub_rows, HS)

    def from_serving(returned):
        return returned.reshape(H, frames_dev, HS).transpose(1, 0, 2).reshape(frames_dev, HD)

    query_mine = lax.all_to_all(
        to_serving(query_local), "seq", split_axis=0, concat_axis=1, tiled=True
    )[0]
    key_send = jnp.repeat(
        key_proj[0].reshape(frames_dev, H, HS).transpose(1, 0, 2), group_size, axis=0
    )
    value_send = jnp.repeat(
        value_proj[0].reshape(frames_dev, H, HS).transpose(1, 0, 2), group_size, axis=0
    )
    key_mine, value_mine = (
        lax.all_to_all(key_send, "seq", split_axis=0, concat_axis=1, tiled=True),
        lax.all_to_all(value_send, "seq", split_axis=0, concat_axis=1, tiled=True),
    )
    key_mine = key_mine[0]
    value_mine = value_mine[0]
    head_out, head_lse = forward_rows(query_mine, key_mine, value_mine, all_valid, score_scale)
    head_attended = head_out.astype(jnp.bfloat16)
    attended = from_serving(
        lax.all_to_all(head_attended[None], "seq", split_axis=1, concat_axis=0, tiled=True)
    )
    projected = lax.dot_general(
        attended, out_proj, (((1,), (1,)), ((), ())), preferred_element_type=jnp.float32
    )
    mixed_rows = (block_input[0].astype(jnp.float32) + projected).astype(jnp.bfloat16)
    masked = jnp.where(local_valid[:, None], mixed_rows, jnp.zeros_like(mixed_rows))
    padded = with_halo(masked, (("seq", 0),), halo_width).astype(jnp.float32)
    conv_rows = jnp.broadcast_to(conv_bias, (frames_dev, D))
    for tap in range(KW):
        conv_rows = conv_rows + kernel[tap] * padded[tap : tap + frames_dev]
    gate_rows = jax.nn.sigmoid(conv_rows)
    block_output = jnp.where(
        local_valid[:, None], mixed_rows.astype(jnp.float32) + conv_rows * gate_rows, 0.0
    ).astype(jnp.bfloat16)
    grad_rows = jnp.where(local_valid[:, None], grad_output[0].astype(jnp.float32), 0.0)
    grad_conv = grad_rows * gate_rows * (1.0 + conv_rows * (1.0 - gate_rows))
    kernel_local = jnp.stack(
        [jnp.sum(grad_conv * padded[tap : tap + frames_dev], axis=0) for tap in range(KW)]
    )
    bias_local = jnp.sum(grad_conv, axis=0)
    grad_padded = with_halo(grad_conv, (("seq", 0),), halo_width)
    grad_masked = jnp.zeros((frames_dev, D), jnp.float32)
    for tap in range(KW):
        begin = 2 * halo_width - tap
        grad_masked = grad_masked + kernel[tap] * grad_padded[begin : begin + frames_dev]
    grad_input = (grad_rows + jnp.where(local_valid[:, None], grad_masked, 0.0)).astype(
        jnp.bfloat16
    )
    grad_attn = jnp.dot(grad_input, out_proj, preferred_element_type=jnp.float32).astype(
        jnp.bfloat16
    )
    grad_mine = lax.all_to_all(
        to_serving(grad_attn), "seq", split_axis=0, concat_axis=1, tiled=True
    )[0]
    delta_mine = jnp.sum(grad_mine.astype(jnp.float32) * head_attended.astype(jnp.float32), axis=-1)
    grad_q_mine = backward_rows(
        query_mine, key_mine, value_mine, grad_mine, head_lse, delta_mine, all_valid, score_scale
    ).astype(jnp.bfloat16)
    grad_query = from_serving(
        lax.all_to_all(grad_q_mine[None], "seq", split_axis=1, concat_axis=0, tiled=True)
    )
    term_block = lax.dot_general(
        grad_input, attended, (((0,), (0,)), ((), ())), preferred_element_type=jnp.float32
    )
    partial_rows = lax.psum_scatter(term_block, "seq", scatter_dimension=0, tiled=True)
    summed = lax.psum(partial_rows.astype(jnp.bfloat16), "dp").astype(jnp.float32)
    kernel_total, bias_total = lax.psum((kernel_local, bias_local), ("seq", "dp"))
    shard_width = D // seq_count
    offset = lax.axis_index("seq") * shard_width
    grad_kernel = lax.dynamic_slice_in_dim(kernel_total, offset, shard_width, 1)
    grad_bias = lax.dynamic_slice_in_dim(bias_total, offset, shard_width, 0)
    return (block_output[None], grad_input[None], grad_query[None], summed, grad_kernel, grad_bias)


BF16 = jnp.bfloat16
F32 = jnp.float32
TAP_ROWS = 32
WIDE = 32
SIDE = 16
CHUNK = 384
LANES = 128
MASKED_SCORE = -1e30
QUERIES, KEYS, VALUES = (slice(place * HS, (place + 1) * HS) for place in range(3))
VMEM_LIMIT = 40 * 1024 * 1024
SCORE_SCALE = 1.0 / math.sqrt(HS)
LOG2_SCALE = SCORE_SCALE * math.log2(math.e)


def fits_fast(sizes):
    seq_count, dp_count = sizes["seq"], sizes["dp"]
    piece = D // (seq_count * dp_count)
    return seq_count == H and dp_count * seq_count * piece == D and piece == 48


def params():
    return pltpu.CompilerParams(vmem_limit_bytes=VMEM_LIMIT)


def whole(shape):
    return pl.BlockSpec(shape, lambda *_: (0,) * len(shape))


def near(array):
    return pltpu.with_memory_space_constraint(array, pltpu.VMEM)


def far(array):
    return pltpu.with_memory_space_constraint(array, pltpu.HBM)


def here(count=None):
    spec = pl.BlockSpec(memory_space=pltpu.VMEM)
    return spec if count is None else [spec] * count


SCALARS = pl.BlockSpec(memory_space=pltpu.SMEM)


def pack_kernel(q_ref, k_ref, v_ref, out_ref):
    for place, ref in enumerate((q_ref, k_ref, v_ref)):
        frames = ref.shape[0]
        out_ref[:, place * HS : (place + 1) * HS, :] = ref[...].T.reshape(H, HS, frames)


def pack_heads(q, k, v):
    frames = q.shape[0]
    return pl.pallas_call(
        pack_kernel,
        out_shape=jax.ShapeDtypeStruct((H, 3 * HS, frames), BF16),
        compiler_params=params(),
        name="pack_heads",
    )(far(q), far(k), far(v))


def key_rows(x_ref, length, keys_sc):
    blocks, _, frames = x_ref.shape
    for block in range(blocks):
        row = lax.broadcasted_iota(jnp.int32, (LANES - HS, frames), 0)
        key = lax.broadcasted_iota(jnp.int32, (LANES - HS, frames), 1) + block * frames
        extra = jnp.where((row == 0) & (key >= length), MASKED_SCORE, 0.0)
        tall = jnp.concatenate([x_ref[block, KEYS].astype(F32), extra], axis=0)
        keys_sc[block * frames : (block + 1) * frames, :] = tall.T.astype(BF16)


def pair_of(ref, first, rows):
    return jnp.concatenate([ref[first, rows], ref[first + 1, rows]], axis=1)


def query_columns(x_ref, first):
    query = pair_of(x_ref, first, QUERIES)
    row = lax.broadcasted_iota(jnp.int32, (LANES - HS, query.shape[1]), 0)
    return jnp.concatenate([query, jnp.where(row == 0, 1.0, 0.0).astype(BF16)], axis=0)


def side_by_side(x_ref, rows, wide_sc):
    blocks, _, frames = x_ref.shape
    for block in range(blocks):
        wide_sc[:, block * frames : (block + 1) * frames] = x_ref[block, rows]


def forward_kernel(info_ref, x_ref, out_ref, lse_ref, keys_sc, values_sc):
    blocks, _, frames = x_ref.shape
    key_rows(x_ref, info_ref[1], keys_sc)
    side_by_side(x_ref, VALUES, values_sc)
    for first in range(0, blocks, 2):
        scores = jnp.dot(keys_sc[...], query_columns(x_ref, first), preferred_element_type=F32)
        scores = scores * LOG2_SCALE
        top = jnp.max(scores, axis=0, keepdims=True)
        raised = jnp.exp2(scores - top)
        total = jnp.sum(raised, axis=0, keepdims=True)
        weights = (raised * (1.0 / total)).astype(BF16)
        lse_ref[:, first * frames : (first + 2) * frames] = top + jnp.log2(total)
        mixed = jnp.dot(values_sc[...], weights, preferred_element_type=F32).astype(BF16)
        out_ref[first, :HS, :] = mixed[:, :frames]
        out_ref[first + 1, :HS, :] = mixed[:, frames:]

    lane = lax.broadcasted_iota(jnp.int32, (HS, frames), 1)
    nothing = jnp.zeros((HS, frames), F32)
    for block in range(blocks):
        left = nothing
        right = nothing
        if block > 0:
            left = pltpu.roll(out_ref[block - 1, :HS, :].astype(F32), WIDE, 1)
        if block < blocks - 1:
            right = pltpu.roll(out_ref[block + 1, :HS, :].astype(F32), WIDE, 1)
        both = jnp.where(lane < WIDE, left, right)
        lower = pltpu.roll(both[HS // 2 :], 2 * WIDE, 1)
        packed = jnp.where(lane[: HS // 2] < 2 * WIDE, both[: HS // 2], lower)
        out_ref[block, HS:, :] = packed.astype(BF16)


def forward_heads(info, received):
    blocks, _, frames = received.shape
    total = blocks * frames
    return pl.pallas_call(
        forward_kernel,
        in_specs=[SCALARS, here()],
        out_specs=here(2),
        out_shape=[
            jax.ShapeDtypeStruct((blocks, HS + HS // 2, frames), BF16),
            jax.ShapeDtypeStruct((1, total), F32),
        ],
        scratch_shapes=[pltpu.VMEM((total, LANES), BF16), pltpu.VMEM((HS, total), BF16)],
        compiler_params=params(),
        name="forward_heads",
    )(info, near(received))


def backward_kernel(info_ref, x_ref, grad_ref, head_ref, lse_ref, *rest):
    outs, (keys_sc, values_sc, wide_sc, result_sc) = rest[:-4], rest[-4:]
    blocks, _, frames = x_ref.shape
    key_rows(x_ref, info_ref[1], keys_sc)
    side_by_side(x_ref, KEYS, wide_sc)
    for block in range(blocks):
        rows = x_ref[block, VALUES].astype(F32).T.astype(BF16)
        values_sc[block * frames : (block + 1) * frames, :] = rows

    for first in range(0, blocks, 2):
        scores = jnp.dot(keys_sc[...], query_columns(x_ref, first), preferred_element_type=F32)
        probs = jnp.exp2(scores * LOG2_SCALE - lse_ref[:, first * frames : (first + 2) * frames])
        grad = pair_of(grad_ref, first, slice(0, HS))
        head = pair_of(head_ref, first, slice(0, HS))
        delta = jnp.sum(grad.astype(F32) * head.astype(F32), axis=0, keepdims=True)
        grad_prob = jnp.dot(values_sc[...], grad, preferred_element_type=F32)
        grad_score = (probs * (grad_prob - delta)).astype(BF16)
        result = jnp.dot(wide_sc[...], grad_score, preferred_element_type=F32) * SCORE_SCALE
        result_sc[first] = result[:, :frames].astype(BF16)
        result_sc[first + 1] = result[:, frames:].astype(BF16)
    for away, out_ref in enumerate(outs):
        out_ref[...] = result_sc[lax.rem(info_ref[3] + away, blocks)]


def backward_heads(info, received, grads, heads, lse):
    blocks, _, frames = received.shape
    total = blocks * frames
    return pl.pallas_call(
        backward_kernel,
        in_specs=[SCALARS] + here(4),
        out_specs=here(blocks),
        out_shape=[jax.ShapeDtypeStruct((HS, frames), BF16)] * blocks,
        scratch_shapes=[
            pltpu.VMEM((total, LANES), BF16),
            pltpu.VMEM((total, HS), BF16),
            pltpu.VMEM((HS, total), BF16),
            pltpu.VMEM((blocks, HS, frames), BF16),
        ],
        compiler_params=params(),
        name="backward_heads",
    )(info, near(received), near(grads), heads, lse)


def shifted_sum(ref, tile, rows, weight_of, start):
    total = start
    for low in range(8):
        base = ref[tile, low : low + rows + 24, :]
        for high in range(4):
            offset = 8 * high + low
            if 1 <= offset < TAP_ROWS:
                total = total + weight_of(offset) * base[8 * high : 8 * high + rows]
    return total


def middle_kernel(
    info_ref,
    att_ref,
    input_ref,
    cot_ref,
    before_ref,
    after_ref,
    proj_ref,
    tap_ref,
    bias_ref,
    block_out_ref,
    grad_in_ref,
    grad_heads_ref,
    *rest,
):
    piece_refs = rest[:-6]
    att_sc, grad_sc, masked_sc, gate_sc, taps_sc, piece_sc = rest[-6:]
    dp_count = len(piece_refs)
    step = pl.program_id(0)
    frames = input_ref.shape[0]
    tiles = CHUNK // LANES
    rows = frames + 2 * WIDE
    span = frames + 2 * SIDE
    first, length, mine = info_ref[0], info_ref[1], info_ref[2]

    @pl.when(step == 0)
    def _():
        main = att_ref[:, :HS, :].reshape(HD, frames)
        att_sc[WIDE : WIDE + frames, :] = main.T
        edge = att_ref[:, HS:, :].astype(F32).reshape(H * (HS // 2), frames)
        lower = pltpu.roll(edge, frames - 2 * WIDE, 1)
        half = (H, HS // 2, frames)
        tall = jnp.concatenate([edge.reshape(half), lower.reshape(half)], axis=1)
        turned = tall.reshape(HD, frames).T.astype(BF16)
        att_sc[:WIDE, :] = turned[:WIDE]
        att_sc[WIDE + frames :, :] = turned[WIDE : 2 * WIDE]
        grad_sc[...] = jnp.zeros_like(grad_sc)

    projected = lax.dot_general(
        att_sc[...], proj_ref[...], (((1,), (1,)), ((), ())), preferred_element_type=F32
    )
    chunk = pl.ds(pl.multiple_of(step * CHUNK, CHUNK), CHUNK)
    wide_input = jnp.concatenate(
        [before_ref[:WIDE, chunk], input_ref[...], after_ref[:WIDE, chunk]], axis=0
    ).astype(F32)
    mixed = (wide_input + projected).astype(BF16).astype(F32)
    frame = first - WIDE + lax.broadcasted_iota(jnp.int32, (rows, CHUNK), 0)
    valid = (frame >= 0) & (frame < length)
    masked = jnp.where(valid, mixed, 0.0)
    cot = jnp.concatenate(
        [before_ref[WIDE:, chunk], cot_ref[...], after_ref[WIDE:, chunk]], axis=0
    ).astype(F32)
    inner = slice(WIDE - SIDE, WIDE + SIDE + frames)
    cot = jnp.where(valid[inner], cot, 0.0)
    for tile in range(tiles):
        masked_sc[tile] = masked[:, tile * LANES : (tile + 1) * LANES]

    own = slice(SIDE, SIDE + frames)
    inside = valid[WIDE : WIDE + frames, :LANES]
    for tile in range(tiles):
        lanes = slice(tile * LANES, (tile + 1) * LANES)
        start = jnp.broadcast_to(bias_ref[:, lanes], (span, LANES))
        conv = shifted_sum(
            masked_sc, tile, span, lambda offset: tap_ref[offset - 1 : offset, lanes], start
        )
        gate = lax.logistic(conv)
        center = masked_sc[tile, WIDE : WIDE + frames, :]
        block_out_ref[:, lanes] = jnp.where(inside, center + conv[own] * gate[own], 0.0).astype(BF16)
        gated = cot[:, lanes] * gate * (1.0 + conv * (1.0 - gate))
        gate_sc[tile] = gated
        owned = gated[own]
        for low in range(8):
            base = masked_sc[tile, SIDE + low : SIDE + low + frames + 24, :]
            for high in range(4):
                offset = 8 * high + low
                if 1 <= offset < TAP_ROWS:
                    product = owned * base[8 * high : 8 * high + frames]
                    taps_sc[offset - 1, :, lanes] = product.reshape(frames // 8, 8, LANES).sum(0)
        taps_sc[TAP_ROWS - 1, :, lanes] = owned.reshape(frames // 8, 8, LANES).sum(0)
        back = shifted_sum(
            gate_sc,
            tile,
            frames,
            lambda offset: tap_ref[KW - offset : KW - offset + 1, lanes],
            jnp.zeros((frames, LANES), F32),
        )
        grad_in_ref[:, lanes] = (cot[own, lanes] + jnp.where(inside, back, 0.0)).astype(BF16)

    grad_in = grad_in_ref[...]
    grad_sc[...] += jnp.dot(grad_in, proj_ref[...], preferred_element_type=F32)

    piece = 48
    half = piece // 2
    slabs = CHUNK // (dp_count * piece)
    turned = grad_in.T.reshape(slabs * dp_count, piece, frames)
    taps = jnp.sum(taps_sc[...], axis=1)
    high_part = taps.astype(BF16).astype(F32)
    low_part = taps - high_part
    four = jnp.concatenate([high_part, low_part, high_part, low_part], axis=0)
    tall = four.T.reshape(slabs * dp_count, piece, LANES)
    lane = lax.broadcasted_iota(jnp.int32, (half, LANES), 1)
    slab_count = D // (dp_count * piece)
    for owner in range(dp_count):
        packed = []
        for slab in range(slabs):
            source = slab * dp_count + owner
            where = pl.multiple_of((step * slabs + slab) * piece, piece)
            piece_sc[owner, pl.ds(where, piece), :] = turned[source]
            packed.append(
                jnp.where(lane < LANES // 2, tall[source, :half], tall[source, half:])
            )
        where = pl.multiple_of(slab_count * piece + step * slabs * half, slabs * half)
        piece_sc[owner, pl.ds(where, slabs * half), :] = jnp.concatenate(packed, axis=0).astype(BF16)

    @pl.when(step == pl.num_programs(0) - 1)
    def _():
        grad_heads_ref[...] = grad_sc[...].T.astype(BF16).reshape(H, HS, frames)
        for away, ref in enumerate(piece_refs):
            ref[...] = piece_sc[lax.rem(mine + away, dp_count)]


def middle(info, returned, block_input, grad_output, before, after, out_proj, kernel, bias, dp_count):
    frames = block_input.shape[0]
    piece_rows = D // dp_count + D // dp_count // 2
    column = lambda count: pl.BlockSpec((count, CHUNK), lambda i: (0, i))
    return pl.pallas_call(
        middle_kernel,
        grid=(D // CHUNK,),
        in_specs=[
            SCALARS,
            here(),
            column(frames),
            column(frames),
            here(),
            here(),
            pl.BlockSpec((CHUNK, HD), lambda i: (i, 0)),
            column(KW),
            column(1),
        ],
        out_specs=[
            column(frames),
            column(frames),
            whole((H, HS, frames)),
        ]
        + [whole((piece_rows, frames))] * dp_count,
        out_shape=[
            jax.ShapeDtypeStruct((frames, D), BF16),
            jax.ShapeDtypeStruct((frames, D), BF16),
            jax.ShapeDtypeStruct((H, HS, frames), BF16),
        ]
        + [jax.ShapeDtypeStruct((piece_rows, frames), BF16)] * dp_count,
        scratch_shapes=[
            pltpu.VMEM((frames + 2 * WIDE, HD), BF16),
            pltpu.VMEM((frames, HD), F32),
            pltpu.VMEM((CHUNK // LANES, frames + 2 * WIDE, LANES), F32),
            pltpu.VMEM((CHUNK // LANES, frames + 2 * SIDE, LANES), F32),
            pltpu.VMEM((TAP_ROWS, 8, CHUNK), F32),
            pltpu.VMEM((dp_count, piece_rows, frames), BF16),
        ],
        compiler_params=params(),
        name="middle",
    )(
        info,
        near(returned),
        far(block_input),
        far(grad_output),
        near(before),
        near(after),
        far(out_proj),
        far(kernel),
        bias,
    )


def split_parts(lane, value):
    high_part = value.astype(BF16).astype(F32)
    low_part = pltpu.roll(value - high_part, TAP_ROWS, 1)
    return jnp.where(lane % (2 * TAP_ROWS) < TAP_ROWS, high_part, low_part)


def join_parts(value):
    return value + pltpu.roll(value, LANES - TAP_ROWS, 1)


def store_share(out_ref, share, taps):
    piece = share.shape[-2]
    for tile in range(HD // LANES):
        rows = slice(tile * piece, (tile + 1) * piece)
        out_ref[..., rows, :] = share[..., tile * LANES : (tile + 1) * LANES].astype(BF16)
    out_ref[..., HD // LANES * piece :, :] = taps.astype(BF16)


def product_kernel(*refs):
    out_ref = refs[-1]
    count = (len(refs) - 1) // 2
    pieces, heads = refs[:count], refs[count : 2 * count]
    slabs = out_ref.shape[0]
    frames = pieces[0].shape[1]
    height = pieces[0].shape[0] * 2 // 3
    piece = height // slabs
    total = jnp.zeros((height, HD), F32)
    taps = jnp.zeros((height // 2, frames), F32)
    for piece_ref, head_ref in zip(pieces, heads):
        total += lax.dot_general(
            piece_ref[:height, :],
            head_ref[:, :HS, :].reshape(HD, frames),
            (((1,), (1,)), ((), ())),
            preferred_element_type=F32,
        )
        taps += piece_ref[height:, :].astype(F32)
    lane = lax.broadcasted_iota(jnp.int32, taps.shape, 1)
    parts = split_parts(lane, join_parts(taps)).reshape(slabs, piece // 2, LANES)
    store_share(out_ref, total.reshape(slabs, piece, HD), parts)


def product(pieces, heads, returned, seq_count):
    height = pieces[0].shape[0] * 2 // 3
    piece = height // seq_count
    share_rows = piece * HD // LANES + piece // 2
    near_heads = [near(array) for array in [returned, *heads]]
    near_pieces = [pieces[0]] + [near(array) for array in pieces[1:]]
    return pl.pallas_call(
        product_kernel,
        in_specs=here(2 * len(pieces)),
        out_specs=here(),
        out_shape=jax.ShapeDtypeStruct((seq_count, share_rows, LANES), BF16),
        compiler_params=params(),
        name="product",
    )(*near_pieces, *near_heads)


def sum_kernel(in_ref, out_ref):
    total = jnp.sum(in_ref[...].astype(F32), axis=0)
    rows = total.shape[0] * 12 // 13
    out_ref[:rows, :] = total[:rows].astype(BF16)
    taps = total[rows:]
    lane = lax.broadcasted_iota(jnp.int32, taps.shape, 1)
    out_ref[rows:, :] = split_parts(lane, join_parts(taps)).astype(BF16)


def sum_shares(shares):
    return pl.pallas_call(
        sum_kernel,
        in_specs=[here()],
        out_specs=here(),
        out_shape=jax.ShapeDtypeStruct(shares.shape[1:], BF16),
        compiler_params=params(),
        name="sum_shares",
    )(near(shares))


def finish_kernel(in_ref, proj_ref, tap_ref, bias_ref):
    owners, share_rows, _ = in_ref.shape
    rows = share_rows * 12 // 13
    piece = rows * LANES // HD
    columns = []
    for owner in range(owners):
        for tile in range(HD // LANES):
            part = in_ref[owner, tile * piece : (tile + 1) * piece, :].astype(F32)
            proj_ref[owner * piece : (owner + 1) * piece, tile * LANES : (tile + 1) * LANES] = part
        taps = join_parts(in_ref[owner, rows:, :].astype(F32))
        columns += [taps, pltpu.roll(taps, LANES // 2, 1)]
    turned = jnp.concatenate(columns, axis=0).T
    tap_ref[...] = turned[:KW]
    bias_ref[...] = turned[KW : KW + 1]


def finish(gathered):
    owners, share_rows, _ = gathered.shape
    width = owners * share_rows * 12 // 13 * LANES // HD
    return pl.pallas_call(
        finish_kernel,
        in_specs=[here()],
        out_specs=here(3),
        out_shape=[
            jax.ShapeDtypeStruct((width, HD), F32),
            jax.ShapeDtypeStruct((KW, width), F32),
            jax.ShapeDtypeStruct((1, width), F32),
        ],
        compiler_params=params(),
        name="finish",
    )(near(gathered))


def unpack_kernel(info_ref, *refs):
    heads, out_ref, heads_sc = refs[:-2], refs[-2], refs[-1]
    for away, head_ref in enumerate(heads):
        heads_sc[lax.rem(info_ref[3] - away + H, H)] = head_ref[...]
    out_ref[...] = heads_sc[...].reshape(HD, heads_sc.shape[2]).T


def unpack_heads(info, heads):
    frames = heads[0].shape[1]
    return pl.pallas_call(
        unpack_kernel,
        in_specs=[SCALARS] + here(H),
        out_specs=here(),
        out_shape=jax.ShapeDtypeStruct((frames, HD), BF16),
        scratch_shapes=[pltpu.VMEM((H, HS, frames), BF16)],
        compiler_params=params(),
        name="unpack_heads",
    )(info, heads[0], *[near(head) for head in heads[1:]])


def ring(count, away):
    return [(i, (i + away) % count) for i in range(count)]


def send_round(blocks, axis):
    count = len(blocks)
    return [blocks[0]] + [
        lax.ppermute(blocks[away], axis, ring(count, away)) for away in range(1, count)
    ]


def exchange(blocks, axis):
    return lax.all_to_all(blocks, axis, split_axis=0, concat_axis=0, tiled=True)


def fast_device(
    block_input, query_proj, key_proj, value_proj, lengths, out_proj, kernel, conv_bias, grad_output
):
    frames = block_input.shape[1]
    seq_count = lax.axis_size("seq")
    dp_count = lax.axis_size("dp")
    place = lax.axis_index("seq")
    info = jnp.stack([place * frames, lengths[0], lax.axis_index("dp"), place]).astype(jnp.int32)
    bias_row = conv_bias[None]

    received = exchange(pack_heads(query_proj[0], key_proj[0], value_proj[0]), "seq")

    last = jnp.concatenate([block_input[0, frames - WIDE :], grad_output[0, frames - SIDE :]])
    leading = jnp.concatenate([block_input[0, :WIDE], grad_output[0, :SIDE]])
    up = [(i, i + 1) for i in range(seq_count - 1)]
    down = [(j, i) for i, j in up]
    before = lax.ppermute(last, "seq", up)
    after = lax.ppermute(leading, "seq", down)
    received, before, after, info, bias_row = lax.optimization_barrier(
        (received, before, after, info, bias_row)
    )

    sent, lse = forward_heads(info, received)
    returned = exchange(sent, "seq")
    mine = returned[:, :HS]
    heads = send_round([mine] * dp_count, "dp")[1:]
    block_output, grad_input, grad_heads, *pieces = middle(
        info,
        returned,
        block_input[0],
        grad_output[0],
        before,
        after,
        out_proj,
        kernel,
        bias_row,
        dp_count,
    )
    grad_heads, heads, pieces = lax.optimization_barrier((grad_heads, heads, pieces))

    grads = exchange(grad_heads, "seq")
    moved = send_round(pieces, "dp")
    grads, moved = lax.optimization_barrier((grads, moved))
    shares = product(moved, heads, returned, seq_count)
    shares, grads = lax.optimization_barrier((shares, grads))
    shares = exchange(shares, "seq")
    query_parts = send_round(backward_heads(info, received, grads, sent, lse), "seq")
    shares, query_parts = lax.optimization_barrier((shares, query_parts))
    grad_query = unpack_heads(info, query_parts)
    gathered = lax.all_gather(sum_shares(shares), "dp")
    grad_proj, grad_kernel, grad_bias = finish(gathered)
    return (block_output[None], grad_input[None], grad_query[None], grad_proj, grad_kernel, grad_bias[0])


def solution(mesh):
    device_fn = fast_device if fits_fast(mesh.shape) else general_device
    placed = (
        P("dp", "seq", None),
        P("dp", "seq", None),
        P("dp", "seq", None),
        P("dp", "seq", None),
        P("dp"),
        P(),
        P(),
        P(),
        P("dp", "seq", None),
    )
    return jax.shard_map(
        device_fn,
        mesh=mesh,
        in_specs=placed,
        out_specs=(
            P("dp", "seq", None),
            P("dp", "seq", None),
            P("dp", "seq", None),
            P("seq", None),
            P(None, "seq"),
            P("seq"),
        ),
        check_vma=False,
    )
```

```python
import functools
import math

import jax
import jax.numpy as jnp
from jax import lax
from jax.experimental import pallas as pl
from jax.experimental.pallas import tpu as pltpu
from jax.sharding import PartitionSpec as P

D = 1536
H = 8
HS = 96
KW = 31
HD = 768


def with_halo(x, sides, width):
    for axis, dim in sides:
        size, length = (lax.axis_size(axis), x.shape[dim])
        up = [(i, (i + 1) % size) for i in range(size - 1)]
        down = [(j, i) for i, j in up]
        last = lax.slice_in_dim(x, length - width, length, axis=dim)
        leading = lax.slice_in_dim(x, 0, width, axis=dim)
        before = lax.ppermute(last, axis, up)
        after = lax.ppermute(leading, axis, down)
        x = jnp.concatenate([before, x, after], axis=dim)
    return x


def forward_rows(query_one, key_one, value_one, key_valid, score_scale):
    row_total = query_one.shape[0]
    block_rows = math.gcd(row_total, 512)
    query_blocks = query_one.reshape(row_total // block_rows, block_rows, query_one.shape[1])

    def forward_one_block(query_block):
        scores = (
            lax.dot_general(
                query_block, key_one, (((1,), (1,)), ((), ())), preferred_element_type=jnp.float32
            )
            * score_scale
        )
        scores = jnp.where(key_valid[None, :], scores, -jnp.inf)
        row_top = jnp.max(scores, axis=-1, keepdims=True)
        log_total = row_top + jnp.log(jnp.sum(jnp.exp(scores - row_top), axis=-1, keepdims=True))
        weights = jnp.exp(scores - log_total).astype(jnp.bfloat16)
        return (jnp.dot(weights, value_one, preferred_element_type=jnp.float32), log_total[:, 0])

    outputs, log_totals = lax.map(forward_one_block, query_blocks)
    return (outputs.reshape(row_total, query_one.shape[1]), log_totals.reshape(row_total))


def backward_rows(
    query_one, key_one, value_one, grad_one, lse_one, delta_one, key_valid, score_scale
):
    row_total = query_one.shape[0]
    block_rows = math.gcd(row_total, 512)
    block_count = row_total // block_rows
    width = query_one.shape[1]

    def backward_one_block(items):
        query_block, grad_block, lse_block, delta_block = items
        scores = (
            lax.dot_general(
                query_block, key_one, (((1,), (1,)), ((), ())), preferred_element_type=jnp.float32
            )
            * score_scale
        )
        scores = jnp.where(key_valid[None, :], scores, -jnp.inf)
        probs = jnp.exp(scores - lse_block[:, None])
        grad_prob = lax.dot_general(
            grad_block, value_one, (((1,), (1,)), ((), ())), preferred_element_type=jnp.float32
        )
        grad_score = (probs * (grad_prob - delta_block[:, None])).astype(jnp.bfloat16)
        return jnp.dot(grad_score, key_one, preferred_element_type=jnp.float32) * score_scale

    results = lax.map(
        backward_one_block,
        (
            query_one.reshape(block_count, block_rows, width),
            grad_one.reshape(block_count, block_rows, width),
            lse_one.reshape(block_count, block_rows),
            delta_one.reshape(block_count, block_rows),
        ),
    )
    return results.reshape(row_total, width)


def general_device(
    block_input, query_proj, key_proj, value_proj, lengths, out_proj, kernel, conv_bias, grad_output
):
    frames_dev = block_input.shape[1]
    seq_count = lax.axis_size("seq")
    total_frames = frames_dev * seq_count
    first_frame = lax.axis_index("seq") * frames_dev
    utt_length = lengths[0]
    local_valid = first_frame + jnp.arange(frames_dev) < utt_length
    all_valid = jnp.arange(total_frames) < utt_length
    score_scale = 1.0 / math.sqrt(HS)
    halo_width = KW // 2
    group_size = seq_count // H
    sub_rows = frames_dev // group_size
    query_local = query_proj[0]

    def to_serving(matrix):
        return matrix.reshape(frames_dev, H, HS).transpose(1, 0, 2).reshape(seq_count, sub_rows, HS)

    def from_serving(returned):
        return returned.reshape(H, frames_dev, HS).transpose(1, 0, 2).reshape(frames_dev, HD)

    query_mine = lax.all_to_all(
        to_serving(query_local), "seq", split_axis=0, concat_axis=1, tiled=True
    )[0]
    key_send = jnp.repeat(
        key_proj[0].reshape(frames_dev, H, HS).transpose(1, 0, 2), group_size, axis=0
    )
    value_send = jnp.repeat(
        value_proj[0].reshape(frames_dev, H, HS).transpose(1, 0, 2), group_size, axis=0
    )
    key_mine, value_mine = (
        lax.all_to_all(key_send, "seq", split_axis=0, concat_axis=1, tiled=True),
        lax.all_to_all(value_send, "seq", split_axis=0, concat_axis=1, tiled=True),
    )
    key_mine = key_mine[0]
    value_mine = value_mine[0]
    head_out, head_lse = forward_rows(query_mine, key_mine, value_mine, all_valid, score_scale)
    head_attended = head_out.astype(jnp.bfloat16)
    attended = from_serving(
        lax.all_to_all(head_attended[None], "seq", split_axis=1, concat_axis=0, tiled=True)
    )
    projected = lax.dot_general(
        attended, out_proj, (((1,), (1,)), ((), ())), preferred_element_type=jnp.float32
    )
    mixed_rows = (block_input[0].astype(jnp.float32) + projected).astype(jnp.bfloat16)
    masked = jnp.where(local_valid[:, None], mixed_rows, jnp.zeros_like(mixed_rows))
    padded = with_halo(masked, (("seq", 0),), halo_width).astype(jnp.float32)
    conv_rows = jnp.broadcast_to(conv_bias, (frames_dev, D))
    for tap in range(KW):
        conv_rows = conv_rows + kernel[tap] * padded[tap : tap + frames_dev]
    gate_rows = jax.nn.sigmoid(conv_rows)
    block_output = jnp.where(
        local_valid[:, None], mixed_rows.astype(jnp.float32) + conv_rows * gate_rows, 0.0
    ).astype(jnp.bfloat16)
    grad_rows = jnp.where(local_valid[:, None], grad_output[0].astype(jnp.float32), 0.0)
    grad_conv = grad_rows * gate_rows * (1.0 + conv_rows * (1.0 - gate_rows))
    kernel_local = jnp.stack(
        [jnp.sum(grad_conv * padded[tap : tap + frames_dev], axis=0) for tap in range(KW)]
    )
    bias_local = jnp.sum(grad_conv, axis=0)
    grad_padded = with_halo(grad_conv, (("seq", 0),), halo_width)
    grad_masked = jnp.zeros((frames_dev, D), jnp.float32)
    for tap in range(KW):
        begin = 2 * halo_width - tap
        grad_masked = grad_masked + kernel[tap] * grad_padded[begin : begin + frames_dev]
    grad_input = (grad_rows + jnp.where(local_valid[:, None], grad_masked, 0.0)).astype(
        jnp.bfloat16
    )
    grad_attn = jnp.dot(grad_input, out_proj, preferred_element_type=jnp.float32).astype(
        jnp.bfloat16
    )
    grad_mine = lax.all_to_all(
        to_serving(grad_attn), "seq", split_axis=0, concat_axis=1, tiled=True
    )[0]
    delta_mine = jnp.sum(grad_mine.astype(jnp.float32) * head_attended.astype(jnp.float32), axis=-1)
    grad_q_mine = backward_rows(
        query_mine, key_mine, value_mine, grad_mine, head_lse, delta_mine, all_valid, score_scale
    ).astype(jnp.bfloat16)
    grad_query = from_serving(
        lax.all_to_all(grad_q_mine[None], "seq", split_axis=1, concat_axis=0, tiled=True)
    )
    term_block = lax.dot_general(
        grad_input, attended, (((0,), (0,)), ((), ())), preferred_element_type=jnp.float32
    )
    partial_rows = lax.psum_scatter(term_block, "seq", scatter_dimension=0, tiled=True)
    summed = lax.psum(partial_rows.astype(jnp.bfloat16), "dp").astype(jnp.float32)
    kernel_total, bias_total = lax.psum((kernel_local, bias_local), ("seq", "dp"))
    shard_width = D // seq_count
    offset = lax.axis_index("seq") * shard_width
    grad_kernel = lax.dynamic_slice_in_dim(kernel_total, offset, shard_width, 1)
    grad_bias = lax.dynamic_slice_in_dim(bias_total, offset, shard_width, 0)
    return (block_output[None], grad_input[None], grad_query[None], summed, grad_kernel, grad_bias)


BF16 = jnp.bfloat16
F32 = jnp.float32
TAP_ROWS = 32
WIDE = 32
SIDE = 16
CHUNK = 384
LANES = 128
MASKED_SCORE = -1e30
QUERIES, KEYS, VALUES = (slice(place * HS, (place + 1) * HS) for place in range(3))
VMEM_LIMIT = 40 * 1024 * 1024
SCORE_SCALE = 1.0 / math.sqrt(HS)
LOG2_SCALE = SCORE_SCALE * math.log2(math.e)


def fits_fast(sizes):
    seq_count, dp_count = sizes["seq"], sizes["dp"]
    piece = D // (seq_count * dp_count)
    return seq_count == H and dp_count * seq_count * piece == D and piece == 48


def params():
    return pltpu.CompilerParams(vmem_limit_bytes=VMEM_LIMIT)


def whole(shape):
    return pl.BlockSpec(shape, lambda *_: (0,) * len(shape))


def near(array):
    return pltpu.with_memory_space_constraint(array, pltpu.VMEM)


def far(array):
    return pltpu.with_memory_space_constraint(array, pltpu.HBM)


def here(count=None):
    spec = pl.BlockSpec(memory_space=pltpu.VMEM)
    return spec if count is None else [spec] * count


SCALARS = pl.BlockSpec(memory_space=pltpu.SMEM)


def pack_kernel(q_ref, k_ref, v_ref, out_ref):
    for place, ref in enumerate((q_ref, k_ref, v_ref)):
        frames = ref.shape[0]
        out_ref[:, place * HS : (place + 1) * HS, :] = ref[...].T.reshape(H, HS, frames)


def pack_heads(q, k, v):
    frames = q.shape[0]
    return pl.pallas_call(
        pack_kernel,
        out_shape=jax.ShapeDtypeStruct((H, 3 * HS, frames), BF16),
        compiler_params=params(),
        name="pack_heads",
    )(far(q), far(k), far(v))


def key_rows(x_ref, length, keys_sc):
    blocks, _, frames = x_ref.shape
    for block in range(blocks):
        row = lax.broadcasted_iota(jnp.int32, (LANES - HS, frames), 0)
        key = lax.broadcasted_iota(jnp.int32, (LANES - HS, frames), 1) + block * frames
        extra = jnp.where((row == 0) & (key >= length), MASKED_SCORE, 0.0)
        tall = jnp.concatenate([x_ref[block, KEYS].astype(F32), extra], axis=0)
        keys_sc[block * frames : (block + 1) * frames, :] = tall.T.astype(BF16)


def pair_of(ref, first, rows):
    return jnp.concatenate([ref[first, rows], ref[first + 1, rows]], axis=1)


def query_columns(x_ref, first):
    query = pair_of(x_ref, first, QUERIES)
    row = lax.broadcasted_iota(jnp.int32, (LANES - HS, query.shape[1]), 0)
    return jnp.concatenate([query, jnp.where(row == 0, 1.0, 0.0).astype(BF16)], axis=0)


def side_by_side(x_ref, rows, wide_sc):
    blocks, _, frames = x_ref.shape
    for block in range(blocks):
        wide_sc[:, block * frames : (block + 1) * frames] = x_ref[block, rows]


def forward_kernel(info_ref, x_ref, out_ref, lse_ref, keys_sc, values_sc):
    blocks, _, frames = x_ref.shape
    key_rows(x_ref, info_ref[1], keys_sc)
    side_by_side(x_ref, VALUES, values_sc)
    for first in range(0, blocks, 2):
        scores = jnp.dot(keys_sc[...], query_columns(x_ref, first), preferred_element_type=F32)
        scores = scores * LOG2_SCALE
        top = jnp.max(scores, axis=0, keepdims=True)
        raised = jnp.exp2(scores - top)
        total = jnp.sum(raised, axis=0, keepdims=True)
        weights = (raised * (1.0 / total)).astype(BF16)
        lse_ref[:, first * frames : (first + 2) * frames] = top + jnp.log2(total)
        mixed = jnp.dot(values_sc[...], weights, preferred_element_type=F32).astype(BF16)
        out_ref[first, :HS, :] = mixed[:, :frames]
        out_ref[first + 1, :HS, :] = mixed[:, frames:]

    lane = lax.broadcasted_iota(jnp.int32, (HS, frames), 1)
    nothing = jnp.zeros((HS, frames), F32)
    for block in range(blocks):
        left = nothing
        right = nothing
        if block > 0:
            left = pltpu.roll(out_ref[block - 1, :HS, :].astype(F32), WIDE, 1)
        if block < blocks - 1:
            right = pltpu.roll(out_ref[block + 1, :HS, :].astype(F32), WIDE, 1)
        both = jnp.where(lane < WIDE, left, right)
        lower = pltpu.roll(both[HS // 2 :], 2 * WIDE, 1)
        packed = jnp.where(lane[: HS // 2] < 2 * WIDE, both[: HS // 2], lower)
        out_ref[block, HS:, :] = packed.astype(BF16)


def forward_heads(info, received):
    blocks, _, frames = received.shape
    total = blocks * frames
    return pl.pallas_call(
        forward_kernel,
        in_specs=[SCALARS, here()],
        out_specs=here(2),
        out_shape=[
            jax.ShapeDtypeStruct((blocks, HS + HS // 2, frames), BF16),
            jax.ShapeDtypeStruct((1, total), F32),
        ],
        scratch_shapes=[pltpu.VMEM((total, LANES), BF16), pltpu.VMEM((HS, total), BF16)],
        compiler_params=params(),
        name="forward_heads",
    )(info, near(received))


def backward_kernel(info_ref, x_ref, grad_ref, head_ref, lse_ref, *rest):
    keep_ref, give_ref, keys_sc, values_sc, wide_sc, result_sc = rest
    blocks, _, frames = x_ref.shape
    key_rows(x_ref, info_ref[1], keys_sc)
    side_by_side(x_ref, KEYS, wide_sc)
    for block in range(blocks):
        rows = x_ref[block, VALUES].astype(F32).T.astype(BF16)
        values_sc[block * frames : (block + 1) * frames, :] = rows

    for first in range(0, blocks, 2):
        scores = jnp.dot(keys_sc[...], query_columns(x_ref, first), preferred_element_type=F32)
        probs = jnp.exp2(scores * LOG2_SCALE - lse_ref[:, first * frames : (first + 2) * frames])
        grad = pair_of(grad_ref, first, slice(0, HS))
        head = pair_of(head_ref, first, slice(0, HS))
        delta = jnp.sum(grad.astype(F32) * head.astype(F32), axis=0, keepdims=True)
        grad_prob = jnp.dot(values_sc[...], grad, preferred_element_type=F32)
        grad_score = (probs * (grad_prob - delta)).astype(BF16)
        result = jnp.dot(wide_sc[...], grad_score, preferred_element_type=F32) * SCORE_SCALE
        result_sc[first] = result[:, :frames].astype(BF16)
        result_sc[first + 1] = result[:, frames:].astype(BF16)
    side = lax.rem(info_ref[3], 2)
    for layer in range(blocks // 2):
        keep_ref[layer] = result_sc[2 * layer + side]
        give_ref[layer] = result_sc[2 * layer + 1 - side]


def backward_heads(info, received, grads, heads, lse):
    blocks, _, frames = received.shape
    total = blocks * frames
    return pl.pallas_call(
        backward_kernel,
        in_specs=[SCALARS] + here(4),
        out_specs=here(2),
        out_shape=[jax.ShapeDtypeStruct((blocks // 2, HS, frames), BF16)] * 2,
        scratch_shapes=[
            pltpu.VMEM((total, LANES), BF16),
            pltpu.VMEM((total, HS), BF16),
            pltpu.VMEM((HS, total), BF16),
            pltpu.VMEM((blocks, HS, frames), BF16),
        ],
        compiler_params=params(),
        name="backward_heads",
    )(info, near(received), near(grads), heads, lse)


def shifted_sum(ref, tile, rows, weight_of, start):
    total = start
    for low in range(8):
        base = ref[tile, low : low + rows + 24, :]
        for high in range(4):
            offset = 8 * high + low
            if 1 <= offset < TAP_ROWS:
                total = total + weight_of(offset) * base[8 * high : 8 * high + rows]
    return total


def middle_kernel(
    info_ref,
    att_ref,
    input_ref,
    cot_ref,
    before_ref,
    after_ref,
    proj_ref,
    tap_ref,
    bias_ref,
    block_out_ref,
    grad_in_ref,
    grad_heads_ref,
    *rest,
):
    piece_refs = rest[:-6]
    att_sc, grad_sc, masked_sc, gate_sc, taps_sc, piece_sc = rest[-6:]
    dp_count = len(piece_refs)
    step = pl.program_id(0)
    frames = input_ref.shape[0]
    tiles = CHUNK // LANES
    rows = frames + 2 * WIDE
    span = frames + 2 * SIDE
    first, length, mine = info_ref[0], info_ref[1], info_ref[2]

    @pl.when(step == 0)
    def _():
        main = att_ref[:, :HS, :].reshape(HD, frames)
        att_sc[WIDE : WIDE + frames, :] = main.T
        edge = att_ref[:, HS:, :].astype(F32).reshape(H * (HS // 2), frames)
        lower = pltpu.roll(edge, frames - 2 * WIDE, 1)
        half = (H, HS // 2, frames)
        tall = jnp.concatenate([edge.reshape(half), lower.reshape(half)], axis=1)
        turned = tall.reshape(HD, frames).T.astype(BF16)
        att_sc[:WIDE, :] = turned[:WIDE]
        att_sc[WIDE + frames :, :] = turned[WIDE : 2 * WIDE]
        grad_sc[...] = jnp.zeros_like(grad_sc)

    projected = lax.dot_general(
        att_sc[...], proj_ref[...], (((1,), (1,)), ((), ())), preferred_element_type=F32
    )
    chunk = pl.ds(pl.multiple_of(step * CHUNK, CHUNK), CHUNK)
    wide_input = jnp.concatenate(
        [before_ref[:WIDE, chunk], input_ref[...], after_ref[:WIDE, chunk]], axis=0
    ).astype(F32)
    mixed = (wide_input + projected).astype(BF16).astype(F32)
    frame = first - WIDE + lax.broadcasted_iota(jnp.int32, (rows, CHUNK), 0)
    valid = (frame >= 0) & (frame < length)
    masked = jnp.where(valid, mixed, 0.0)
    cot = jnp.concatenate(
        [before_ref[WIDE:, chunk], cot_ref[...], after_ref[WIDE:, chunk]], axis=0
    ).astype(F32)
    inner = slice(WIDE - SIDE, WIDE + SIDE + frames)
    cot = jnp.where(valid[inner], cot, 0.0)
    for tile in range(tiles):
        masked_sc[tile] = masked[:, tile * LANES : (tile + 1) * LANES]

    own = slice(SIDE, SIDE + frames)
    inside = valid[WIDE : WIDE + frames, :LANES]
    for tile in range(tiles):
        lanes = slice(tile * LANES, (tile + 1) * LANES)
        start = jnp.broadcast_to(bias_ref[:, lanes], (span, LANES))
        conv = shifted_sum(
            masked_sc, tile, span, lambda offset: tap_ref[offset - 1 : offset, lanes], start
        )
        gate = lax.logistic(conv)
        center = masked_sc[tile, WIDE : WIDE + frames, :]
        block_out_ref[:, lanes] = jnp.where(inside, center + conv[own] * gate[own], 0.0).astype(BF16)
        gated = cot[:, lanes] * gate * (1.0 + conv * (1.0 - gate))
        gate_sc[tile] = gated
        owned = gated[own]
        for low in range(8):
            base = masked_sc[tile, SIDE + low : SIDE + low + frames + 24, :]
            for high in range(4):
                offset = 8 * high + low
                if 1 <= offset < TAP_ROWS:
                    product = owned * base[8 * high : 8 * high + frames]
                    taps_sc[offset - 1, :, lanes] = product.reshape(frames // 8, 8, LANES).sum(0)
        taps_sc[TAP_ROWS - 1, :, lanes] = owned.reshape(frames // 8, 8, LANES).sum(0)
        back = shifted_sum(
            gate_sc,
            tile,
            frames,
            lambda offset: tap_ref[KW - offset : KW - offset + 1, lanes],
            jnp.zeros((frames, LANES), F32),
        )
        grad_in_ref[:, lanes] = (cot[own, lanes] + jnp.where(inside, back, 0.0)).astype(BF16)

    grad_in = grad_in_ref[...]
    grad_sc[...] += jnp.dot(grad_in, proj_ref[...], preferred_element_type=F32)

    piece = 48
    half = piece // 2
    slabs = CHUNK // (dp_count * piece)
    turned = grad_in.T.reshape(slabs * dp_count, piece, frames)
    taps = jnp.sum(taps_sc[...], axis=1)
    high_part = taps.astype(BF16).astype(F32)
    low_part = taps - high_part
    four = jnp.concatenate([high_part, low_part, high_part, low_part], axis=0)
    tall = four.T.reshape(slabs * dp_count, piece, LANES)
    lane = lax.broadcasted_iota(jnp.int32, (half, LANES), 1)
    slab_count = D // (dp_count * piece)
    for owner in range(dp_count):
        packed = []
        for slab in range(slabs):
            source = slab * dp_count + owner
            where = pl.multiple_of((step * slabs + slab) * piece, piece)
            piece_sc[owner, pl.ds(where, piece), :] = turned[source]
            packed.append(
                jnp.where(lane < LANES // 2, tall[source, :half], tall[source, half:])
            )
        where = pl.multiple_of(slab_count * piece + step * slabs * half, slabs * half)
        piece_sc[owner, pl.ds(where, slabs * half), :] = jnp.concatenate(packed, axis=0).astype(BF16)

    @pl.when(step == pl.num_programs(0) - 1)
    def _():
        grad_heads_ref[...] = grad_sc[...].T.astype(BF16).reshape(H, HS, frames)
        for away, ref in enumerate(piece_refs):
            ref[...] = piece_sc[lax.rem(mine + away, dp_count)]


def middle(info, returned, block_input, grad_output, before, after, out_proj, kernel, bias, dp_count):
    frames = block_input.shape[0]
    piece_rows = D // dp_count + D // dp_count // 2
    column = lambda count: pl.BlockSpec((count, CHUNK), lambda i: (0, i))
    return pl.pallas_call(
        middle_kernel,
        grid=(D // CHUNK,),
        in_specs=[
            SCALARS,
            here(),
            column(frames),
            column(frames),
            here(),
            here(),
            pl.BlockSpec((CHUNK, HD), lambda i: (i, 0)),
            column(KW),
            column(1),
        ],
        out_specs=[
            column(frames),
            column(frames),
            whole((H, HS, frames)),
        ]
        + [whole((piece_rows, frames))] * dp_count,
        out_shape=[
            jax.ShapeDtypeStruct((frames, D), BF16),
            jax.ShapeDtypeStruct((frames, D), BF16),
            jax.ShapeDtypeStruct((H, HS, frames), BF16),
        ]
        + [jax.ShapeDtypeStruct((piece_rows, frames), BF16)] * dp_count,
        scratch_shapes=[
            pltpu.VMEM((frames + 2 * WIDE, HD), BF16),
            pltpu.VMEM((frames, HD), F32),
            pltpu.VMEM((CHUNK // LANES, frames + 2 * WIDE, LANES), F32),
            pltpu.VMEM((CHUNK // LANES, frames + 2 * SIDE, LANES), F32),
            pltpu.VMEM((TAP_ROWS, 8, CHUNK), F32),
            pltpu.VMEM((dp_count, piece_rows, frames), BF16),
        ],
        compiler_params=params(),
        name="middle",
    )(
        info,
        near(returned),
        far(block_input),
        far(grad_output),
        near(before),
        near(after),
        far(out_proj),
        far(kernel),
        bias,
    )


def split_parts(lane, value):
    high_part = value.astype(BF16).astype(F32)
    low_part = pltpu.roll(value - high_part, TAP_ROWS, 1)
    return jnp.where(lane % (2 * TAP_ROWS) < TAP_ROWS, high_part, low_part)


def join_parts(value):
    return value + pltpu.roll(value, LANES - TAP_ROWS, 1)


def store_share(out_ref, share, taps):
    piece = share.shape[-2]
    for tile in range(HD // LANES):
        rows = slice(tile * piece, (tile + 1) * piece)
        out_ref[..., rows, :] = share[..., tile * LANES : (tile + 1) * LANES].astype(BF16)
    out_ref[..., HD // LANES * piece :, :] = taps.astype(BF16)


def product_kernel(*refs):
    out_ref = refs[-1]
    count = (len(refs) - 1) // 2
    pieces, heads = refs[:count], refs[count : 2 * count]
    slabs = out_ref.shape[0]
    frames = pieces[0].shape[1]
    height = pieces[0].shape[0] * 2 // 3
    piece = height // slabs
    total = jnp.zeros((height, HD), F32)
    taps = jnp.zeros((height // 2, frames), F32)
    for piece_ref, head_ref in zip(pieces, heads):
        total += lax.dot_general(
            piece_ref[:height, :],
            head_ref[:, :HS, :].reshape(HD, frames),
            (((1,), (1,)), ((), ())),
            preferred_element_type=F32,
        )
        taps += piece_ref[height:, :].astype(F32)
    lane = lax.broadcasted_iota(jnp.int32, taps.shape, 1)
    parts = split_parts(lane, join_parts(taps)).reshape(slabs, piece // 2, LANES)
    store_share(out_ref, total.reshape(slabs, piece, HD), parts)


def product(pieces, heads, returned, seq_count):
    height = pieces[0].shape[0] * 2 // 3
    piece = height // seq_count
    share_rows = piece * HD // LANES + piece // 2
    near_heads = [near(array) for array in [returned, *heads]]
    near_pieces = [pieces[0]] + [near(array) for array in pieces[1:]]
    return pl.pallas_call(
        product_kernel,
        in_specs=here(2 * len(pieces)),
        out_specs=here(),
        out_shape=jax.ShapeDtypeStruct((seq_count, share_rows, LANES), BF16),
        compiler_params=params(),
        name="product",
    )(*near_pieces, *near_heads)


def sum_kernel(in_ref, out_ref):
    total = jnp.sum(in_ref[...].astype(F32), axis=0)
    rows = total.shape[0] * 12 // 13
    out_ref[:rows, :] = total[:rows].astype(BF16)
    taps = total[rows:]
    lane = lax.broadcasted_iota(jnp.int32, taps.shape, 1)
    out_ref[rows:, :] = split_parts(lane, join_parts(taps)).astype(BF16)


def sum_shares(shares):
    return pl.pallas_call(
        sum_kernel,
        in_specs=[here()],
        out_specs=here(),
        out_shape=jax.ShapeDtypeStruct(shares.shape[1:], BF16),
        compiler_params=params(),
        name="sum_shares",
    )(near(shares))


def pair_kernel(info_ref, own_ref, other_ref, *outs):
    count = len(outs)
    layer = lax.div(info_ref[3], 2)
    for away, out_ref in enumerate(outs):
        target = lax.rem(layer + away, count)
        out_ref[0] = own_ref[target]
        out_ref[1] = other_ref[target]


def pair_heads(info, own, other):
    count, rows, frames = own.shape
    return pl.pallas_call(
        pair_kernel,
        in_specs=[SCALARS] + here(2),
        out_specs=here(count),
        out_shape=[jax.ShapeDtypeStruct((2, rows, frames), BF16)] * count,
        compiler_params=params(),
        name="pair_heads",
    )(info, own, near(other))


def finish_kernel(info_ref, in_ref, *rest):
    pairs, (proj_ref, tap_ref, bias_ref, query_ref, heads_sc) = rest[:-5], rest[-5:]
    owners, share_rows, _ = in_ref.shape
    rows = share_rows * 12 // 13
    piece = rows * LANES // HD
    columns = []
    for owner in range(owners):
        for tile in range(HD // LANES):
            part = in_ref[owner, tile * piece : (tile + 1) * piece, :].astype(F32)
            proj_ref[owner * piece : (owner + 1) * piece, tile * LANES : (tile + 1) * LANES] = part
        taps = join_parts(in_ref[owner, rows:, :].astype(F32))
        columns += [taps, pltpu.roll(taps, LANES // 2, 1)]
    turned = jnp.concatenate(columns, axis=0).T
    tap_ref[...] = turned[:KW]
    bias_ref[...] = turned[KW : KW + 1]
    count = len(pairs)
    layer, side = lax.div(info_ref[3], 2), lax.rem(info_ref[3], 2)
    for away, pair_ref in enumerate(pairs):
        source = 2 * lax.rem(layer - away + count, count)
        heads_sc[source + side] = pair_ref[0]
        heads_sc[source + 1 - side] = pair_ref[1]
    query_ref[...] = heads_sc[...].reshape(HD, heads_sc.shape[2]).T


def finish(info, gathered, pairs):
    owners, share_rows, _ = gathered.shape
    width = owners * share_rows * 12 // 13 * LANES // HD
    frames = pairs[0].shape[2]
    return pl.pallas_call(
        finish_kernel,
        in_specs=[SCALARS] + here(1 + len(pairs)),
        out_specs=here(4),
        out_shape=[
            jax.ShapeDtypeStruct((width, HD), F32),
            jax.ShapeDtypeStruct((KW, width), F32),
            jax.ShapeDtypeStruct((1, width), F32),
            jax.ShapeDtypeStruct((frames, HD), BF16),
        ],
        scratch_shapes=[pltpu.VMEM((H, HS, frames), BF16)],
        compiler_params=params(),
        name="finish",
    )(info, near(gathered), pairs[0], *[near(pair) for pair in pairs[1:]])


def ring(count, away):
    return [(i, (i + away) % count) for i in range(count)]


def send_round(blocks, axis, stride=1):
    count = len(blocks) * stride
    return [blocks[0]] + [
        lax.ppermute(blocks[away], axis, ring(count, away * stride))
        for away in range(1, len(blocks))
    ]


def exchange(blocks, axis):
    return lax.all_to_all(blocks, axis, split_axis=0, concat_axis=0, tiled=True)


def fast_device(
    block_input, query_proj, key_proj, value_proj, lengths, out_proj, kernel, conv_bias, grad_output
):
    frames = block_input.shape[1]
    seq_count = lax.axis_size("seq")
    dp_count = lax.axis_size("dp")
    place = lax.axis_index("seq")
    info = jnp.stack([place * frames, lengths[0], lax.axis_index("dp"), place]).astype(jnp.int32)
    bias_row = conv_bias[None]

    received = exchange(pack_heads(query_proj[0], key_proj[0], value_proj[0]), "seq")

    last = jnp.concatenate([block_input[0, frames - WIDE :], grad_output[0, frames - SIDE :]])
    leading = jnp.concatenate([block_input[0, :WIDE], grad_output[0, :SIDE]])
    up = [(i, i + 1) for i in range(seq_count - 1)]
    down = [(j, i) for i, j in up]
    before = lax.ppermute(last, "seq", up)
    after = lax.ppermute(leading, "seq", down)
    received, before, after, info, bias_row = lax.optimization_barrier(
        (received, before, after, info, bias_row)
    )

    sent, lse = forward_heads(info, received)
    returned = exchange(sent, "seq")
    mine = returned[:, :HS]
    heads = send_round([mine] * dp_count, "dp")[1:]
    block_output, grad_input, grad_heads, *pieces = middle(
        info,
        returned,
        block_input[0],
        grad_output[0],
        before,
        after,
        out_proj,
        kernel,
        bias_row,
        dp_count,
    )
    grad_heads, heads, pieces = lax.optimization_barrier((grad_heads, heads, pieces))

    grads = exchange(grad_heads, "seq")
    moved = send_round(pieces, "dp")
    grads, moved = lax.optimization_barrier((grads, moved))
    shares = product(moved, heads, returned, seq_count)
    shares, grads = lax.optimization_barrier((shares, grads))
    shares = exchange(shares, "seq")
    keep, give = backward_heads(info, received, grads, sent, lse)
    other = lax.ppermute(give, "seq", [(i, i ^ 1) for i in range(seq_count)])
    pairs = send_round(pair_heads(info, keep, other), "seq", 2)
    gathered = lax.all_gather(sum_shares(shares), "dp")
    grad_proj, grad_kernel, grad_bias, grad_query = finish(info, gathered, pairs)
    return (block_output[None], grad_input[None], grad_query[None], grad_proj, grad_kernel, grad_bias[0])


def solution(mesh):
    device_fn = fast_device if fits_fast(mesh.shape) else general_device
    placed = (
        P("dp", "seq", None),
        P("dp", "seq", None),
        P("dp", "seq", None),
        P("dp", "seq", None),
        P("dp"),
        P(),
        P(),
        P(),
        P("dp", "seq", None),
    )
    return jax.shard_map(
        device_fn,
        mesh=mesh,
        in_specs=placed,
        out_specs=(
            P("dp", "seq", None),
            P("dp", "seq", None),
            P("dp", "seq", None),
            P("seq", None),
            P(None, "seq"),
            P("seq"),
        ),
        check_vma=False,
    )
```

```python
import functools
import math

import jax
import jax.numpy as jnp
from jax import lax
from jax.experimental import pallas as pl
from jax.experimental.pallas import tpu as pltpu
from jax.sharding import PartitionSpec as P

D = 1536
H = 8
HS = 96
KW = 31
HD = 768


def with_halo(x, sides, width):
    for axis, dim in sides:
        size, length = (lax.axis_size(axis), x.shape[dim])
        up = [(i, (i + 1) % size) for i in range(size - 1)]
        down = [(j, i) for i, j in up]
        last = lax.slice_in_dim(x, length - width, length, axis=dim)
        leading = lax.slice_in_dim(x, 0, width, axis=dim)
        before = lax.ppermute(last, axis, up)
        after = lax.ppermute(leading, axis, down)
        x = jnp.concatenate([before, x, after], axis=dim)
    return x


def forward_rows(query_one, key_one, value_one, key_valid, score_scale):
    row_total = query_one.shape[0]
    block_rows = math.gcd(row_total, 512)
    query_blocks = query_one.reshape(row_total // block_rows, block_rows, query_one.shape[1])

    def forward_one_block(query_block):
        scores = (
            lax.dot_general(
                query_block, key_one, (((1,), (1,)), ((), ())), preferred_element_type=jnp.float32
            )
            * score_scale
        )
        scores = jnp.where(key_valid[None, :], scores, -jnp.inf)
        row_top = jnp.max(scores, axis=-1, keepdims=True)
        log_total = row_top + jnp.log(jnp.sum(jnp.exp(scores - row_top), axis=-1, keepdims=True))
        weights = jnp.exp(scores - log_total).astype(jnp.bfloat16)
        return (jnp.dot(weights, value_one, preferred_element_type=jnp.float32), log_total[:, 0])

    outputs, log_totals = lax.map(forward_one_block, query_blocks)
    return (outputs.reshape(row_total, query_one.shape[1]), log_totals.reshape(row_total))


def backward_rows(
    query_one, key_one, value_one, grad_one, lse_one, delta_one, key_valid, score_scale
):
    row_total = query_one.shape[0]
    block_rows = math.gcd(row_total, 512)
    block_count = row_total // block_rows
    width = query_one.shape[1]

    def backward_one_block(items):
        query_block, grad_block, lse_block, delta_block = items
        scores = (
            lax.dot_general(
                query_block, key_one, (((1,), (1,)), ((), ())), preferred_element_type=jnp.float32
            )
            * score_scale
        )
        scores = jnp.where(key_valid[None, :], scores, -jnp.inf)
        probs = jnp.exp(scores - lse_block[:, None])
        grad_prob = lax.dot_general(
            grad_block, value_one, (((1,), (1,)), ((), ())), preferred_element_type=jnp.float32
        )
        grad_score = (probs * (grad_prob - delta_block[:, None])).astype(jnp.bfloat16)
        return jnp.dot(grad_score, key_one, preferred_element_type=jnp.float32) * score_scale

    results = lax.map(
        backward_one_block,
        (
            query_one.reshape(block_count, block_rows, width),
            grad_one.reshape(block_count, block_rows, width),
            lse_one.reshape(block_count, block_rows),
            delta_one.reshape(block_count, block_rows),
        ),
    )
    return results.reshape(row_total, width)


def general_device(
    block_input, query_proj, key_proj, value_proj, lengths, out_proj, kernel, conv_bias, grad_output
):
    frames_dev = block_input.shape[1]
    seq_count = lax.axis_size("seq")
    total_frames = frames_dev * seq_count
    first_frame = lax.axis_index("seq") * frames_dev
    utt_length = lengths[0]
    local_valid = first_frame + jnp.arange(frames_dev) < utt_length
    all_valid = jnp.arange(total_frames) < utt_length
    score_scale = 1.0 / math.sqrt(HS)
    halo_width = KW // 2
    group_size = seq_count // H
    sub_rows = frames_dev // group_size
    query_local = query_proj[0]

    def to_serving(matrix):
        return matrix.reshape(frames_dev, H, HS).transpose(1, 0, 2).reshape(seq_count, sub_rows, HS)

    def from_serving(returned):
        return returned.reshape(H, frames_dev, HS).transpose(1, 0, 2).reshape(frames_dev, HD)

    query_mine = lax.all_to_all(
        to_serving(query_local), "seq", split_axis=0, concat_axis=1, tiled=True
    )[0]
    key_send = jnp.repeat(
        key_proj[0].reshape(frames_dev, H, HS).transpose(1, 0, 2), group_size, axis=0
    )
    value_send = jnp.repeat(
        value_proj[0].reshape(frames_dev, H, HS).transpose(1, 0, 2), group_size, axis=0
    )
    key_mine, value_mine = (
        lax.all_to_all(key_send, "seq", split_axis=0, concat_axis=1, tiled=True),
        lax.all_to_all(value_send, "seq", split_axis=0, concat_axis=1, tiled=True),
    )
    key_mine = key_mine[0]
    value_mine = value_mine[0]
    head_out, head_lse = forward_rows(query_mine, key_mine, value_mine, all_valid, score_scale)
    head_attended = head_out.astype(jnp.bfloat16)
    attended = from_serving(
        lax.all_to_all(head_attended[None], "seq", split_axis=1, concat_axis=0, tiled=True)
    )
    projected = lax.dot_general(
        attended, out_proj, (((1,), (1,)), ((), ())), preferred_element_type=jnp.float32
    )
    mixed_rows = (block_input[0].astype(jnp.float32) + projected).astype(jnp.bfloat16)
    masked = jnp.where(local_valid[:, None], mixed_rows, jnp.zeros_like(mixed_rows))
    padded = with_halo(masked, (("seq", 0),), halo_width).astype(jnp.float32)
    conv_rows = jnp.broadcast_to(conv_bias, (frames_dev, D))
    for tap in range(KW):
        conv_rows = conv_rows + kernel[tap] * padded[tap : tap + frames_dev]
    gate_rows = jax.nn.sigmoid(conv_rows)
    block_output = jnp.where(
        local_valid[:, None], mixed_rows.astype(jnp.float32) + conv_rows * gate_rows, 0.0
    ).astype(jnp.bfloat16)
    grad_rows = jnp.where(local_valid[:, None], grad_output[0].astype(jnp.float32), 0.0)
    grad_conv = grad_rows * gate_rows * (1.0 + conv_rows * (1.0 - gate_rows))
    kernel_local = jnp.stack(
        [jnp.sum(grad_conv * padded[tap : tap + frames_dev], axis=0) for tap in range(KW)]
    )
    bias_local = jnp.sum(grad_conv, axis=0)
    grad_padded = with_halo(grad_conv, (("seq", 0),), halo_width)
    grad_masked = jnp.zeros((frames_dev, D), jnp.float32)
    for tap in range(KW):
        begin = 2 * halo_width - tap
        grad_masked = grad_masked + kernel[tap] * grad_padded[begin : begin + frames_dev]
    grad_input = (grad_rows + jnp.where(local_valid[:, None], grad_masked, 0.0)).astype(
        jnp.bfloat16
    )
    grad_attn = jnp.dot(grad_input, out_proj, preferred_element_type=jnp.float32).astype(
        jnp.bfloat16
    )
    grad_mine = lax.all_to_all(
        to_serving(grad_attn), "seq", split_axis=0, concat_axis=1, tiled=True
    )[0]
    delta_mine = jnp.sum(grad_mine.astype(jnp.float32) * head_attended.astype(jnp.float32), axis=-1)
    grad_q_mine = backward_rows(
        query_mine, key_mine, value_mine, grad_mine, head_lse, delta_mine, all_valid, score_scale
    ).astype(jnp.bfloat16)
    grad_query = from_serving(
        lax.all_to_all(grad_q_mine[None], "seq", split_axis=1, concat_axis=0, tiled=True)
    )
    term_block = lax.dot_general(
        grad_input, attended, (((0,), (0,)), ((), ())), preferred_element_type=jnp.float32
    )
    partial_rows = lax.psum_scatter(term_block, "seq", scatter_dimension=0, tiled=True)
    summed = lax.psum(partial_rows.astype(jnp.bfloat16), "dp").astype(jnp.float32)
    kernel_total, bias_total = lax.psum((kernel_local, bias_local), ("seq", "dp"))
    shard_width = D // seq_count
    offset = lax.axis_index("seq") * shard_width
    grad_kernel = lax.dynamic_slice_in_dim(kernel_total, offset, shard_width, 1)
    grad_bias = lax.dynamic_slice_in_dim(bias_total, offset, shard_width, 0)
    return (block_output[None], grad_input[None], grad_query[None], summed, grad_kernel, grad_bias)


BF16 = jnp.bfloat16
F32 = jnp.float32
TAP_ROWS = 32
WIDE = 32
SIDE = 16
CHUNK = 768
LANES = 128
MASKED_SCORE = -1e30
QUERIES, KEYS, VALUES = (slice(place * HS, (place + 1) * HS) for place in range(3))
VMEM_LIMIT = 40 * 1024 * 1024
SCORE_SCALE = 1.0 / math.sqrt(HS)
LOG2_SCALE = SCORE_SCALE * math.log2(math.e)


def fits_fast(sizes):
    seq_count, dp_count = sizes["seq"], sizes["dp"]
    piece = D // (seq_count * dp_count)
    return seq_count == H and dp_count * seq_count * piece == D and piece == 48


def params():
    return pltpu.CompilerParams(vmem_limit_bytes=VMEM_LIMIT)


def whole(shape):
    return pl.BlockSpec(shape, lambda *_: (0,) * len(shape))


def near(array):
    return pltpu.with_memory_space_constraint(array, pltpu.VMEM)


def far(array):
    return pltpu.with_memory_space_constraint(array, pltpu.HBM)


def here(count=None):
    spec = pl.BlockSpec(memory_space=pltpu.VMEM)
    return spec if count is None else [spec] * count


SCALARS = pl.BlockSpec(memory_space=pltpu.SMEM)


def pack_kernel(q_ref, k_ref, v_ref, out_ref):
    for place, ref in enumerate((q_ref, k_ref, v_ref)):
        frames = ref.shape[0]
        out_ref[:, place * HS : (place + 1) * HS, :] = ref[...].T.reshape(H, HS, frames)


def pack_heads(q, k, v):
    frames = q.shape[0]
    return pl.pallas_call(
        pack_kernel,
        out_shape=jax.ShapeDtypeStruct((H, 3 * HS, frames), BF16),
        compiler_params=params(),
        name="pack_heads",
    )(far(q), far(k), far(v))


def key_rows(x_ref, length, keys_sc):
    blocks, _, frames = x_ref.shape
    for block in range(blocks):
        row = lax.broadcasted_iota(jnp.int32, (LANES - HS, frames), 0)
        key = lax.broadcasted_iota(jnp.int32, (LANES - HS, frames), 1) + block * frames
        extra = jnp.where((row == 0) & (key >= length), MASKED_SCORE, 0.0)
        tall = jnp.concatenate([x_ref[block, KEYS].astype(F32), extra], axis=0)
        keys_sc[block * frames : (block + 1) * frames, :] = tall.T.astype(BF16)


def pair_of(ref, first, rows):
    return jnp.concatenate([ref[first, rows], ref[first + 1, rows]], axis=1)


def query_columns(x_ref, first):
    query = pair_of(x_ref, first, QUERIES)
    row = lax.broadcasted_iota(jnp.int32, (LANES - HS, query.shape[1]), 0)
    return jnp.concatenate([query, jnp.where(row == 0, 1.0, 0.0).astype(BF16)], axis=0)


def side_by_side(x_ref, rows, wide_sc):
    blocks, _, frames = x_ref.shape
    for block in range(blocks):
        wide_sc[:, block * frames : (block + 1) * frames] = x_ref[block, rows]


def forward_kernel(
    info_ref, x_ref, out_ref, lse_ref, keys_sc, values_sc, scores_sc, weights_sc
):
    blocks, _, frames = x_ref.shape
    key_rows(x_ref, info_ref[1], keys_sc)
    side_by_side(x_ref, VALUES, values_sc)
    for first in range(0, blocks, 2):
        turn = first // 2 % 2
        query = query_columns(x_ref, first)
        wide = query.shape[1]
        chunks = [slice(row, row + frames) for row in range(0, blocks * frames, frames)]
        peak = None
        for chunk in chunks:
            part = jnp.dot(keys_sc[chunk, :], query, preferred_element_type=F32)
            scores_sc[turn, chunk, :] = part
            part = part.reshape(frames // 8, 8, wide).max(0)
            peak = part if peak is None else jnp.maximum(peak, part)
        top = jnp.max(peak, axis=0, keepdims=True) * LOG2_SCALE
        total = jnp.zeros((8, wide), F32)
        for chunk in chunks:
            raised = jnp.exp2(scores_sc[turn, chunk, :] * LOG2_SCALE - top)
            scores_sc[turn, chunk, :] = raised
            total += raised.reshape(frames // 8, 8, wide).sum(0)
        total = jnp.sum(total, axis=0, keepdims=True)
        shrink = 1.0 / total
        lse_ref[:, first * frames : (first + 2) * frames] = top + jnp.log2(total)
        for chunk in chunks:
            weights_sc[turn, chunk, :] = (scores_sc[turn, chunk, :] * shrink).astype(BF16)
        mixed = jnp.dot(values_sc[...], weights_sc[turn], preferred_element_type=F32).astype(BF16)
        out_ref[first, :HS, :] = mixed[:, :frames]
        out_ref[first + 1, :HS, :] = mixed[:, frames:]

    lane = lax.broadcasted_iota(jnp.int32, (HS, frames), 1)
    nothing = jnp.zeros((HS, frames), F32)
    for block in range(blocks):
        left = nothing
        right = nothing
        if block > 0:
            left = pltpu.roll(out_ref[block - 1, :HS, :].astype(F32), WIDE, 1)
        if block < blocks - 1:
            right = pltpu.roll(out_ref[block + 1, :HS, :].astype(F32), WIDE, 1)
        both = jnp.where(lane < WIDE, left, right)
        lower = pltpu.roll(both[HS // 2 :], 2 * WIDE, 1)
        packed = jnp.where(lane[: HS // 2] < 2 * WIDE, both[: HS // 2], lower)
        out_ref[block, HS:, :] = packed.astype(BF16)


def forward_heads(info, received):
    blocks, _, frames = received.shape
    total = blocks * frames
    return pl.pallas_call(
        forward_kernel,
        in_specs=[SCALARS, here()],
        out_specs=here(2),
        out_shape=[
            jax.ShapeDtypeStruct((blocks, HS + HS // 2, frames), BF16),
            jax.ShapeDtypeStruct((1, total), F32),
        ],
        scratch_shapes=[
            pltpu.VMEM((total, LANES), BF16),
            pltpu.VMEM((HS, total), BF16),
            pltpu.VMEM((2, total, 2 * frames), F32),
            pltpu.VMEM((2, total, 2 * frames), BF16),
        ],
        compiler_params=params(),
        name="forward_heads",
    )(info, near(received))


def backward_kernel(info_ref, x_ref, grad_ref, head_ref, lse_ref, *rest):
    keep_ref, give_ref, keys_sc, values_sc, wide_sc, result_sc = rest
    blocks, _, frames = x_ref.shape
    key_rows(x_ref, info_ref[1], keys_sc)
    side_by_side(x_ref, KEYS, wide_sc)
    for block in range(blocks):
        rows = x_ref[block, VALUES].astype(F32).T.astype(BF16)
        values_sc[block * frames : (block + 1) * frames, :] = rows

    for first in range(0, blocks, 2):
        scores = jnp.dot(keys_sc[...], query_columns(x_ref, first), preferred_element_type=F32)
        probs = jnp.exp2(scores * LOG2_SCALE - lse_ref[:, first * frames : (first + 2) * frames])
        grad = pair_of(grad_ref, first, slice(0, HS))
        head = pair_of(head_ref, first, slice(0, HS))
        delta = jnp.sum(grad.astype(F32) * head.astype(F32), axis=0, keepdims=True)
        grad_prob = jnp.dot(values_sc[...], grad, preferred_element_type=F32)
        grad_score = (probs * (grad_prob - delta)).astype(BF16)
        result = jnp.dot(wide_sc[...], grad_score, preferred_element_type=F32) * SCORE_SCALE
        result_sc[first] = result[:, :frames].astype(BF16)
        result_sc[first + 1] = result[:, frames:].astype(BF16)
    side = lax.rem(info_ref[3], 2)
    for layer in range(blocks // 2):
        keep_ref[layer] = result_sc[2 * layer + side]
        give_ref[layer] = result_sc[2 * layer + 1 - side]


def backward_heads(info, received, grads, heads, lse):
    blocks, _, frames = received.shape
    total = blocks * frames
    return pl.pallas_call(
        backward_kernel,
        in_specs=[SCALARS] + here(4),
        out_specs=here(2),
        out_shape=[jax.ShapeDtypeStruct((blocks // 2, HS, frames), BF16)] * 2,
        scratch_shapes=[
            pltpu.VMEM((total, LANES), BF16),
            pltpu.VMEM((total, HS), BF16),
            pltpu.VMEM((HS, total), BF16),
            pltpu.VMEM((blocks, HS, frames), BF16),
        ],
        compiler_params=params(),
        name="backward_heads",
    )(info, near(received), near(grads), heads, lse)


def shifted_sum(ref, tile, rows, weight_of, start):
    total = start
    for low in range(8):
        base = ref[tile, low : low + rows + 24, :]
        for high in range(4):
            offset = 8 * high + low
            if 1 <= offset < TAP_ROWS:
                total = total + weight_of(offset) * base[8 * high : 8 * high + rows]
    return total


def middle_kernel(
    info_ref,
    att_ref,
    input_ref,
    cot_ref,
    before_ref,
    after_ref,
    proj_ref,
    tap_ref,
    bias_ref,
    block_out_ref,
    grad_in_ref,
    grad_heads_ref,
    *rest,
):
    piece_refs = rest[:-6]
    att_sc, grad_sc, masked_sc, gate_sc, taps_sc, piece_sc = rest[-6:]
    dp_count = len(piece_refs)
    step = pl.program_id(0)
    frames = input_ref.shape[0]
    tiles = CHUNK // LANES
    rows = frames + 2 * WIDE
    span = frames + 2 * SIDE
    first, length, mine = info_ref[0], info_ref[1], info_ref[2]

    @pl.when(step == 0)
    def _():
        main = att_ref[:, :HS, :].reshape(HD, frames)
        att_sc[WIDE : WIDE + frames, :] = main.T
        edge = att_ref[:, HS:, :].astype(F32).reshape(H * (HS // 2), frames)
        lower = pltpu.roll(edge, frames - 2 * WIDE, 1)
        half = (H, HS // 2, frames)
        tall = jnp.concatenate([edge.reshape(half), lower.reshape(half)], axis=1)
        turned = tall.reshape(HD, frames).T.astype(BF16)
        att_sc[:WIDE, :] = turned[:WIDE]
        att_sc[WIDE + frames :, :] = turned[WIDE : 2 * WIDE]
        grad_sc[...] = jnp.zeros_like(grad_sc)

    frame = first - WIDE + lax.broadcasted_iota(jnp.int32, (rows, LANES), 0)
    valid = (frame >= 0) & (frame < length)
    inner = slice(WIDE - SIDE, WIDE + SIDE + frames)
    own = slice(SIDE, SIDE + frames)
    inside = valid[WIDE : WIDE + frames]
    for tile in range(tiles):
        lanes = slice(tile * LANES, (tile + 1) * LANES)
        place = pl.ds(pl.multiple_of(step * CHUNK + tile * LANES, LANES), LANES)
        wide_input = jnp.concatenate(
            [before_ref[:WIDE, place], input_ref[:, lanes], after_ref[:WIDE, place]], axis=0
        ).astype(F32)
        projected = lax.dot_general(
            att_sc[...], proj_ref[lanes, :], (((1,), (1,)), ((), ())), preferred_element_type=F32
        )
        mixed = (wide_input + projected).astype(BF16).astype(F32)
        masked_sc[tile] = jnp.where(valid, mixed, 0.0)
        cot = jnp.concatenate(
            [before_ref[WIDE:, place], cot_ref[:, lanes], after_ref[WIDE:, place]], axis=0
        ).astype(F32)
        cot = jnp.where(valid[inner], cot, 0.0)
        start = jnp.broadcast_to(bias_ref[:, lanes], (span, LANES))
        conv = shifted_sum(
            masked_sc, tile, span, lambda offset: tap_ref[offset - 1 : offset, lanes], start
        )
        gate = lax.logistic(conv)
        center = masked_sc[tile, WIDE : WIDE + frames, :]
        block_out_ref[:, lanes] = jnp.where(inside, center + conv[own] * gate[own], 0.0).astype(BF16)
        gated = cot * gate * (1.0 + conv * (1.0 - gate))
        gate_sc[tile] = gated
        owned = gated[own]
        for low in range(8):
            base = masked_sc[tile, SIDE + low : SIDE + low + frames + 24, :]
            for high in range(4):
                offset = 8 * high + low
                if 1 <= offset < TAP_ROWS:
                    product = owned * base[8 * high : 8 * high + frames]
                    taps_sc[offset - 1, :, lanes] = product.reshape(frames // 8, 8, LANES).sum(0)
        taps_sc[TAP_ROWS - 1, :, lanes] = owned.reshape(frames // 8, 8, LANES).sum(0)
        back = shifted_sum(
            gate_sc,
            tile,
            frames,
            lambda offset: tap_ref[KW - offset : KW - offset + 1, lanes],
            jnp.zeros((frames, LANES), F32),
        )
        grad_in_ref[:, lanes] = (cot[own] + jnp.where(inside, back, 0.0)).astype(BF16)

    grad_in = grad_in_ref[...]
    grad_sc[...] += jnp.dot(grad_in, proj_ref[...], preferred_element_type=F32)

    piece = 48
    half = piece // 2
    slabs = CHUNK // (dp_count * piece)
    turned = grad_in.T.reshape(slabs * dp_count, piece, frames)
    taps = jnp.sum(taps_sc[...], axis=1)
    high_part = taps.astype(BF16).astype(F32)
    low_part = taps - high_part
    four = jnp.concatenate([high_part, low_part, high_part, low_part], axis=0)
    tall = four.T.reshape(slabs * dp_count, piece, LANES)
    lane = lax.broadcasted_iota(jnp.int32, (half, LANES), 1)
    slab_count = D // (dp_count * piece)
    for owner in range(dp_count):
        packed = []
        for slab in range(slabs):
            source = slab * dp_count + owner
            where = pl.multiple_of((step * slabs + slab) * piece, piece)
            piece_sc[owner, pl.ds(where, piece), :] = turned[source]
            packed.append(
                jnp.where(lane < LANES // 2, tall[source, :half], tall[source, half:])
            )
        where = pl.multiple_of(slab_count * piece + step * slabs * half, slabs * half)
        piece_sc[owner, pl.ds(where, slabs * half), :] = jnp.concatenate(packed, axis=0).astype(BF16)

    @pl.when(step == pl.num_programs(0) - 1)
    def _():
        grad_heads_ref[...] = grad_sc[...].T.astype(BF16).reshape(H, HS, frames)
        for away, ref in enumerate(piece_refs):
            ref[...] = piece_sc[lax.rem(mine + away, dp_count)]


def middle(info, returned, block_input, grad_output, before, after, out_proj, kernel, bias, dp_count):
    frames = block_input.shape[0]
    piece_rows = D // dp_count + D // dp_count // 2
    column = lambda count: pl.BlockSpec((count, CHUNK), lambda i: (0, i))
    return pl.pallas_call(
        middle_kernel,
        grid=(D // CHUNK,),
        in_specs=[
            SCALARS,
            here(),
            column(frames),
            column(frames),
            here(),
            here(),
            pl.BlockSpec((CHUNK, HD), lambda i: (i, 0)),
            column(KW),
            column(1),
        ],
        out_specs=[
            column(frames),
            column(frames),
            whole((H, HS, frames)),
        ]
        + [whole((piece_rows, frames))] * dp_count,
        out_shape=[
            jax.ShapeDtypeStruct((frames, D), BF16),
            jax.ShapeDtypeStruct((frames, D), BF16),
            jax.ShapeDtypeStruct((H, HS, frames), BF16),
        ]
        + [jax.ShapeDtypeStruct((piece_rows, frames), BF16)] * dp_count,
        scratch_shapes=[
            pltpu.VMEM((frames + 2 * WIDE, HD), BF16),
            pltpu.VMEM((frames, HD), F32),
            pltpu.VMEM((CHUNK // LANES, frames + 2 * WIDE, LANES), F32),
            pltpu.VMEM((CHUNK // LANES, frames + 2 * SIDE, LANES), F32),
            pltpu.VMEM((TAP_ROWS, 8, CHUNK), F32),
            pltpu.VMEM((dp_count, piece_rows, frames), BF16),
        ],
        compiler_params=params(),
        name="middle",
    )(
        info,
        near(returned),
        far(block_input),
        far(grad_output),
        near(before),
        near(after),
        far(out_proj),
        far(kernel),
        bias,
    )


def split_parts(lane, value):
    high_part = value.astype(BF16).astype(F32)
    low_part = pltpu.roll(value - high_part, TAP_ROWS, 1)
    return jnp.where(lane % (2 * TAP_ROWS) < TAP_ROWS, high_part, low_part)


def join_parts(value):
    return value + pltpu.roll(value, LANES - TAP_ROWS, 1)


def store_share(out_ref, share, taps):
    piece = share.shape[-2]
    for tile in range(HD // LANES):
        rows = slice(tile * piece, (tile + 1) * piece)
        out_ref[..., rows, :] = share[..., tile * LANES : (tile + 1) * LANES].astype(BF16)
    out_ref[..., HD // LANES * piece :, :] = taps.astype(BF16)


def product_kernel(*refs):
    out_ref = refs[-1]
    count = (len(refs) - 1) // 2
    pieces, heads = refs[:count], refs[count : 2 * count]
    slabs = out_ref.shape[0]
    frames = pieces[0].shape[1]
    height = pieces[0].shape[0] * 2 // 3
    piece = height // slabs
    total = jnp.zeros((height, HD), F32)
    taps = jnp.zeros((height // 2, frames), F32)
    for piece_ref, head_ref in zip(pieces, heads):
        total += lax.dot_general(
            piece_ref[:height, :],
            head_ref[:, :HS, :].reshape(HD, frames),
            (((1,), (1,)), ((), ())),
            preferred_element_type=F32,
        )
        taps += piece_ref[height:, :].astype(F32)
    lane = lax.broadcasted_iota(jnp.int32, taps.shape, 1)
    parts = split_parts(lane, join_parts(taps)).reshape(slabs, piece // 2, LANES)
    store_share(out_ref, total.reshape(slabs, piece, HD), parts)


def product(pieces, heads, returned, seq_count):
    height = pieces[0].shape[0] * 2 // 3
    piece = height // seq_count
    share_rows = piece * HD // LANES + piece // 2
    near_heads = [near(array) for array in [returned, *heads]]
    near_pieces = [pieces[0]] + [near(array) for array in pieces[1:]]
    return pl.pallas_call(
        product_kernel,
        in_specs=here(2 * len(pieces)),
        out_specs=here(),
        out_shape=jax.ShapeDtypeStruct((seq_count, share_rows, LANES), BF16),
        compiler_params=params(),
        name="product",
    )(*near_pieces, *near_heads)


def sum_kernel(in_ref, out_ref):
    total = jnp.sum(in_ref[...].astype(F32), axis=0)
    rows = total.shape[0] * 12 // 13
    out_ref[:rows, :] = total[:rows].astype(BF16)
    taps = total[rows:]
    lane = lax.broadcasted_iota(jnp.int32, taps.shape, 1)
    out_ref[rows:, :] = split_parts(lane, join_parts(taps)).astype(BF16)


def sum_shares(shares):
    return pl.pallas_call(
        sum_kernel,
        in_specs=[here()],
        out_specs=here(),
        out_shape=jax.ShapeDtypeStruct(shares.shape[1:], BF16),
        compiler_params=params(),
        name="sum_shares",
    )(near(shares))


def pair_kernel(info_ref, own_ref, other_ref, *outs):
    count = len(outs)
    layer = lax.div(info_ref[3], 2)
    for away, out_ref in enumerate(outs):
        target = lax.rem(layer + away, count)
        out_ref[0] = own_ref[target]
        out_ref[1] = other_ref[target]


def pair_heads(info, own, other):
    count, rows, frames = own.shape
    return pl.pallas_call(
        pair_kernel,
        in_specs=[SCALARS] + here(2),
        out_specs=here(count),
        out_shape=[jax.ShapeDtypeStruct((2, rows, frames), BF16)] * count,
        compiler_params=params(),
        name="pair_heads",
    )(info, own, near(other))


def finish_kernel(info_ref, in_ref, *rest):
    pairs, (proj_ref, tap_ref, bias_ref, query_ref, heads_sc) = rest[:-5], rest[-5:]
    owners, share_rows, _ = in_ref.shape
    rows = share_rows * 12 // 13
    piece = rows * LANES // HD
    columns = []
    for owner in range(owners):
        for tile in range(HD // LANES):
            part = in_ref[owner, tile * piece : (tile + 1) * piece, :].astype(F32)
            proj_ref[owner * piece : (owner + 1) * piece, tile * LANES : (tile + 1) * LANES] = part
        taps = join_parts(in_ref[owner, rows:, :].astype(F32))
        columns += [taps, pltpu.roll(taps, LANES // 2, 1)]
    turned = jnp.concatenate(columns, axis=0).T
    tap_ref[...] = turned[:KW]
    bias_ref[...] = turned[KW : KW + 1]
    count = len(pairs)
    layer, side = lax.div(info_ref[3], 2), lax.rem(info_ref[3], 2)
    for away, pair_ref in enumerate(pairs):
        source = 2 * lax.rem(layer - away + count, count)
        heads_sc[source + side] = pair_ref[0]
        heads_sc[source + 1 - side] = pair_ref[1]
    query_ref[...] = heads_sc[...].reshape(HD, heads_sc.shape[2]).T


def finish(info, gathered, pairs):
    owners, share_rows, _ = gathered.shape
    width = owners * share_rows * 12 // 13 * LANES // HD
    frames = pairs[0].shape[2]
    return pl.pallas_call(
        finish_kernel,
        in_specs=[SCALARS] + here(1 + len(pairs)),
        out_specs=here(4),
        out_shape=[
            jax.ShapeDtypeStruct((width, HD), F32),
            jax.ShapeDtypeStruct((KW, width), F32),
            jax.ShapeDtypeStruct((1, width), F32),
            jax.ShapeDtypeStruct((frames, HD), BF16),
        ],
        scratch_shapes=[pltpu.VMEM((H, HS, frames), BF16)],
        compiler_params=params(),
        name="finish",
    )(info, near(gathered), pairs[0], *[near(pair) for pair in pairs[1:]])


def ring(count, away):
    return [(i, (i + away) % count) for i in range(count)]


def send_round(blocks, axis, stride=1):
    count = len(blocks) * stride
    return [blocks[0]] + [
        lax.ppermute(blocks[away], axis, ring(count, away * stride))
        for away in range(1, len(blocks))
    ]


def exchange(blocks, axis):
    return lax.all_to_all(blocks, axis, split_axis=0, concat_axis=0, tiled=True)


def fast_device(
    block_input, query_proj, key_proj, value_proj, lengths, out_proj, kernel, conv_bias, grad_output
):
    frames = block_input.shape[1]
    seq_count = lax.axis_size("seq")
    dp_count = lax.axis_size("dp")
    place = lax.axis_index("seq")
    info = jnp.stack([place * frames, lengths[0], lax.axis_index("dp"), place]).astype(jnp.int32)
    bias_row = conv_bias[None]

    received = exchange(pack_heads(query_proj[0], key_proj[0], value_proj[0]), "seq")

    last = jnp.concatenate([block_input[0, frames - WIDE :], grad_output[0, frames - SIDE :]])
    leading = jnp.concatenate([block_input[0, :WIDE], grad_output[0, :SIDE]])
    up = [(i, i + 1) for i in range(seq_count - 1)]
    down = [(j, i) for i, j in up]
    before = lax.ppermute(last, "seq", up)
    after = lax.ppermute(leading, "seq", down)
    received, before, after, info, bias_row = lax.optimization_barrier(
        (received, before, after, info, bias_row)
    )

    sent, lse = forward_heads(info, received)
    returned = exchange(sent, "seq")
    mine = returned[:, :HS]
    heads = send_round([mine] * dp_count, "dp")[1:]
    block_output, grad_input, grad_heads, *pieces = middle(
        info,
        returned,
        block_input[0],
        grad_output[0],
        before,
        after,
        out_proj,
        kernel,
        bias_row,
        dp_count,
    )
    grad_heads, heads, pieces = lax.optimization_barrier((grad_heads, heads, pieces))

    grads = exchange(grad_heads, "seq")
    moved = send_round(pieces, "dp")
    grads, moved = lax.optimization_barrier((grads, moved))
    shares = product(moved, heads, returned, seq_count)
    shares, grads = lax.optimization_barrier((shares, grads))
    shares = exchange(shares, "seq")
    keep, give = backward_heads(info, received, grads, sent, lse)
    other = lax.ppermute(give, "seq", [(i, i ^ 1) for i in range(seq_count)])
    pairs = send_round(pair_heads(info, keep, other), "seq", 2)
    gathered = lax.all_gather(sum_shares(shares), "dp")
    grad_proj, grad_kernel, grad_bias, grad_query = finish(info, gathered, pairs)
    return (block_output[None], grad_input[None], grad_query[None], grad_proj, grad_kernel, grad_bias[0])


def solution(mesh):
    device_fn = fast_device if fits_fast(mesh.shape) else general_device
    placed = (
        P("dp", "seq", None),
        P("dp", "seq", None),
        P("dp", "seq", None),
        P("dp", "seq", None),
        P("dp"),
        P(),
        P(),
        P(),
        P("dp", "seq", None),
    )
    return jax.shard_map(
        device_fn,
        mesh=mesh,
        in_specs=placed,
        out_specs=(
            P("dp", "seq", None),
            P("dp", "seq", None),
            P("dp", "seq", None),
            P("seq", None),
            P(None, "seq"),
            P("seq"),
        ),
        check_vma=False,
    )
```

```python
import functools
import math

import jax
import jax.numpy as jnp
from jax import lax
from jax.experimental import pallas as pl
from jax.experimental.pallas import tpu as pltpu
from jax.sharding import PartitionSpec as P

D = 1536
H = 8
HS = 96
KW = 31
HD = 768


def with_halo(x, sides, width):
    for axis, dim in sides:
        size, length = (lax.axis_size(axis), x.shape[dim])
        up = [(i, (i + 1) % size) for i in range(size - 1)]
        down = [(j, i) for i, j in up]
        last = lax.slice_in_dim(x, length - width, length, axis=dim)
        leading = lax.slice_in_dim(x, 0, width, axis=dim)
        before = lax.ppermute(last, axis, up)
        after = lax.ppermute(leading, axis, down)
        x = jnp.concatenate([before, x, after], axis=dim)
    return x


def forward_rows(query_one, key_one, value_one, key_valid, score_scale):
    row_total = query_one.shape[0]
    block_rows = math.gcd(row_total, 512)
    query_blocks = query_one.reshape(row_total // block_rows, block_rows, query_one.shape[1])

    def forward_one_block(query_block):
        scores = (
            lax.dot_general(
                query_block, key_one, (((1,), (1,)), ((), ())), preferred_element_type=jnp.float32
            )
            * score_scale
        )
        scores = jnp.where(key_valid[None, :], scores, -jnp.inf)
        row_top = jnp.max(scores, axis=-1, keepdims=True)
        log_total = row_top + jnp.log(jnp.sum(jnp.exp(scores - row_top), axis=-1, keepdims=True))
        weights = jnp.exp(scores - log_total).astype(jnp.bfloat16)
        return (jnp.dot(weights, value_one, preferred_element_type=jnp.float32), log_total[:, 0])

    outputs, log_totals = lax.map(forward_one_block, query_blocks)
    return (outputs.reshape(row_total, query_one.shape[1]), log_totals.reshape(row_total))


def backward_rows(
    query_one, key_one, value_one, grad_one, lse_one, delta_one, key_valid, score_scale
):
    row_total = query_one.shape[0]
    block_rows = math.gcd(row_total, 512)
    block_count = row_total // block_rows
    width = query_one.shape[1]

    def backward_one_block(items):
        query_block, grad_block, lse_block, delta_block = items
        scores = (
            lax.dot_general(
                query_block, key_one, (((1,), (1,)), ((), ())), preferred_element_type=jnp.float32
            )
            * score_scale
        )
        scores = jnp.where(key_valid[None, :], scores, -jnp.inf)
        probs = jnp.exp(scores - lse_block[:, None])
        grad_prob = lax.dot_general(
            grad_block, value_one, (((1,), (1,)), ((), ())), preferred_element_type=jnp.float32
        )
        grad_score = (probs * (grad_prob - delta_block[:, None])).astype(jnp.bfloat16)
        return jnp.dot(grad_score, key_one, preferred_element_type=jnp.float32) * score_scale

    results = lax.map(
        backward_one_block,
        (
            query_one.reshape(block_count, block_rows, width),
            grad_one.reshape(block_count, block_rows, width),
            lse_one.reshape(block_count, block_rows),
            delta_one.reshape(block_count, block_rows),
        ),
    )
    return results.reshape(row_total, width)


def general_device(
    block_input, query_proj, key_proj, value_proj, lengths, out_proj, kernel, conv_bias, grad_output
):
    frames_dev = block_input.shape[1]
    seq_count = lax.axis_size("seq")
    total_frames = frames_dev * seq_count
    first_frame = lax.axis_index("seq") * frames_dev
    utt_length = lengths[0]
    local_valid = first_frame + jnp.arange(frames_dev) < utt_length
    all_valid = jnp.arange(total_frames) < utt_length
    score_scale = 1.0 / math.sqrt(HS)
    halo_width = KW // 2
    group_size = seq_count // H
    sub_rows = frames_dev // group_size
    query_local = query_proj[0]

    def to_serving(matrix):
        return matrix.reshape(frames_dev, H, HS).transpose(1, 0, 2).reshape(seq_count, sub_rows, HS)

    def from_serving(returned):
        return returned.reshape(H, frames_dev, HS).transpose(1, 0, 2).reshape(frames_dev, HD)

    query_mine = lax.all_to_all(
        to_serving(query_local), "seq", split_axis=0, concat_axis=1, tiled=True
    )[0]
    key_send = jnp.repeat(
        key_proj[0].reshape(frames_dev, H, HS).transpose(1, 0, 2), group_size, axis=0
    )
    value_send = jnp.repeat(
        value_proj[0].reshape(frames_dev, H, HS).transpose(1, 0, 2), group_size, axis=0
    )
    key_mine, value_mine = (
        lax.all_to_all(key_send, "seq", split_axis=0, concat_axis=1, tiled=True),
        lax.all_to_all(value_send, "seq", split_axis=0, concat_axis=1, tiled=True),
    )
    key_mine = key_mine[0]
    value_mine = value_mine[0]
    head_out, head_lse = forward_rows(query_mine, key_mine, value_mine, all_valid, score_scale)
    head_attended = head_out.astype(jnp.bfloat16)
    attended = from_serving(
        lax.all_to_all(head_attended[None], "seq", split_axis=1, concat_axis=0, tiled=True)
    )
    projected = lax.dot_general(
        attended, out_proj, (((1,), (1,)), ((), ())), preferred_element_type=jnp.float32
    )
    mixed_rows = (block_input[0].astype(jnp.float32) + projected).astype(jnp.bfloat16)
    masked = jnp.where(local_valid[:, None], mixed_rows, jnp.zeros_like(mixed_rows))
    padded = with_halo(masked, (("seq", 0),), halo_width).astype(jnp.float32)
    conv_rows = jnp.broadcast_to(conv_bias, (frames_dev, D))
    for tap in range(KW):
        conv_rows = conv_rows + kernel[tap] * padded[tap : tap + frames_dev]
    gate_rows = jax.nn.sigmoid(conv_rows)
    block_output = jnp.where(
        local_valid[:, None], mixed_rows.astype(jnp.float32) + conv_rows * gate_rows, 0.0
    ).astype(jnp.bfloat16)
    grad_rows = jnp.where(local_valid[:, None], grad_output[0].astype(jnp.float32), 0.0)
    grad_conv = grad_rows * gate_rows * (1.0 + conv_rows * (1.0 - gate_rows))
    kernel_local = jnp.stack(
        [jnp.sum(grad_conv * padded[tap : tap + frames_dev], axis=0) for tap in range(KW)]
    )
    bias_local = jnp.sum(grad_conv, axis=0)
    grad_padded = with_halo(grad_conv, (("seq", 0),), halo_width)
    grad_masked = jnp.zeros((frames_dev, D), jnp.float32)
    for tap in range(KW):
        begin = 2 * halo_width - tap
        grad_masked = grad_masked + kernel[tap] * grad_padded[begin : begin + frames_dev]
    grad_input = (grad_rows + jnp.where(local_valid[:, None], grad_masked, 0.0)).astype(
        jnp.bfloat16
    )
    grad_attn = jnp.dot(grad_input, out_proj, preferred_element_type=jnp.float32).astype(
        jnp.bfloat16
    )
    grad_mine = lax.all_to_all(
        to_serving(grad_attn), "seq", split_axis=0, concat_axis=1, tiled=True
    )[0]
    delta_mine = jnp.sum(grad_mine.astype(jnp.float32) * head_attended.astype(jnp.float32), axis=-1)
    grad_q_mine = backward_rows(
        query_mine, key_mine, value_mine, grad_mine, head_lse, delta_mine, all_valid, score_scale
    ).astype(jnp.bfloat16)
    grad_query = from_serving(
        lax.all_to_all(grad_q_mine[None], "seq", split_axis=1, concat_axis=0, tiled=True)
    )
    term_block = lax.dot_general(
        grad_input, attended, (((0,), (0,)), ((), ())), preferred_element_type=jnp.float32
    )
    partial_rows = lax.psum_scatter(term_block, "seq", scatter_dimension=0, tiled=True)
    summed = lax.psum(partial_rows.astype(jnp.bfloat16), "dp").astype(jnp.float32)
    kernel_total, bias_total = lax.psum((kernel_local, bias_local), ("seq", "dp"))
    shard_width = D // seq_count
    offset = lax.axis_index("seq") * shard_width
    grad_kernel = lax.dynamic_slice_in_dim(kernel_total, offset, shard_width, 1)
    grad_bias = lax.dynamic_slice_in_dim(bias_total, offset, shard_width, 0)
    return (block_output[None], grad_input[None], grad_query[None], summed, grad_kernel, grad_bias)


BF16 = jnp.bfloat16
F32 = jnp.float32
TAP_ROWS = 32
WIDE = 32
SIDE = 16
CHUNK = 768
LANES = 128
MASKED_SCORE = -1e30
QUERIES, KEYS, VALUES = (slice(place * HS, (place + 1) * HS) for place in range(3))
VMEM_LIMIT = 40 * 1024 * 1024
SCORE_SCALE = 1.0 / math.sqrt(HS)
LOG2_SCALE = SCORE_SCALE * math.log2(math.e)


def fits_fast(sizes):
    seq_count, dp_count = sizes["seq"], sizes["dp"]
    piece = D // (seq_count * dp_count)
    return seq_count == H and dp_count * seq_count * piece == D and piece == 48


def params():
    return pltpu.CompilerParams(vmem_limit_bytes=VMEM_LIMIT)


def whole(shape):
    return pl.BlockSpec(shape, lambda *_: (0,) * len(shape))


def near(array):
    return pltpu.with_memory_space_constraint(array, pltpu.VMEM)


def far(array):
    return pltpu.with_memory_space_constraint(array, pltpu.HBM)


def here(count=None):
    spec = pl.BlockSpec(memory_space=pltpu.VMEM)
    return spec if count is None else [spec] * count


SCALARS = pl.BlockSpec(memory_space=pltpu.SMEM)


def pack_kernel(q_ref, k_ref, v_ref, out_ref):
    heads, _, frames = out_ref.shape
    for place, ref in enumerate((q_ref, k_ref, v_ref)):
        out_ref[:, place * HS : (place + 1) * HS, :] = ref[...].T.reshape(heads, HS, frames)


def pack_heads(q, k, v):
    frames = q.shape[0]
    return pl.pallas_call(
        pack_kernel,
        grid=(2,),
        in_specs=[pl.BlockSpec((frames, HD // 2), lambda i: (0, i))] * 3,
        out_specs=pl.BlockSpec((H // 2, 3 * HS, frames), lambda i: (i, 0, 0)),
        out_shape=jax.ShapeDtypeStruct((H, 3 * HS, frames), BF16),
        compiler_params=params(),
        name="pack_heads",
    )(far(q), far(k), far(v))


def key_rows(x_ref, length, keys_sc):
    blocks, _, frames = x_ref.shape
    for block in range(blocks):
        row = lax.broadcasted_iota(jnp.int32, (LANES - HS, frames), 0)
        key = lax.broadcasted_iota(jnp.int32, (LANES - HS, frames), 1) + block * frames
        extra = jnp.where((row == 0) & (key >= length), MASKED_SCORE, 0.0)
        tall = jnp.concatenate([x_ref[block, KEYS].astype(F32), extra], axis=0)
        keys_sc[block * frames : (block + 1) * frames, :] = tall.T.astype(BF16)


def pair_of(ref, first, rows):
    return jnp.concatenate([ref[first, rows], ref[first + 1, rows]], axis=1)


def query_columns(x_ref, first):
    query = pair_of(x_ref, first, QUERIES)
    row = lax.broadcasted_iota(jnp.int32, (LANES - HS, query.shape[1]), 0)
    return jnp.concatenate([query, jnp.where(row == 0, 1.0, 0.0).astype(BF16)], axis=0)


def side_by_side(x_ref, rows, wide_sc):
    blocks, _, frames = x_ref.shape
    for block in range(blocks):
        wide_sc[:, block * frames : (block + 1) * frames] = x_ref[block, rows]


def forward_kernel(
    info_ref, x_ref, out_ref, lse_ref, keys_sc, values_sc, scores_sc, weights_sc
):
    blocks, _, frames = x_ref.shape
    key_rows(x_ref, info_ref[1], keys_sc)
    side_by_side(x_ref, VALUES, values_sc)
    for first in range(0, blocks, 2):
        turn = first // 2 % 2
        query = query_columns(x_ref, first)
        wide = query.shape[1]
        chunks = [slice(row, row + frames) for row in range(0, blocks * frames, frames)]
        peak = None
        for chunk in chunks:
            part = jnp.dot(keys_sc[chunk, :], query, preferred_element_type=F32)
            scores_sc[turn, chunk, :] = part
            part = part.reshape(frames // 8, 8, wide).max(0)
            peak = part if peak is None else jnp.maximum(peak, part)
        top = jnp.max(peak, axis=0, keepdims=True) * LOG2_SCALE
        total = jnp.zeros((8, wide), F32)
        for chunk in chunks:
            raised = jnp.exp2(scores_sc[turn, chunk, :] * LOG2_SCALE - top)
            scores_sc[turn, chunk, :] = raised
            total += raised.reshape(frames // 8, 8, wide).sum(0)
        total = jnp.sum(total, axis=0, keepdims=True)
        shrink = 1.0 / total
        lse_ref[:, first * frames : (first + 2) * frames] = top + jnp.log2(total)
        for chunk in chunks:
            weights_sc[turn, chunk, :] = (scores_sc[turn, chunk, :] * shrink).astype(BF16)
        mixed = jnp.dot(values_sc[...], weights_sc[turn], preferred_element_type=F32).astype(BF16)
        out_ref[first, :HS, :] = mixed[:, :frames]
        out_ref[first + 1, :HS, :] = mixed[:, frames:]

    lane = lax.broadcasted_iota(jnp.int32, (HS, frames), 1)
    nothing = jnp.zeros((HS, frames), F32)
    for block in range(blocks):
        left = nothing
        right = nothing
        if block > 0:
            left = pltpu.roll(out_ref[block - 1, :HS, :].astype(F32), WIDE, 1)
        if block < blocks - 1:
            right = pltpu.roll(out_ref[block + 1, :HS, :].astype(F32), WIDE, 1)
        both = jnp.where(lane < WIDE, left, right)
        lower = pltpu.roll(both[HS // 2 :], 2 * WIDE, 1)
        packed = jnp.where(lane[: HS // 2] < 2 * WIDE, both[: HS // 2], lower)
        out_ref[block, HS:, :] = packed.astype(BF16)


def forward_heads(info, received):
    blocks, _, frames = received.shape
    total = blocks * frames
    return pl.pallas_call(
        forward_kernel,
        in_specs=[SCALARS, here()],
        out_specs=here(2),
        out_shape=[
            jax.ShapeDtypeStruct((blocks, HS + HS // 2, frames), BF16),
            jax.ShapeDtypeStruct((1, total), F32),
        ],
        scratch_shapes=[
            pltpu.VMEM((total, LANES), BF16),
            pltpu.VMEM((HS, total), BF16),
            pltpu.VMEM((2, total, 2 * frames), F32),
            pltpu.VMEM((2, total, 2 * frames), BF16),
        ],
        compiler_params=params(),
        name="forward_heads",
    )(info, near(received))


def backward_kernel(info_ref, x_ref, grad_ref, head_ref, lse_ref, *rest):
    keep_ref, give_ref, keys_sc, values_sc, wide_sc, result_sc = rest
    blocks, _, frames = x_ref.shape
    key_rows(x_ref, info_ref[1], keys_sc)
    side_by_side(x_ref, KEYS, wide_sc)
    for block in range(blocks):
        rows = x_ref[block, VALUES].astype(F32).T.astype(BF16)
        values_sc[block * frames : (block + 1) * frames, :] = rows

    for first in range(0, blocks, 2):
        scores = jnp.dot(keys_sc[...], query_columns(x_ref, first), preferred_element_type=F32)
        probs = jnp.exp2(scores * LOG2_SCALE - lse_ref[:, first * frames : (first + 2) * frames])
        grad = pair_of(grad_ref, first, slice(0, HS))
        head = pair_of(head_ref, first, slice(0, HS))
        delta = jnp.sum(grad.astype(F32) * head.astype(F32), axis=0, keepdims=True)
        grad_prob = jnp.dot(values_sc[...], grad, preferred_element_type=F32)
        grad_score = (probs * (grad_prob - delta)).astype(BF16)
        result = jnp.dot(wide_sc[...], grad_score, preferred_element_type=F32) * SCORE_SCALE
        result_sc[first] = result[:, :frames].astype(BF16)
        result_sc[first + 1] = result[:, frames:].astype(BF16)
    side = lax.rem(info_ref[3], 2)
    for layer in range(blocks // 2):
        keep_ref[layer] = result_sc[2 * layer + side]
        give_ref[layer] = result_sc[2 * layer + 1 - side]


def backward_heads(info, received, grads, heads, lse):
    blocks, _, frames = received.shape
    total = blocks * frames
    return pl.pallas_call(
        backward_kernel,
        in_specs=[SCALARS] + here(4),
        out_specs=here(2),
        out_shape=[jax.ShapeDtypeStruct((blocks // 2, HS, frames), BF16)] * 2,
        scratch_shapes=[
            pltpu.VMEM((total, LANES), BF16),
            pltpu.VMEM((total, HS), BF16),
            pltpu.VMEM((HS, total), BF16),
            pltpu.VMEM((blocks, HS, frames), BF16),
        ],
        compiler_params=params(),
        name="backward_heads",
    )(info, near(received), near(grads), heads, lse)


def shifted_sum(ref, tile, rows, weight_of, start):
    total = start
    for low in range(8):
        base = ref[tile, low : low + rows + 24, :]
        for high in range(4):
            offset = 8 * high + low
            if 1 <= offset < TAP_ROWS:
                total = total + weight_of(offset) * base[8 * high : 8 * high + rows]
    return total


def middle_kernel(
    info_ref,
    att_ref,
    input_ref,
    cot_ref,
    before_ref,
    after_ref,
    proj_ref,
    tap_ref,
    bias_ref,
    block_out_ref,
    grad_in_ref,
    grad_heads_ref,
    *rest,
):
    piece_refs = rest[:-6]
    att_sc, grad_sc, masked_sc, gate_sc, taps_sc, piece_sc = rest[-6:]
    dp_count = len(piece_refs)
    step = pl.program_id(0)
    frames = input_ref.shape[0]
    tiles = CHUNK // LANES
    rows = frames + 2 * WIDE
    span = frames + 2 * SIDE
    first, length, mine = info_ref[0], info_ref[1], info_ref[2]

    @pl.when(step == 0)
    def _():
        main = att_ref[:, :HS, :].reshape(HD, frames)
        att_sc[WIDE : WIDE + frames, :] = main.T
        edge = att_ref[:, HS:, :].astype(F32).reshape(H * (HS // 2), frames)
        lower = pltpu.roll(edge, frames - 2 * WIDE, 1)
        half = (H, HS // 2, frames)
        tall = jnp.concatenate([edge.reshape(half), lower.reshape(half)], axis=1)
        turned = tall.reshape(HD, frames).T.astype(BF16)
        att_sc[:WIDE, :] = turned[:WIDE]
        att_sc[WIDE + frames :, :] = turned[WIDE : 2 * WIDE]
        grad_sc[...] = jnp.zeros_like(grad_sc)

    frame = first - WIDE + lax.broadcasted_iota(jnp.int32, (rows, LANES), 0)
    valid = (frame >= 0) & (frame < length)
    inner = slice(WIDE - SIDE, WIDE + SIDE + frames)
    own = slice(SIDE, SIDE + frames)
    inside = valid[WIDE : WIDE + frames]
    for tile in range(tiles):
        lanes = slice(tile * LANES, (tile + 1) * LANES)
        place = pl.ds(pl.multiple_of(step * CHUNK + tile * LANES, LANES), LANES)
        wide_input = jnp.concatenate(
            [before_ref[:WIDE, place], input_ref[:, lanes], after_ref[:WIDE, place]], axis=0
        ).astype(F32)
        projected = lax.dot_general(
            att_sc[...], proj_ref[lanes, :], (((1,), (1,)), ((), ())), preferred_element_type=F32
        )
        mixed = (wide_input + projected).astype(BF16).astype(F32)
        masked_sc[tile] = jnp.where(valid, mixed, 0.0)
        cot = jnp.concatenate(
            [before_ref[WIDE:, place], cot_ref[:, lanes], after_ref[WIDE:, place]], axis=0
        ).astype(F32)
        cot = jnp.where(valid[inner], cot, 0.0)
        start = jnp.broadcast_to(bias_ref[:, lanes], (span, LANES))
        conv = shifted_sum(
            masked_sc, tile, span, lambda offset: tap_ref[offset - 1 : offset, lanes], start
        )
        gate = lax.logistic(conv)
        center = masked_sc[tile, WIDE : WIDE + frames, :]
        block_out_ref[:, lanes] = jnp.where(inside, center + conv[own] * gate[own], 0.0).astype(BF16)
        gated = cot * gate * (1.0 + conv * (1.0 - gate))
        gate_sc[tile] = gated
        owned = gated[own]
        for low in range(8):
            base = masked_sc[tile, SIDE + low : SIDE + low + frames + 24, :]
            for high in range(4):
                offset = 8 * high + low
                if 1 <= offset < TAP_ROWS:
                    product = owned * base[8 * high : 8 * high + frames]
                    taps_sc[offset - 1, :, lanes] = product.reshape(frames // 8, 8, LANES).sum(0)
        taps_sc[TAP_ROWS - 1, :, lanes] = owned.reshape(frames // 8, 8, LANES).sum(0)
        back = shifted_sum(
            gate_sc,
            tile,
            frames,
            lambda offset: tap_ref[KW - offset : KW - offset + 1, lanes],
            jnp.zeros((frames, LANES), F32),
        )
        grad_in_ref[:, lanes] = (cot[own] + jnp.where(inside, back, 0.0)).astype(BF16)

    grad_in = grad_in_ref[...]
    grad_sc[...] += jnp.dot(grad_in, proj_ref[...], preferred_element_type=F32)

    piece = 48
    half = piece // 2
    slabs = CHUNK // (dp_count * piece)
    turned = grad_in.T.reshape(slabs * dp_count, piece, frames)
    taps = jnp.sum(taps_sc[...], axis=1)
    high_part = taps.astype(BF16).astype(F32)
    low_part = taps - high_part
    four = jnp.concatenate([high_part, low_part, high_part, low_part], axis=0)
    tall = four.T.reshape(slabs * dp_count, piece, LANES)
    lane = lax.broadcasted_iota(jnp.int32, (half, LANES), 1)
    slab_count = D // (dp_count * piece)
    for owner in range(dp_count):
        packed = []
        for slab in range(slabs):
            source = slab * dp_count + owner
            where = pl.multiple_of((step * slabs + slab) * piece, piece)
            piece_sc[owner, pl.ds(where, piece), :] = turned[source]
            packed.append(
                jnp.where(lane < LANES // 2, tall[source, :half], tall[source, half:])
            )
        where = pl.multiple_of(slab_count * piece + step * slabs * half, slabs * half)
        piece_sc[owner, pl.ds(where, slabs * half), :] = jnp.concatenate(packed, axis=0).astype(BF16)

    @pl.when(step == pl.num_programs(0) - 1)
    def _():
        grad_heads_ref[...] = grad_sc[...].T.astype(BF16).reshape(H, HS, frames)
        for away, ref in enumerate(piece_refs):
            ref[...] = piece_sc[lax.rem(mine + away, dp_count)]


def middle(info, returned, block_input, grad_output, before, after, out_proj, kernel, bias, dp_count):
    frames = block_input.shape[0]
    piece_rows = D // dp_count + D // dp_count // 2
    column = lambda count: pl.BlockSpec((count, CHUNK), lambda i: (0, i))
    return pl.pallas_call(
        middle_kernel,
        grid=(D // CHUNK,),
        in_specs=[
            SCALARS,
            here(),
            column(frames),
            column(frames),
            here(),
            here(),
            pl.BlockSpec((CHUNK, HD), lambda i: (i, 0)),
            column(KW),
            column(1),
        ],
        out_specs=[
            column(frames),
            column(frames),
            whole((H, HS, frames)),
        ]
        + [whole((piece_rows, frames))] * dp_count,
        out_shape=[
            jax.ShapeDtypeStruct((frames, D), BF16),
            jax.ShapeDtypeStruct((frames, D), BF16),
            jax.ShapeDtypeStruct((H, HS, frames), BF16),
        ]
        + [jax.ShapeDtypeStruct((piece_rows, frames), BF16)] * dp_count,
        scratch_shapes=[
            pltpu.VMEM((frames + 2 * WIDE, HD), BF16),
            pltpu.VMEM((frames, HD), F32),
            pltpu.VMEM((CHUNK // LANES, frames + 2 * WIDE, LANES), F32),
            pltpu.VMEM((CHUNK // LANES, frames + 2 * SIDE, LANES), F32),
            pltpu.VMEM((TAP_ROWS, 8, CHUNK), F32),
            pltpu.VMEM((dp_count, piece_rows, frames), BF16),
        ],
        compiler_params=params(),
        name="middle",
    )(
        info,
        near(returned),
        far(block_input),
        far(grad_output),
        near(before),
        near(after),
        far(out_proj),
        far(kernel),
        bias,
    )


def split_parts(lane, value):
    high_part = value.astype(BF16).astype(F32)
    low_part = pltpu.roll(value - high_part, TAP_ROWS, 1)
    return jnp.where(lane % (2 * TAP_ROWS) < TAP_ROWS, high_part, low_part)


def join_parts(value):
    return value + pltpu.roll(value, LANES - TAP_ROWS, 1)


def store_share(out_ref, share, taps):
    piece = share.shape[-2]
    for tile in range(HD // LANES):
        rows = slice(tile * piece, (tile + 1) * piece)
        out_ref[..., rows, :] = share[..., tile * LANES : (tile + 1) * LANES].astype(BF16)
    out_ref[..., HD // LANES * piece :, :] = taps.astype(BF16)


def product_kernel(*refs):
    out_ref = refs[-1]
    count = (len(refs) - 1) // 2
    pieces, heads = refs[:count], refs[count : 2 * count]
    slabs = out_ref.shape[0]
    frames = pieces[0].shape[1]
    height = pieces[0].shape[0] * 2 // 3
    piece = height // slabs
    total = jnp.zeros((height, HD), F32)
    taps = jnp.zeros((height // 2, frames), F32)
    for piece_ref, head_ref in zip(pieces, heads):
        total += lax.dot_general(
            piece_ref[:height, :],
            head_ref[:, :HS, :].reshape(HD, frames),
            (((1,), (1,)), ((), ())),
            preferred_element_type=F32,
        )
        taps += piece_ref[height:, :].astype(F32)
    lane = lax.broadcasted_iota(jnp.int32, taps.shape, 1)
    parts = split_parts(lane, join_parts(taps)).reshape(slabs, piece // 2, LANES)
    store_share(out_ref, total.reshape(slabs, piece, HD), parts)


def product(pieces, heads, returned, seq_count):
    height = pieces[0].shape[0] * 2 // 3
    piece = height // seq_count
    share_rows = piece * HD // LANES + piece // 2
    near_heads = [near(array) for array in [returned, *heads]]
    near_pieces = [pieces[0]] + [near(array) for array in pieces[1:]]
    return pl.pallas_call(
        product_kernel,
        in_specs=here(2 * len(pieces)),
        out_specs=here(),
        out_shape=jax.ShapeDtypeStruct((seq_count, share_rows, LANES), BF16),
        compiler_params=params(),
        name="product",
    )(*near_pieces, *near_heads)


def sum_kernel(in_ref, out_ref):
    total = jnp.sum(in_ref[...].astype(F32), axis=0)
    rows = total.shape[0] * 12 // 13
    out_ref[:rows, :] = total[:rows].astype(BF16)
    taps = total[rows:]
    lane = lax.broadcasted_iota(jnp.int32, taps.shape, 1)
    out_ref[rows:, :] = split_parts(lane, join_parts(taps)).astype(BF16)


def sum_shares(shares):
    return pl.pallas_call(
        sum_kernel,
        in_specs=[here()],
        out_specs=here(),
        out_shape=jax.ShapeDtypeStruct(shares.shape[1:], BF16),
        compiler_params=params(),
        name="sum_shares",
    )(near(shares))


def pair_kernel(info_ref, own_ref, other_ref, *outs):
    count = len(outs)
    layer = lax.div(info_ref[3], 2)
    for away, out_ref in enumerate(outs):
        target = lax.rem(layer + away, count)
        out_ref[0] = own_ref[target]
        out_ref[1] = other_ref[target]


def pair_heads(info, own, other):
    count, rows, frames = own.shape
    return pl.pallas_call(
        pair_kernel,
        in_specs=[SCALARS] + here(2),
        out_specs=here(count),
        out_shape=[jax.ShapeDtypeStruct((2, rows, frames), BF16)] * count,
        compiler_params=params(),
        name="pair_heads",
    )(info, own, near(other))


def finish_kernel(info_ref, in_ref, *rest):
    pairs, (proj_ref, tap_ref, bias_ref, query_ref, heads_sc) = rest[:-5], rest[-5:]
    owners, share_rows, _ = in_ref.shape
    rows = share_rows * 12 // 13
    piece = rows * LANES // HD
    columns = []
    for owner in range(owners):
        for tile in range(HD // LANES):
            part = in_ref[owner, tile * piece : (tile + 1) * piece, :].astype(F32)
            proj_ref[owner * piece : (owner + 1) * piece, tile * LANES : (tile + 1) * LANES] = part
        taps = join_parts(in_ref[owner, rows:, :].astype(F32))
        columns += [taps, pltpu.roll(taps, LANES // 2, 1)]
    turned = jnp.concatenate(columns, axis=0).T
    tap_ref[...] = turned[:KW]
    bias_ref[...] = turned[KW : KW + 1]
    count = len(pairs)
    layer, side = lax.div(info_ref[3], 2), lax.rem(info_ref[3], 2)
    for away, pair_ref in enumerate(pairs):
        source = 2 * lax.rem(layer - away + count, count)
        heads_sc[source + side] = pair_ref[0]
        heads_sc[source + 1 - side] = pair_ref[1]
    query_ref[...] = heads_sc[...].reshape(HD, heads_sc.shape[2]).T


def finish(info, gathered, pairs):
    owners, share_rows, _ = gathered.shape
    width = owners * share_rows * 12 // 13 * LANES // HD
    frames = pairs[0].shape[2]
    return pl.pallas_call(
        finish_kernel,
        in_specs=[SCALARS] + here(1 + len(pairs)),
        out_specs=here(4),
        out_shape=[
            jax.ShapeDtypeStruct((width, HD), F32),
            jax.ShapeDtypeStruct((KW, width), F32),
            jax.ShapeDtypeStruct((1, width), F32),
            jax.ShapeDtypeStruct((frames, HD), BF16),
        ],
        scratch_shapes=[pltpu.VMEM((H, HS, frames), BF16)],
        compiler_params=params(),
        name="finish",
    )(info, near(gathered), pairs[0], *[near(pair) for pair in pairs[1:]])


def ring(count, away):
    return [(i, (i + away) % count) for i in range(count)]


def send_round(blocks, axis, stride=1):
    count = len(blocks) * stride
    return [blocks[0]] + [
        lax.ppermute(blocks[away], axis, ring(count, away * stride))
        for away in range(1, len(blocks))
    ]


def exchange(blocks, axis):
    return lax.all_to_all(blocks, axis, split_axis=0, concat_axis=0, tiled=True)


def fast_device(
    block_input, query_proj, key_proj, value_proj, lengths, out_proj, kernel, conv_bias, grad_output
):
    frames = block_input.shape[1]
    seq_count = lax.axis_size("seq")
    dp_count = lax.axis_size("dp")
    place = lax.axis_index("seq")
    info = jnp.stack([place * frames, lengths[0], lax.axis_index("dp"), place]).astype(jnp.int32)
    bias_row = conv_bias[None]

    received = exchange(pack_heads(query_proj[0], key_proj[0], value_proj[0]), "seq")

    last = jnp.concatenate([block_input[0, frames - WIDE :], grad_output[0, frames - SIDE :]])
    leading = jnp.concatenate([block_input[0, :WIDE], grad_output[0, :SIDE]])
    up = [(i, i + 1) for i in range(seq_count - 1)]
    down = [(j, i) for i, j in up]
    before = lax.ppermute(last, "seq", up)
    after = lax.ppermute(leading, "seq", down)
    received, before, after, info, bias_row = lax.optimization_barrier(
        (received, before, after, info, bias_row)
    )

    sent, lse = forward_heads(info, received)
    returned = exchange(sent, "seq")
    mine = returned[:, :HS]
    heads = send_round([mine] * dp_count, "dp")[1:]
    block_output, grad_input, grad_heads, *pieces = middle(
        info,
        returned,
        block_input[0],
        grad_output[0],
        before,
        after,
        out_proj,
        kernel,
        bias_row,
        dp_count,
    )
    grad_heads, heads, pieces = lax.optimization_barrier((grad_heads, heads, pieces))

    grads = exchange(grad_heads, "seq")
    moved = send_round(pieces, "dp")
    grads, moved = lax.optimization_barrier((grads, moved))
    shares = product(moved, heads, returned, seq_count)
    shares, grads = lax.optimization_barrier((shares, grads))
    shares = exchange(shares, "seq")
    keep, give = backward_heads(info, received, grads, sent, lse)
    other = lax.ppermute(give, "seq", [(i, i ^ 1) for i in range(seq_count)])
    pairs = send_round(pair_heads(info, keep, other), "seq", 2)
    gathered = lax.all_gather(sum_shares(shares), "dp")
    grad_proj, grad_kernel, grad_bias, grad_query = finish(info, gathered, pairs)
    return (block_output[None], grad_input[None], grad_query[None], grad_proj, grad_kernel, grad_bias[0])


def solution(mesh):
    device_fn = fast_device if fits_fast(mesh.shape) else general_device
    placed = (
        P("dp", "seq", None),
        P("dp", "seq", None),
        P("dp", "seq", None),
        P("dp", "seq", None),
        P("dp"),
        P(),
        P(),
        P(),
        P("dp", "seq", None),
    )
    return jax.shard_map(
        device_fn,
        mesh=mesh,
        in_specs=placed,
        out_specs=(
            P("dp", "seq", None),
            P("dp", "seq", None),
            P("dp", "seq", None),
            P("seq", None),
            P(None, "seq"),
            P("seq"),
        ),
        check_vma=False,
    )
```

```python
import functools
import math

import jax
import jax.numpy as jnp
from jax import lax
from jax.experimental import pallas as pl
from jax.experimental.pallas import tpu as pltpu
from jax.sharding import PartitionSpec as P

D = 1536
H = 8
HS = 96
KW = 31
HD = 768


def with_halo(x, sides, width):
    for axis, dim in sides:
        size, length = (lax.axis_size(axis), x.shape[dim])
        up = [(i, (i + 1) % size) for i in range(size - 1)]
        down = [(j, i) for i, j in up]
        last = lax.slice_in_dim(x, length - width, length, axis=dim)
        leading = lax.slice_in_dim(x, 0, width, axis=dim)
        before = lax.ppermute(last, axis, up)
        after = lax.ppermute(leading, axis, down)
        x = jnp.concatenate([before, x, after], axis=dim)
    return x


def forward_rows(query_one, key_one, value_one, key_valid, score_scale):
    row_total = query_one.shape[0]
    block_rows = math.gcd(row_total, 512)
    query_blocks = query_one.reshape(row_total // block_rows, block_rows, query_one.shape[1])

    def forward_one_block(query_block):
        scores = (
            lax.dot_general(
                query_block, key_one, (((1,), (1,)), ((), ())), preferred_element_type=jnp.float32
            )
            * score_scale
        )
        scores = jnp.where(key_valid[None, :], scores, -jnp.inf)
        row_top = jnp.max(scores, axis=-1, keepdims=True)
        log_total = row_top + jnp.log(jnp.sum(jnp.exp(scores - row_top), axis=-1, keepdims=True))
        weights = jnp.exp(scores - log_total).astype(jnp.bfloat16)
        return (jnp.dot(weights, value_one, preferred_element_type=jnp.float32), log_total[:, 0])

    outputs, log_totals = lax.map(forward_one_block, query_blocks)
    return (outputs.reshape(row_total, query_one.shape[1]), log_totals.reshape(row_total))


def backward_rows(
    query_one, key_one, value_one, grad_one, lse_one, delta_one, key_valid, score_scale
):
    row_total = query_one.shape[0]
    block_rows = math.gcd(row_total, 512)
    block_count = row_total // block_rows
    width = query_one.shape[1]

    def backward_one_block(items):
        query_block, grad_block, lse_block, delta_block = items
        scores = (
            lax.dot_general(
                query_block, key_one, (((1,), (1,)), ((), ())), preferred_element_type=jnp.float32
            )
            * score_scale
        )
        scores = jnp.where(key_valid[None, :], scores, -jnp.inf)
        probs = jnp.exp(scores - lse_block[:, None])
        grad_prob = lax.dot_general(
            grad_block, value_one, (((1,), (1,)), ((), ())), preferred_element_type=jnp.float32
        )
        grad_score = (probs * (grad_prob - delta_block[:, None])).astype(jnp.bfloat16)
        return jnp.dot(grad_score, key_one, preferred_element_type=jnp.float32) * score_scale

    results = lax.map(
        backward_one_block,
        (
            query_one.reshape(block_count, block_rows, width),
            grad_one.reshape(block_count, block_rows, width),
            lse_one.reshape(block_count, block_rows),
            delta_one.reshape(block_count, block_rows),
        ),
    )
    return results.reshape(row_total, width)


def general_device(
    block_input, query_proj, key_proj, value_proj, lengths, out_proj, kernel, conv_bias, grad_output
):
    frames_dev = block_input.shape[1]
    seq_count = lax.axis_size("seq")
    total_frames = frames_dev * seq_count
    first_frame = lax.axis_index("seq") * frames_dev
    utt_length = lengths[0]
    local_valid = first_frame + jnp.arange(frames_dev) < utt_length
    all_valid = jnp.arange(total_frames) < utt_length
    score_scale = 1.0 / math.sqrt(HS)
    halo_width = KW // 2
    group_size = seq_count // H
    sub_rows = frames_dev // group_size
    query_local = query_proj[0]

    def to_serving(matrix):
        return matrix.reshape(frames_dev, H, HS).transpose(1, 0, 2).reshape(seq_count, sub_rows, HS)

    def from_serving(returned):
        return returned.reshape(H, frames_dev, HS).transpose(1, 0, 2).reshape(frames_dev, HD)

    query_mine = lax.all_to_all(
        to_serving(query_local), "seq", split_axis=0, concat_axis=1, tiled=True
    )[0]
    key_send = jnp.repeat(
        key_proj[0].reshape(frames_dev, H, HS).transpose(1, 0, 2), group_size, axis=0
    )
    value_send = jnp.repeat(
        value_proj[0].reshape(frames_dev, H, HS).transpose(1, 0, 2), group_size, axis=0
    )
    key_mine, value_mine = (
        lax.all_to_all(key_send, "seq", split_axis=0, concat_axis=1, tiled=True),
        lax.all_to_all(value_send, "seq", split_axis=0, concat_axis=1, tiled=True),
    )
    key_mine = key_mine[0]
    value_mine = value_mine[0]
    head_out, head_lse = forward_rows(query_mine, key_mine, value_mine, all_valid, score_scale)
    head_attended = head_out.astype(jnp.bfloat16)
    attended = from_serving(
        lax.all_to_all(head_attended[None], "seq", split_axis=1, concat_axis=0, tiled=True)
    )
    projected = lax.dot_general(
        attended, out_proj, (((1,), (1,)), ((), ())), preferred_element_type=jnp.float32
    )
    mixed_rows = (block_input[0].astype(jnp.float32) + projected).astype(jnp.bfloat16)
    masked = jnp.where(local_valid[:, None], mixed_rows, jnp.zeros_like(mixed_rows))
    padded = with_halo(masked, (("seq", 0),), halo_width).astype(jnp.float32)
    conv_rows = jnp.broadcast_to(conv_bias, (frames_dev, D))
    for tap in range(KW):
        conv_rows = conv_rows + kernel[tap] * padded[tap : tap + frames_dev]
    gate_rows = jax.nn.sigmoid(conv_rows)
    block_output = jnp.where(
        local_valid[:, None], mixed_rows.astype(jnp.float32) + conv_rows * gate_rows, 0.0
    ).astype(jnp.bfloat16)
    grad_rows = jnp.where(local_valid[:, None], grad_output[0].astype(jnp.float32), 0.0)
    grad_conv = grad_rows * gate_rows * (1.0 + conv_rows * (1.0 - gate_rows))
    kernel_local = jnp.stack(
        [jnp.sum(grad_conv * padded[tap : tap + frames_dev], axis=0) for tap in range(KW)]
    )
    bias_local = jnp.sum(grad_conv, axis=0)
    grad_padded = with_halo(grad_conv, (("seq", 0),), halo_width)
    grad_masked = jnp.zeros((frames_dev, D), jnp.float32)
    for tap in range(KW):
        begin = 2 * halo_width - tap
        grad_masked = grad_masked + kernel[tap] * grad_padded[begin : begin + frames_dev]
    grad_input = (grad_rows + jnp.where(local_valid[:, None], grad_masked, 0.0)).astype(
        jnp.bfloat16
    )
    grad_attn = jnp.dot(grad_input, out_proj, preferred_element_type=jnp.float32).astype(
        jnp.bfloat16
    )
    grad_mine = lax.all_to_all(
        to_serving(grad_attn), "seq", split_axis=0, concat_axis=1, tiled=True
    )[0]
    delta_mine = jnp.sum(grad_mine.astype(jnp.float32) * head_attended.astype(jnp.float32), axis=-1)
    grad_q_mine = backward_rows(
        query_mine, key_mine, value_mine, grad_mine, head_lse, delta_mine, all_valid, score_scale
    ).astype(jnp.bfloat16)
    grad_query = from_serving(
        lax.all_to_all(grad_q_mine[None], "seq", split_axis=1, concat_axis=0, tiled=True)
    )
    term_block = lax.dot_general(
        grad_input, attended, (((0,), (0,)), ((), ())), preferred_element_type=jnp.float32
    )
    partial_rows = lax.psum_scatter(term_block, "seq", scatter_dimension=0, tiled=True)
    summed = lax.psum(partial_rows.astype(jnp.bfloat16), "dp").astype(jnp.float32)
    kernel_total, bias_total = lax.psum((kernel_local, bias_local), ("seq", "dp"))
    shard_width = D // seq_count
    offset = lax.axis_index("seq") * shard_width
    grad_kernel = lax.dynamic_slice_in_dim(kernel_total, offset, shard_width, 1)
    grad_bias = lax.dynamic_slice_in_dim(bias_total, offset, shard_width, 0)
    return (block_output[None], grad_input[None], grad_query[None], summed, grad_kernel, grad_bias)


BF16 = jnp.bfloat16
F32 = jnp.float32
TAP_ROWS = 32
WIDE = 32
SIDE = 16
CHUNK = 768
LANES = 128
MASKED_SCORE = -1e30
QUERIES, KEYS, VALUES = (slice(place * HS, (place + 1) * HS) for place in range(3))
VMEM_LIMIT = 40 * 1024 * 1024
SCORE_SCALE = 1.0 / math.sqrt(HS)
LOG2_SCALE = SCORE_SCALE * math.log2(math.e)


def fits_fast(sizes):
    seq_count, dp_count = sizes["seq"], sizes["dp"]
    piece = D // (seq_count * dp_count)
    return seq_count == H and dp_count * seq_count * piece == D and piece == 48


def params():
    return pltpu.CompilerParams(vmem_limit_bytes=VMEM_LIMIT)


def whole(shape):
    return pl.BlockSpec(shape, lambda *_: (0,) * len(shape))


def near(array):
    return pltpu.with_memory_space_constraint(array, pltpu.VMEM)


def far(array):
    return pltpu.with_memory_space_constraint(array, pltpu.HBM)


def here(count=None):
    spec = pl.BlockSpec(memory_space=pltpu.VMEM)
    return spec if count is None else [spec] * count


SCALARS = pl.BlockSpec(memory_space=pltpu.SMEM)


def pack_kernel(q_ref, k_ref, v_ref, out_ref):
    heads, _, frames = out_ref.shape
    for place, ref in enumerate((q_ref, k_ref, v_ref)):
        out_ref[:, place * HS : (place + 1) * HS, :] = ref[...].T.reshape(heads, HS, frames)


def pack_heads(q, k, v):
    frames = q.shape[0]
    return pl.pallas_call(
        pack_kernel,
        grid=(2,),
        in_specs=[pl.BlockSpec((frames, HD // 2), lambda i: (0, i))] * 3,
        out_specs=pl.BlockSpec((H // 2, 3 * HS, frames), lambda i: (i, 0, 0)),
        out_shape=jax.ShapeDtypeStruct((H, 3 * HS, frames), BF16),
        compiler_params=params(),
        name="pack_heads",
    )(far(q), far(k), far(v))


def key_rows(x_ref, length, keys_sc):
    blocks, _, frames = x_ref.shape
    for block in range(blocks):
        row = lax.broadcasted_iota(jnp.int32, (LANES - HS, frames), 0)
        key = lax.broadcasted_iota(jnp.int32, (LANES - HS, frames), 1) + block * frames
        extra = jnp.where((row == 0) & (key >= length), MASKED_SCORE, 0.0)
        tall = jnp.concatenate([x_ref[block, KEYS].astype(F32), extra], axis=0)
        keys_sc[block * frames : (block + 1) * frames, :] = tall.T.astype(BF16)


def pair_of(ref, first, rows):
    return jnp.concatenate([ref[first, rows], ref[first + 1, rows]], axis=1)


def query_columns(x_ref, first):
    query = pair_of(x_ref, first, QUERIES)
    row = lax.broadcasted_iota(jnp.int32, (LANES - HS, query.shape[1]), 0)
    return jnp.concatenate([query, jnp.where(row == 0, 1.0, 0.0).astype(BF16)], axis=0)


def side_by_side(x_ref, rows, wide_sc):
    blocks, _, frames = x_ref.shape
    for block in range(blocks):
        wide_sc[:, block * frames : (block + 1) * frames] = x_ref[block, rows]


def forward_kernel(
    info_ref, x_ref, out_ref, lse_ref, keys_sc, values_sc, scores_sc, weights_sc
):
    blocks, _, frames = x_ref.shape
    key_rows(x_ref, info_ref[1], keys_sc)
    side_by_side(x_ref, VALUES, values_sc)
    for first in range(0, blocks, 2):
        turn = first // 2 % 2
        query = query_columns(x_ref, first)
        wide = query.shape[1]
        chunks = [slice(row, row + frames) for row in range(0, blocks * frames, frames)]
        peak = None
        for chunk in chunks:
            part = jnp.dot(keys_sc[chunk, :], query, preferred_element_type=F32)
            scores_sc[turn, chunk, :] = part
            part = part.reshape(frames // 8, 8, wide).max(0)
            peak = part if peak is None else jnp.maximum(peak, part)
        top = jnp.max(peak, axis=0, keepdims=True) * LOG2_SCALE
        total = jnp.zeros((8, wide), F32)
        for chunk in chunks:
            raised = jnp.exp2(scores_sc[turn, chunk, :] * LOG2_SCALE - top)
            scores_sc[turn, chunk, :] = raised
            total += raised.reshape(frames // 8, 8, wide).sum(0)
        total = jnp.sum(total, axis=0, keepdims=True)
        shrink = 1.0 / total
        lse_ref[:, first * frames : (first + 2) * frames] = top + jnp.log2(total)
        for chunk in chunks:
            weights_sc[turn, chunk, :] = (scores_sc[turn, chunk, :] * shrink).astype(BF16)
        mixed = jnp.dot(values_sc[...], weights_sc[turn], preferred_element_type=F32).astype(BF16)
        out_ref[first, :HS, :] = mixed[:, :frames]
        out_ref[first + 1, :HS, :] = mixed[:, frames:]

    lane = lax.broadcasted_iota(jnp.int32, (HS, frames), 1)
    nothing = jnp.zeros((HS, frames), F32)
    for block in range(blocks):
        left = nothing
        right = nothing
        if block > 0:
            left = pltpu.roll(out_ref[block - 1, :HS, :].astype(F32), WIDE, 1)
        if block < blocks - 1:
            right = pltpu.roll(out_ref[block + 1, :HS, :].astype(F32), WIDE, 1)
        both = jnp.where(lane < WIDE, left, right)
        lower = pltpu.roll(both[HS // 2 :], 2 * WIDE, 1)
        packed = jnp.where(lane[: HS // 2] < 2 * WIDE, both[: HS // 2], lower)
        out_ref[block, HS:, :] = packed.astype(BF16)


def forward_heads(info, received):
    blocks, _, frames = received.shape
    total = blocks * frames
    return pl.pallas_call(
        forward_kernel,
        in_specs=[SCALARS, here()],
        out_specs=here(2),
        out_shape=[
            jax.ShapeDtypeStruct((blocks, HS + HS // 2, frames), BF16),
            jax.ShapeDtypeStruct((1, total), F32),
        ],
        scratch_shapes=[
            pltpu.VMEM((total, LANES), BF16),
            pltpu.VMEM((HS, total), BF16),
            pltpu.VMEM((2, total, 2 * frames), F32),
            pltpu.VMEM((2, total, 2 * frames), BF16),
        ],
        compiler_params=params(),
        name="forward_heads",
    )(info, near(received))


def split_sides(place, blocks_ref, keep_ref, give_ref):
    side = lax.rem(place, 2)
    for layer in range(keep_ref.shape[0]):
        keep_ref[layer] = blocks_ref[2 * layer + side]
        give_ref[layer] = blocks_ref[2 * layer + 1 - side]


def join_sides(place, pairs, blocks_ref):
    count = len(pairs)
    layer, side = lax.div(place, 2), lax.rem(place, 2)
    for away, pair_ref in enumerate(pairs):
        source = 2 * lax.rem(layer - away + count, count)
        blocks_ref[source + side] = pair_ref[0]
        blocks_ref[source + 1 - side] = pair_ref[1]


def backward_kernel(info_ref, x_ref, head_ref, lse_ref, *rest):
    pairs, rest = rest[:-7], rest[-7:]
    keep_ref, give_ref, keys_sc, values_sc, wide_sc, result_sc, grad_ref = rest
    blocks, _, frames = x_ref.shape
    join_sides(info_ref[3], pairs, grad_ref)
    key_rows(x_ref, info_ref[1], keys_sc)
    side_by_side(x_ref, KEYS, wide_sc)
    for block in range(blocks):
        rows = x_ref[block, VALUES].astype(F32).T.astype(BF16)
        values_sc[block * frames : (block + 1) * frames, :] = rows

    for first in range(0, blocks, 2):
        scores = jnp.dot(keys_sc[...], query_columns(x_ref, first), preferred_element_type=F32)
        probs = jnp.exp2(scores * LOG2_SCALE - lse_ref[:, first * frames : (first + 2) * frames])
        grad = pair_of(grad_ref, first, slice(0, HS))
        head = pair_of(head_ref, first, slice(0, HS))
        delta = jnp.sum(grad.astype(F32) * head.astype(F32), axis=0, keepdims=True)
        grad_prob = jnp.dot(values_sc[...], grad, preferred_element_type=F32)
        grad_score = (probs * (grad_prob - delta)).astype(BF16)
        result = jnp.dot(wide_sc[...], grad_score, preferred_element_type=F32) * SCORE_SCALE
        result_sc[first] = result[:, :frames].astype(BF16)
        result_sc[first + 1] = result[:, frames:].astype(BF16)
    split_sides(info_ref[3], result_sc, keep_ref, give_ref)


def backward_heads(info, received, heads, lse, pairs):
    blocks, _, frames = received.shape
    total = blocks * frames
    return pl.pallas_call(
        backward_kernel,
        in_specs=[SCALARS] + here(3 + len(pairs)),
        out_specs=here(2),
        out_shape=[jax.ShapeDtypeStruct((blocks // 2, HS, frames), BF16)] * 2,
        scratch_shapes=[
            pltpu.VMEM((total, LANES), BF16),
            pltpu.VMEM((total, HS), BF16),
            pltpu.VMEM((HS, total), BF16),
            pltpu.VMEM((blocks, HS, frames), BF16),
            pltpu.VMEM((blocks, HS, frames), BF16),
        ],
        compiler_params=params(),
        name="backward_heads",
    )(info, near(received), heads, lse, pairs[0], *[near(pair) for pair in pairs[1:]])


def shifted_sum(ref, tile, rows, weight_of, start):
    total = start
    for low in range(8):
        base = ref[tile, low : low + rows + 24, :]
        for high in range(4):
            offset = 8 * high + low
            if 1 <= offset < TAP_ROWS:
                total = total + weight_of(offset) * base[8 * high : 8 * high + rows]
    return total


def middle_kernel(
    info_ref,
    att_ref,
    input_ref,
    cot_ref,
    before_ref,
    after_ref,
    proj_ref,
    tap_ref,
    bias_ref,
    block_out_ref,
    grad_in_ref,
    keep_ref,
    give_ref,
    *rest,
):
    piece_refs = rest[:-7]
    att_sc, grad_sc, masked_sc, gate_sc, taps_sc, piece_sc, heads_sc = rest[-7:]
    dp_count = len(piece_refs)
    step = pl.program_id(0)
    frames = input_ref.shape[0]
    tiles = CHUNK // LANES
    rows = frames + 2 * WIDE
    span = frames + 2 * SIDE
    first, length, mine = info_ref[0], info_ref[1], info_ref[2]

    @pl.when(step == 0)
    def _():
        main = att_ref[:, :HS, :].reshape(HD, frames)
        att_sc[WIDE : WIDE + frames, :] = main.T
        edge = att_ref[:, HS:, :].astype(F32).reshape(H * (HS // 2), frames)
        lower = pltpu.roll(edge, frames - 2 * WIDE, 1)
        half = (H, HS // 2, frames)
        tall = jnp.concatenate([edge.reshape(half), lower.reshape(half)], axis=1)
        turned = tall.reshape(HD, frames).T.astype(BF16)
        att_sc[:WIDE, :] = turned[:WIDE]
        att_sc[WIDE + frames :, :] = turned[WIDE : 2 * WIDE]
        grad_sc[...] = jnp.zeros_like(grad_sc)

    frame = first - WIDE + lax.broadcasted_iota(jnp.int32, (rows, LANES), 0)
    valid = (frame >= 0) & (frame < length)
    inner = slice(WIDE - SIDE, WIDE + SIDE + frames)
    own = slice(SIDE, SIDE + frames)
    inside = valid[WIDE : WIDE + frames]
    for tile in range(tiles):
        lanes = slice(tile * LANES, (tile + 1) * LANES)
        place = pl.ds(pl.multiple_of(step * CHUNK + tile * LANES, LANES), LANES)
        wide_input = jnp.concatenate(
            [before_ref[:WIDE, place], input_ref[:, lanes], after_ref[:WIDE, place]], axis=0
        ).astype(F32)
        projected = lax.dot_general(
            att_sc[...], proj_ref[lanes, :], (((1,), (1,)), ((), ())), preferred_element_type=F32
        )
        mixed = (wide_input + projected).astype(BF16).astype(F32)
        masked_sc[tile] = jnp.where(valid, mixed, 0.0)
        cot = jnp.concatenate(
            [before_ref[WIDE:, place], cot_ref[:, lanes], after_ref[WIDE:, place]], axis=0
        ).astype(F32)
        cot = jnp.where(valid[inner], cot, 0.0)
        start = jnp.broadcast_to(bias_ref[:, lanes], (span, LANES))
        conv = shifted_sum(
            masked_sc, tile, span, lambda offset: tap_ref[offset - 1 : offset, lanes], start
        )
        gate = lax.logistic(conv)
        center = masked_sc[tile, WIDE : WIDE + frames, :]
        block_out_ref[:, lanes] = jnp.where(inside, center + conv[own] * gate[own], 0.0).astype(BF16)
        gated = cot * gate * (1.0 + conv * (1.0 - gate))
        gate_sc[tile] = gated
        owned = gated[own]
        for low in range(8):
            base = masked_sc[tile, SIDE + low : SIDE + low + frames + 24, :]
            for high in range(4):
                offset = 8 * high + low
                if 1 <= offset < TAP_ROWS:
                    product = owned * base[8 * high : 8 * high + frames]
                    taps_sc[offset - 1, :, lanes] = product.reshape(frames // 8, 8, LANES).sum(0)
        taps_sc[TAP_ROWS - 1, :, lanes] = owned.reshape(frames // 8, 8, LANES).sum(0)
        back = shifted_sum(
            gate_sc,
            tile,
            frames,
            lambda offset: tap_ref[KW - offset : KW - offset + 1, lanes],
            jnp.zeros((frames, LANES), F32),
        )
        grad_in_ref[:, lanes] = (cot[own] + jnp.where(inside, back, 0.0)).astype(BF16)

    grad_in = grad_in_ref[...]
    grad_sc[...] += jnp.dot(grad_in, proj_ref[...], preferred_element_type=F32)

    piece = 48
    half = piece // 2
    slabs = CHUNK // (dp_count * piece)
    turned = grad_in.T.reshape(slabs * dp_count, piece, frames)
    taps = jnp.sum(taps_sc[...], axis=1)
    high_part = taps.astype(BF16).astype(F32)
    low_part = taps - high_part
    four = jnp.concatenate([high_part, low_part, high_part, low_part], axis=0)
    tall = four.T.reshape(slabs * dp_count, piece, LANES)
    lane = lax.broadcasted_iota(jnp.int32, (half, LANES), 1)
    slab_count = D // (dp_count * piece)
    for owner in range(dp_count):
        packed = []
        for slab in range(slabs):
            source = slab * dp_count + owner
            where = pl.multiple_of((step * slabs + slab) * piece, piece)
            piece_sc[owner, pl.ds(where, piece), :] = turned[source]
            packed.append(
                jnp.where(lane < LANES // 2, tall[source, :half], tall[source, half:])
            )
        where = pl.multiple_of(slab_count * piece + step * slabs * half, slabs * half)
        piece_sc[owner, pl.ds(where, slabs * half), :] = jnp.concatenate(packed, axis=0).astype(BF16)

    @pl.when(step == pl.num_programs(0) - 1)
    def _():
        heads_sc[...] = grad_sc[...].T.astype(BF16).reshape(H, HS, frames)
        split_sides(info_ref[3], heads_sc, keep_ref, give_ref)
        for away, ref in enumerate(piece_refs):
            ref[...] = piece_sc[lax.rem(mine + away, dp_count)]


def middle(info, returned, block_input, grad_output, before, after, out_proj, kernel, bias, dp_count):
    frames = block_input.shape[0]
    piece_rows = D // dp_count + D // dp_count // 2
    column = lambda count: pl.BlockSpec((count, CHUNK), lambda i: (0, i))
    return pl.pallas_call(
        middle_kernel,
        grid=(D // CHUNK,),
        in_specs=[
            SCALARS,
            here(),
            column(frames),
            column(frames),
            here(),
            here(),
            pl.BlockSpec((CHUNK, HD), lambda i: (i, 0)),
            column(KW),
            column(1),
        ],
        out_specs=[
            column(frames),
            column(frames),
            whole((H // 2, HS, frames)),
            whole((H // 2, HS, frames)),
        ]
        + [whole((piece_rows, frames))] * dp_count,
        out_shape=[
            jax.ShapeDtypeStruct((frames, D), BF16),
            jax.ShapeDtypeStruct((frames, D), BF16),
            jax.ShapeDtypeStruct((H // 2, HS, frames), BF16),
            jax.ShapeDtypeStruct((H // 2, HS, frames), BF16),
        ]
        + [jax.ShapeDtypeStruct((piece_rows, frames), BF16)] * dp_count,
        scratch_shapes=[
            pltpu.VMEM((frames + 2 * WIDE, HD), BF16),
            pltpu.VMEM((frames, HD), F32),
            pltpu.VMEM((CHUNK // LANES, frames + 2 * WIDE, LANES), F32),
            pltpu.VMEM((CHUNK // LANES, frames + 2 * SIDE, LANES), F32),
            pltpu.VMEM((TAP_ROWS, 8, CHUNK), F32),
            pltpu.VMEM((dp_count, piece_rows, frames), BF16),
            pltpu.VMEM((H, HS, frames), BF16),
        ],
        compiler_params=params(),
        name="middle",
    )(
        info,
        near(returned),
        far(block_input),
        far(grad_output),
        near(before),
        near(after),
        far(out_proj),
        far(kernel),
        bias,
    )


def split_parts(lane, value):
    high_part = value.astype(BF16).astype(F32)
    low_part = pltpu.roll(value - high_part, TAP_ROWS, 1)
    return jnp.where(lane % (2 * TAP_ROWS) < TAP_ROWS, high_part, low_part)


def join_parts(value):
    return value + pltpu.roll(value, LANES - TAP_ROWS, 1)


def store_share(out_ref, share, taps):
    piece = share.shape[-2]
    for tile in range(HD // LANES):
        rows = slice(tile * piece, (tile + 1) * piece)
        out_ref[..., rows, :] = share[..., tile * LANES : (tile + 1) * LANES].astype(BF16)
    out_ref[..., HD // LANES * piece :, :] = taps.astype(BF16)


def product_kernel(*refs):
    out_ref = refs[-1]
    count = (len(refs) - 1) // 2
    pieces, heads = refs[:count], refs[count : 2 * count]
    slabs = out_ref.shape[0]
    frames = pieces[0].shape[1]
    height = pieces[0].shape[0] * 2 // 3
    piece = height // slabs
    total = jnp.zeros((height, HD), F32)
    taps = jnp.zeros((height // 2, frames), F32)
    for piece_ref, head_ref in zip(pieces, heads):
        total += lax.dot_general(
            piece_ref[:height, :],
            head_ref[:, :HS, :].reshape(HD, frames),
            (((1,), (1,)), ((), ())),
            preferred_element_type=F32,
        )
        taps += piece_ref[height:, :].astype(F32)
    lane = lax.broadcasted_iota(jnp.int32, taps.shape, 1)
    parts = split_parts(lane, join_parts(taps)).reshape(slabs, piece // 2, LANES)
    store_share(out_ref, total.reshape(slabs, piece, HD), parts)


def product(pieces, heads, returned, seq_count):
    height = pieces[0].shape[0] * 2 // 3
    piece = height // seq_count
    share_rows = piece * HD // LANES + piece // 2
    near_heads = [near(array) for array in [returned, *heads]]
    near_pieces = [pieces[0]] + [near(array) for array in pieces[1:]]
    return pl.pallas_call(
        product_kernel,
        in_specs=here(2 * len(pieces)),
        out_specs=here(),
        out_shape=jax.ShapeDtypeStruct((seq_count, share_rows, LANES), BF16),
        compiler_params=params(),
        name="product",
    )(*near_pieces, *near_heads)


def sum_kernel(in_ref, out_ref):
    total = jnp.sum(in_ref[...].astype(F32), axis=0)
    rows = total.shape[0] * 12 // 13
    out_ref[:rows, :] = total[:rows].astype(BF16)
    taps = total[rows:]
    lane = lax.broadcasted_iota(jnp.int32, taps.shape, 1)
    out_ref[rows:, :] = split_parts(lane, join_parts(taps)).astype(BF16)


def sum_shares(shares):
    return pl.pallas_call(
        sum_kernel,
        in_specs=[here()],
        out_specs=here(),
        out_shape=jax.ShapeDtypeStruct(shares.shape[1:], BF16),
        compiler_params=params(),
        name="sum_shares",
    )(near(shares))


def pair_kernel(info_ref, own_ref, other_ref, *outs):
    count = len(outs)
    layer = lax.div(info_ref[3], 2)
    for away, out_ref in enumerate(outs):
        target = lax.rem(layer + away, count)
        out_ref[0] = own_ref[target]
        out_ref[1] = other_ref[target]


def pair_heads(info, own, other):
    count, rows, frames = own.shape
    return pl.pallas_call(
        pair_kernel,
        in_specs=[SCALARS] + here(2),
        out_specs=here(count),
        out_shape=[jax.ShapeDtypeStruct((2, rows, frames), BF16)] * count,
        compiler_params=params(),
        name="pair_heads",
    )(info, own, near(other))


def finish_kernel(info_ref, in_ref, *rest):
    pairs, (proj_ref, tap_ref, bias_ref, query_ref, heads_sc) = rest[:-5], rest[-5:]
    owners, share_rows, _ = in_ref.shape
    rows = share_rows * 12 // 13
    piece = rows * LANES // HD
    columns = []
    for owner in range(owners):
        for tile in range(HD // LANES):
            part = in_ref[owner, tile * piece : (tile + 1) * piece, :].astype(F32)
            proj_ref[owner * piece : (owner + 1) * piece, tile * LANES : (tile + 1) * LANES] = part
        taps = join_parts(in_ref[owner, rows:, :].astype(F32))
        columns += [taps, pltpu.roll(taps, LANES // 2, 1)]
    turned = jnp.concatenate(columns, axis=0).T
    tap_ref[...] = turned[:KW]
    bias_ref[...] = turned[KW : KW + 1]
    join_sides(info_ref[3], pairs, heads_sc)
    query_ref[...] = heads_sc[...].reshape(HD, heads_sc.shape[2]).T


def finish(info, gathered, pairs):
    owners, share_rows, _ = gathered.shape
    width = owners * share_rows * 12 // 13 * LANES // HD
    frames = pairs[0].shape[2]
    return pl.pallas_call(
        finish_kernel,
        in_specs=[SCALARS] + here(1 + len(pairs)),
        out_specs=here(4),
        out_shape=[
            jax.ShapeDtypeStruct((width, HD), F32),
            jax.ShapeDtypeStruct((KW, width), F32),
            jax.ShapeDtypeStruct((1, width), F32),
            jax.ShapeDtypeStruct((frames, HD), BF16),
        ],
        scratch_shapes=[pltpu.VMEM((H, HS, frames), BF16)],
        compiler_params=params(),
        name="finish",
    )(info, near(gathered), pairs[0], *[near(pair) for pair in pairs[1:]])


def ring(count, away):
    return [(i, (i + away) % count) for i in range(count)]


def send_round(blocks, axis, stride=1):
    count = len(blocks) * stride
    return [blocks[0]] + [
        lax.ppermute(blocks[away], axis, ring(count, away * stride))
        for away in range(1, len(blocks))
    ]


def exchange(blocks, axis):
    return lax.all_to_all(blocks, axis, split_axis=0, concat_axis=0, tiled=True)


def first_stage(info, keep, give, count):
    other = lax.ppermute(give, "seq", [(i, i ^ 1) for i in range(count)])
    return pair_heads(info, keep, other)


def fast_device(
    block_input, query_proj, key_proj, value_proj, lengths, out_proj, kernel, conv_bias, grad_output
):
    frames = block_input.shape[1]
    seq_count = lax.axis_size("seq")
    dp_count = lax.axis_size("dp")
    place = lax.axis_index("seq")
    info = jnp.stack([place * frames, lengths[0], lax.axis_index("dp"), place]).astype(jnp.int32)
    bias_row = conv_bias[None]

    received = exchange(pack_heads(query_proj[0], key_proj[0], value_proj[0]), "seq")

    last = jnp.concatenate([block_input[0, frames - WIDE :], grad_output[0, frames - SIDE :]])
    leading = jnp.concatenate([block_input[0, :WIDE], grad_output[0, :SIDE]])
    up = [(i, i + 1) for i in range(seq_count - 1)]
    down = [(j, i) for i, j in up]
    before = lax.ppermute(last, "seq", up)
    after = lax.ppermute(leading, "seq", down)
    received, before, after, info, bias_row = lax.optimization_barrier(
        (received, before, after, info, bias_row)
    )

    sent, lse = forward_heads(info, received)
    returned = exchange(sent, "seq")
    mine = returned[:, :HS]
    heads = send_round([mine] * dp_count, "dp")[1:]
    block_output, grad_input, keep, give, *pieces = middle(
        info,
        returned,
        block_input[0],
        grad_output[0],
        before,
        after,
        out_proj,
        kernel,
        bias_row,
        dp_count,
    )
    keep, give, heads, pieces = lax.optimization_barrier((keep, give, heads, pieces))

    paired = first_stage(info, keep, give, seq_count)
    moved = send_round(pieces, "dp")
    grads = send_round(paired, "seq", 2)
    moved, grads = lax.optimization_barrier((moved, grads))
    shares = product(moved, heads, returned, seq_count)
    later, _ = lax.optimization_barrier((lse, shares))
    shares = exchange(shares, "seq")
    keep, give = backward_heads(info, received, sent, later, grads)
    pairs = send_round(first_stage(info, keep, give, seq_count), "seq", 2)
    gathered = lax.all_gather(sum_shares(shares), "dp")
    grad_proj, grad_kernel, grad_bias, grad_query = finish(info, gathered, pairs)
    return (block_output[None], grad_input[None], grad_query[None], grad_proj, grad_kernel, grad_bias[0])


def solution(mesh):
    device_fn = fast_device if fits_fast(mesh.shape) else general_device
    placed = (
        P("dp", "seq", None),
        P("dp", "seq", None),
        P("dp", "seq", None),
        P("dp", "seq", None),
        P("dp"),
        P(),
        P(),
        P(),
        P("dp", "seq", None),
    )
    return jax.shard_map(
        device_fn,
        mesh=mesh,
        in_specs=placed,
        out_specs=(
            P("dp", "seq", None),
            P("dp", "seq", None),
            P("dp", "seq", None),
            P("seq", None),
            P(None, "seq"),
            P("seq"),
        ),
        check_vma=False,
    )
```
